256 devices in a mesh: section: 16 (over y, z_lo), dp: 8 (over z_hi, x), tensor: 2 (over core).
Axes of the slice: x: 4, y: 4, z: 8 (z_hi: 2, z_lo: 4; z = z_hi * 4 + z_lo), core: 2. Of those that a mesh axis runs over, the one named last changes fastest.
Arguments:
- context: bfloat16 [16, 16, 256, 2048], P('section', 'dp'), may hold values from -6 to 6
- queries: bfloat16 [16, 16, 64, 2048], P('section', 'dp'), may hold values from -6 to 6
- lengths: int32 [16, 16], P('section', 'dp'), may hold values from 32 to 256
- norm_gain: float32 [16, 2048], P('section'), may hold values from 0.1 to 1.9
- qkv_weight: bfloat16 [16, 2048, 3, 2048], P('section', 'dp', None, 'tensor')
- out_weight: bfloat16 [16, 2048, 2048], P('section', 'tensor', 'dp'), may hold values from -0.5 to 0.5
Outputs:
- next_context: bfloat16 [16, 16, 256, 2048], P('section', 'dp')
- next_queries: bfloat16 [16, 16, 64, 2048], P('section', 'dp')
The draws below stay inside these ranges and needn't reach their ends.
All inputs are finite; a program needn't handle non-finite values.
Results may differ from the reference program's by a relative error of at most 0.014.
The reference program's roundings to bfloat16 on the way count: a program that leaves them out, or rounds other values in their place, can miss the bound.
Values may be sent and summed in bfloat16 or wider, within the bound.
No kernel may reach another device: no remote copies, remote signals or barrier semaphores. Data moves between devices by JAX's collectives and lax.ppermute only.
A program may use at most 128 MiB of HBM per device.

```python
import math
import jax
import jax.numpy as jnp
from jax import lax

D = 2048
HEADS = 16
HEAD = 128
MEM = 256
QRY = 64
LAYERS = 16
ENC = 8
SCENES = 16
INNER = 2048


def scene_tokens(key):
    base_key = jax.random.fold_in(key, 101)
    context_shape = (LAYERS, SCENES, MEM, D)
    query_shape = (LAYERS, SCENES, QRY, D)
    context_vals = jnp.clip(jax.random.normal(jax.random.fold_in(base_key, 1), context_shape, jnp.float32), -6.0, 6.0)
    query_vals = jnp.clip(jax.random.normal(jax.random.fold_in(base_key, 2), query_shape, jnp.float32), -6.0, 6.0)
    return (context_vals, query_vals)


def draw_context(key, part):
    return scene_tokens(key)[0].astype(jnp.bfloat16)


def draw_queries(key, part):
    return scene_tokens(key)[1].astype(jnp.bfloat16)


def draw_qkv_weight(key, part):
    weight_shape = (LAYERS, D, 3, HEADS, HEAD)
    spread = D ** (-0.5)
    values = jnp.clip(jax.random.normal(jax.random.fold_in(key, 1), weight_shape, jnp.float32), -6.0, 6.0) * spread
    return values.reshape(LAYERS, D, 3, HEADS * HEAD).astype(jnp.bfloat16)


def plant(drawn, key, low, largest):
    shape = drawn.shape
    spot = [jax.random.randint(jax.random.fold_in(key, axis), (), 0, shape[axis]) for axis in range(len(shape))]
    drawn = drawn.at[tuple(spot)].set(low)
    longest = shape.index(max(shape))
    spot[longest] = (spot[longest] + 1) % shape[longest]
    return drawn.at[tuple(spot)].set(largest)


def shard_levels(rng, dims, pieces, least, top_value):
    loudness = 1.0
    for dim, parts in pieces:
        steps = jax.random.uniform(jax.random.fold_in(jax.random.fold_in(rng, 6), dim), (parts,), jnp.float32, least / len(pieces), top_value / len(pieces))
        loudness = loudness * jnp.repeat(jnp.exp(steps), dims[dim] // parts).reshape((-1,) + (1,) * (len(dims) - 1 - dim))
    return loudness


def normal_values(own_key, shape, scale, limit, split=(), kind=jnp.bfloat16):
    values = jax.random.normal(own_key, shape, jnp.float32) * scale
    if len(split) > 0:
        values = shard_levels(own_key, shape, split, -0.22, 0.18) * values
    return jnp.clip(values, min=-limit, max=limit).astype(kind)


def setup_inputs(seed: int = 0) -> dict:
    streams_of = jax.random.split(jax.random.key(seed), 7)
    context = draw_context(jax.random.fold_in(streams_of[6], 71), 0)
    queries = draw_queries(jax.random.fold_in(streams_of[6], 71), 0)
    lengths = plant(jax.random.randint(streams_of[2], (LAYERS, SCENES), MEM // 8, MEM + 1), jax.random.fold_in(streams_of[2], 1), MEM // 8, MEM).astype(jnp.int32)
    norm_gain = jnp.clip(1.0 + 0.18 * jax.random.normal(streams_of[3], (LAYERS, D), jnp.float32), 0.1, 1.9)
    qkv_weight = draw_qkv_weight(jax.random.fold_in(streams_of[6], 71), 0)
    out_weight = normal_values(streams_of[5], (LAYERS, INNER, D), HEAD ** -0.5, 0.5, ((0, 16), (1, 2), (2, 8)))
    return {"context": context, "queries": queries, "lengths": lengths, "norm_gain": norm_gain, "qkv_weight": qkv_weight, "out_weight": out_weight}


def section_pass(stream_rows, valid_len, gain_row, qkv_mat, out_mat, encoder_flag):
    scene_count = stream_rows.shape[0]
    row_total = stream_rows.shape[1]
    model_width = stream_rows.shape[2]
    widened = stream_rows.astype(jnp.float32)
    mean_square = lax.optimization_barrier(jnp.mean(widened * widened, axis=-1, keepdims=True))
    normed = (widened * lax.rsqrt(mean_square + 1e-06) * gain_row).astype(jnp.bfloat16)
    flat_rows = normed.reshape(scene_count * row_total, model_width)
    projected = jnp.dot(flat_rows, qkv_mat.reshape(model_width, 3 * INNER), preferred_element_type=jnp.float32)
    projected = projected.astype(jnp.bfloat16).reshape(scene_count, row_total, 3, HEADS, HEAD)
    query_part = projected[:, :, 0].astype(jnp.float32)
    key_part = projected[:, :MEM, 1].astype(jnp.float32)
    value_part = projected[:, :MEM, 2].astype(jnp.float32)
    scores = jnp.einsum('brhd,bjhd->bhrj', query_part, key_part) * (1.0 / math.sqrt(HEAD))
    key_index = jnp.arange(MEM, dtype=jnp.int32)
    valid = key_index[None, None, None, :] < valid_len[:, None, None, None]
    scores = jnp.where(valid, scores, -1e+30)
    top_score = lax.optimization_barrier(jnp.max(scores, axis=-1, keepdims=True))
    expo = jnp.exp(scores - top_score)
    probs = (expo / lax.optimization_barrier(jnp.sum(expo, axis=-1, keepdims=True))).astype(jnp.bfloat16)
    mixed = jnp.einsum('bhrj,bjhd->brhd', probs.astype(jnp.float32), value_part).astype(jnp.bfloat16)
    row_index = jnp.arange(row_total, dtype=jnp.int32)
    keep_rows = jnp.where(encoder_flag, row_index < MEM, row_index >= MEM)
    mixed = mixed * keep_rows[None, :, None, None].astype(jnp.bfloat16)
    update = jnp.dot(mixed.reshape(scene_count * row_total, INNER), out_mat, preferred_element_type=jnp.float32)
    return (widened + update.reshape(scene_count, row_total, model_width)).astype(jnp.bfloat16)

def reference(context, queries, lengths, norm_gain, qkv_weight, out_weight):
    streams = jnp.concatenate([context, queries], axis=2)
    flags = jnp.arange(LAYERS, dtype=jnp.int32) < ENC

    def one_section(items):
        return section_pass(items[0], items[1], items[2], items[3], items[4], items[5])
    results = lax.map(one_section, (streams, lengths, norm_gain, qkv_weight, out_weight, flags))
    moved = jnp.roll(results, 1, axis=0)
    return (moved[:, :, :MEM], moved[:, :, MEM:])
```

```python
import functools
import math

import jax
import jax.numpy as jnp
from jax import lax
from jax.experimental import pallas as pl
from jax.experimental.pallas import tpu as pltpu
from jax.sharding import PartitionSpec as P

HEAD = 128
RING = 4
VMEM_LIMIT = 56 * 1024 * 1024
ANY = pl.BlockSpec(memory_space=pl.ANY)
SMEM = pl.BlockSpec(memory_space=pltpu.SMEM)
VMEM = pl.BlockSpec(memory_space=pltpu.VMEM)
BF16 = jnp.bfloat16
F32 = jnp.float32


def around_x(array, by, sections=None):
    pairs = [
        (z * RING + x, z * RING + (x + by) % RING) for z in range(2) for x in range(RING)
    ]
    return lax.ppermute(array, "dp", pairs)


def around_x_of(array, by, sections):
    pairs = []
    for s in sections:
        for z in range(2):
            for x in range(RING):
                base = s * 2 * RING + z * RING
                pairs.append((base + x, base + (x + by) % RING))
    return lax.ppermute(array, ("section", "dp"), pairs)


def across_z(array):
    return lax.ppermute(array, "dp", [(d, (d + RING) % (2 * RING)) for d in range(2 * RING)])


def other_core(array):
    return lax.ppermute(array, "tensor", [(0, 1), (1, 0)])


def relay(array, sections, count):
    return lax.ppermute(array, "section", [(s, (s + 1) % count) for s in sections])


def after(array, *others):
    return lax.optimization_barrier((array,) + others)[0]


def copy_all(copies):
    for copy in copies:
        copy.start()
    return copies


def wait_all(copies):
    for copy in copies:
        copy.wait()


def call(kernel, outs, in_specs, out_specs, scratch=(), flops=0, moved=0):
    return pl.pallas_call(
        kernel,
        out_shape=outs,
        in_specs=in_specs,
        out_specs=out_specs,
        scratch_shapes=list(scratch),
        compiler_params=pltpu.CompilerParams(vmem_limit_bytes=VMEM_LIMIT),
        cost_estimate=pl.CostEstimate(flops=flops, bytes_accessed=moved, transcendentals=0),
    )


def quarter_kernel(where, weight, *pieces):
    x = where[0]
    width = pieces[0].shape[2]
    for step, piece in enumerate(pieces):
        start = pl.multiple_of(((x + step) % RING) * width, width)
        piece[...] = weight[:, :, pl.ds(start, width)]


def quarters(where, weight):
    planes, rows, columns = weight.shape
    piece = jax.ShapeDtypeStruct((planes, rows, columns // RING), BF16)
    return call(
        quarter_kernel, (piece,) * RING, [SMEM, VMEM], (VMEM,) * RING, moved=4 * weight.size
    )(where, weight)


def norm_kernel(where, context, queries, gain, ctx_out, qry_out, ctx_norm, qry_norm, *scratch):
    ctx, qry, sems = scratch
    core = where[3]
    copies = copy_all(
        [
            pltpu.make_async_copy(context.at[core], ctx, sems.at[0]),
            pltpu.make_async_copy(queries.at[core], qry, sems.at[1]),
        ]
    )
    step = 32

    def rows_of(source, raw, target):
        @pl.loop(0, source.shape[0] // step)
        def _(i):
            at = pl.ds(pl.multiple_of(i * step, step), step)
            low = source[at, :]
            wide = low.astype(F32)
            mean = jnp.mean(wide * wide, axis=-1, keepdims=True)
            target[at, :] = (wide * lax.rsqrt(mean + 1e-06) * gain[...]).astype(BF16)
            raw[at, :] = low

    copies[0].wait()
    rows_of(ctx, ctx_out, ctx_norm)
    copies[1].wait()
    rows_of(qry, qry_out, qry_norm)


def norm_scene(where, context, queries, gain):
    ctx = jax.ShapeDtypeStruct(context.shape[1:], BF16)
    qry = jax.ShapeDtypeStruct(queries.shape[1:], BF16)
    return call(
        norm_kernel,
        (ctx, qry, ctx, qry),
        [SMEM, ANY, ANY, VMEM],
        (VMEM,) * 4,
        [
            pltpu.VMEM(ctx.shape, BF16),
            pltpu.VMEM(qry.shape, BF16),
            pltpu.SemaphoreType.DMA((2,)),
        ],
        moved=6 * ctx.size,
    )(where, context, queries, gain)


def attend_kernel(where, lengths, *refs):
    ctx = refs[:5]
    qry = refs[5:9]
    near = refs[9:17]
    far = refs[17:25]
    outs = refs[25:29]
    rows_all, qry_all, weight, q_buf, k_buf, v_buf, mixed, sems = refs[29:]
    x, z, encoder = where[0], where[1], where[2]
    mem = rows_all.shape[1]
    few = qry_all.shape[1]
    part = near[0].shape[2]
    block = near[0].shape[1]
    half = mem // 2
    copies = [
        pltpu.make_async_copy(ctx[0], rows_all.at[0], sems.at[0]),
        pltpu.make_async_copy(ctx[1], rows_all.at[1], sems.at[1]),
        pltpu.make_async_copy(ctx[2], rows_all.at[2, pl.ds(0, half)], sems.at[2]),
        pltpu.make_async_copy(ctx[3], rows_all.at[2, pl.ds(half, half)], sems.at[3]),
        pltpu.make_async_copy(ctx[4], rows_all.at[3], sems.at[4]),
    ]
    for slot in range(RING):
        copies.append(pltpu.make_async_copy(qry[slot], qry_all.at[slot], sems.at[5 + slot]))
    for side, (group, high) in enumerate(((near, z), (far, 1 - z))):
        for step in range(RING):
            first = (high * RING + (x - step + RING) % RING) * block
            first = pl.multiple_of(first, block)
            for side_core in range(2):
                copies.append(
                    pltpu.make_async_copy(
                        group[side_core * RING + step],
                        weight.at[:, pl.ds(first, block), pl.ds(side_core * part, part)],
                        sems.at[9 + side * 8 + step * 2 + side_core],
                    )
                )
    copy_all(copies)
    wait_all(copies)
    heads = 2 * part // HEAD
    scale = 1.0 / math.sqrt(HEAD)
    column = lax.broadcasted_iota(jnp.int32, (mem, mem), 1)

    @pl.loop(0, RING)
    def _(slot):
        rows = rows_all[slot]

        @pl.when(encoder == 1)
        def _():
            q_buf[...] = jnp.dot(rows, weight[0], preferred_element_type=F32).astype(BF16)

        @pl.when(encoder == 0)
        def _():
            q_buf[...] = jnp.zeros_like(q_buf)
            q_buf[pl.ds(0, few), :] = jnp.dot(
                qry_all[slot], weight[0], preferred_element_type=F32
            ).astype(BF16)

        k_buf[...] = jnp.dot(rows, weight[1], preferred_element_type=F32).astype(BF16)
        v_buf[...] = jnp.dot(rows, weight[2], preferred_element_type=F32).astype(BF16)
        valid = column < lengths[slot]
        for head in range(heads):
            at = pl.ds(head * HEAD, HEAD)
            scores = (
                lax.dot_general(
                    q_buf[:, at],
                    k_buf[:, at],
                    (((1,), (1,)), ((), ())),
                    preferred_element_type=F32,
                )
                * scale
            )
            scores = jnp.where(valid, scores, -1e30)
            expo = jnp.exp(scores - jnp.max(scores, axis=-1, keepdims=True))
            probs = (expo / jnp.sum(expo, axis=-1, keepdims=True)).astype(BF16)
            mixed[slot, :, at] = jnp.dot(
                probs, v_buf[:, at], preferred_element_type=F32
            ).astype(BF16)

    wait_all(
        copy_all(
            [
                pltpu.make_async_copy(mixed.at[slot], outs[slot], sems.at[slot])
                for slot in range(RING)
            ]
        )
    )


def attend(where, lengths, ctx, qry, near, far):
    mem, width = ctx[0].shape
    few = qry[0].shape[0]
    planes, block, part = near[0].shape
    out = jax.ShapeDtypeStruct((mem, 2 * part), BF16)
    operands = (*ctx, *qry, *near, *far)
    return call(
        attend_kernel,
        (out,) * RING,
        [SMEM, SMEM] + [ANY] * len(operands),
        (ANY,) * RING,
        [
            pltpu.VMEM((RING, mem, width), BF16),
            pltpu.VMEM((RING, few, width), BF16),
            pltpu.VMEM((planes, width, 2 * part), BF16),
            pltpu.VMEM((mem, 2 * part), BF16),
            pltpu.VMEM((mem, 2 * part), BF16),
            pltpu.VMEM((mem, 2 * part), BF16),
            pltpu.VMEM((RING, mem, 2 * part), BF16),
            pltpu.SemaphoreType.DMA((25,)),
        ],
        flops=2 * RING * mem * width * planes * 2 * part,
        moved=2 * (RING * mem * width + planes * width * 2 * part),
    )(where, lengths, *operands)


def project_kernel(crossed, where, context, queries, *refs):
    mixed = refs[:4]
    weights = refs[4:12]
    out = refs[12]
    heads, weight, base, sems = refs[13:]
    x, z, encoder, core = where[0], where[1], where[2], where[3]
    part = mixed[0].shape[1] // 2
    inner, block = weights[0].shape
    half = (1 - z) if crossed else z
    first = pl.multiple_of(half * RING * block, RING * block)
    few = queries.shape[1]

    @pl.when(encoder == 1)
    def _():
        pltpu.make_async_copy(
            context.at[core, :, pl.ds(first, RING * block)], base, sems.at[0]
        ).start()

    @pl.when(encoder == 0)
    def _():
        pltpu.make_async_copy(
            queries.at[core, :, pl.ds(first, RING * block)],
            base.at[pl.ds(0, few)],
            sems.at[0],
        ).start()

    copies = []
    for step in range(RING):
        for side in range(2):
            at = pl.multiple_of(side * inner + ((x + step) % RING) * part, part)
            copies.append(
                pltpu.make_async_copy(
                    mixed[step].at[:, pl.ds(side * part, part)],
                    heads.at[:, pl.ds(at, part)],
                    sems.at[1 + step * 2 + side],
                )
            )
    pieces = []
    for step in range(RING):
        for side in range(2):
            pieces.append(
                pltpu.make_async_copy(
                    weights[side * RING + step],
                    weight.at[step, pl.ds(side * inner, inner)],
                    sems.at[9 + step * 2 + side],
                )
            )
    copy_all(copies)
    copy_all(pieces)

    @pl.when(encoder == 1)
    def _():
        pltpu.make_async_copy(
            context.at[core, :, pl.ds(first, RING * block)], base, sems.at[0]
        ).wait()

    @pl.when(encoder == 0)
    def _():
        pltpu.make_async_copy(
            queries.at[core, :, pl.ds(first, RING * block)],
            base.at[pl.ds(0, few)],
            sems.at[0],
        ).wait()

    wait_all(copies)
    for step in range(RING):
        wait_all(pieces[2 * step : 2 * step + 2])
        at = pl.ds(pl.multiple_of(((x - step + RING) % RING) * block, block), block)
        update = jnp.dot(heads[...], weight[step], preferred_element_type=F32)
        out[:, at] = (base[:, at].astype(F32) + update).astype(BF16)


def project(crossed, where, context, queries, mixed, weights):
    mem = context.shape[1]
    inner, block = weights[0].shape
    return call(
        functools.partial(project_kernel, crossed),
        jax.ShapeDtypeStruct((mem, RING * block), BF16),
        [SMEM] + [ANY] * 14,
        VMEM,
        [
            pltpu.VMEM((mem, 2 * inner), BF16),
            pltpu.VMEM((RING, 2 * inner, block), BF16),
            pltpu.VMEM((mem, RING * block), BF16),
            pltpu.SemaphoreType.DMA((17,)),
        ],
        flops=2 * mem * 2 * inner * RING * block,
        moved=2 * (2 * inner * RING * block + 3 * mem * inner),
    )(where, context, queries, *mixed, *weights)


def gather_kernel(where, *refs):
    near, far, ctx, qry = refs[0:2], refs[2:4], refs[4:6], refs[6:8]
    ctx_out, qry_out, sems = refs[8:]
    z, core, from_encoder = where[1], where[3], where[4]
    width = near[0].shape[1]
    few = qry[0].shape[0]

    @pl.when(from_encoder == 1)
    def _():
        copies = []
        for side in range(2):
            scene = core if side == 0 else 1 - core
            for i, (piece, half) in enumerate(((near, z), (far, 1 - z))):
                at = pl.ds(pl.multiple_of(half * width, width), width)
                copies.append(
                    pltpu.make_async_copy(
                        piece[side], ctx_out.at[scene, :, at], sems.at[3 * side + i]
                    )
                )
            copies.append(
                pltpu.make_async_copy(qry[side], qry_out.at[scene], sems.at[3 * side + 2])
            )
        wait_all(copy_all(copies))

    @pl.when(from_encoder == 0)
    def _():
        copies = []
        for side in range(2):
            scene = core if side == 0 else 1 - core
            for i, (piece, half) in enumerate(((near, z), (far, 1 - z))):
                at = pl.ds(pl.multiple_of(half * width, width), width)
                copies.append(
                    pltpu.make_async_copy(
                        piece[side].at[pl.ds(0, few)],
                        qry_out.at[scene, :, at],
                        sems.at[3 * side + i],
                    )
                )
            copies.append(
                pltpu.make_async_copy(ctx[side], ctx_out.at[scene], sems.at[3 * side + 2])
            )
        wait_all(copy_all(copies))


def gather_result(where, near, far, ctx, qry):
    mem, width = ctx[0].shape
    few = qry[0].shape[0]
    return call(
        gather_kernel,
        (
            jax.ShapeDtypeStruct((2, mem, width), BF16),
            jax.ShapeDtypeStruct((2, few, width), BF16),
        ),
        [SMEM] + [ANY] * 8,
        (ANY, ANY),
        [pltpu.SemaphoreType.DMA((6,))],
        moved=8 * mem * width,
    )(where, *near, *far, *ctx, *qry)


def per_device(context, queries, lengths, norm_gain, qkv_weight, out_weight):
    count = lax.axis_size("section")
    section = lax.axis_index("section")
    place = lax.axis_index("dp")
    core = lax.axis_index("tensor")
    encoders = list(range(count // 2))
    decoders = list(range(count // 2, count))
    before = (section + count - 1) % count
    where = jnp.stack(
        [
            place % RING,
            place // RING,
            (section < count // 2).astype(jnp.int32),
            core,
            (before < count // 2).astype(jnp.int32),
        ]
    ).astype(jnp.int32)
    context, queries = context[0], queries[0]

    own = quarters(where, jnp.swapaxes(qkv_weight[0], 0, 1))
    near = [own[0]] + [around_x(own[step], step) for step in range(1, RING)]
    far = [across_z(piece) for piece in near]
    near_both = near + [other_core(piece) for piece in near]
    far_both = far + [other_core(piece) for piece in far]

    ctx, qry, ctx_norm, qry_norm = norm_scene(where, context, queries, norm_gain)
    half = ctx_norm.shape[0] // 2
    ctx_norm_sent = after(ctx_norm, near[1], near[2], near[3])
    from_left = around_x(ctx_norm_sent, 1)
    from_right = around_x(ctx_norm_sent, -1)
    opposite = [around_x(from_left[:half], 1), around_x(from_right[half:], -1)]
    ctx_rows = [ctx_norm, from_left, *opposite, from_right]
    qry_rows = [qry_norm] + [around_x_of(qry_norm, step, decoders) for step in range(1, RING)]
    length = jnp.full((8, 128), lax.dynamic_index_in_dim(lengths[0], core, keepdims=False))
    all_lengths = jnp.stack(
        [length[0, 0]] + [around_x(length, step)[0, 0] for step in range(1, RING)]
    )

    shard = after(out_weight[0], from_left, from_right)
    out_near = [shard] + [around_x(shard, step) for step in range(1, RING)]
    out_near += [other_core(piece) for piece in out_near]
    shard = across_z(after(out_weight[0], *far))
    out_far = [shard] + [around_x(shard, step) for step in range(1, RING)]
    out_far += [other_core(piece) for piece in out_far]

    ctx_early = relay(after(ctx, *far), decoders, count)
    qry_early = relay(after(qry, *far), encoders, count)

    mixed = attend(where, all_lengths, ctx_rows, qry_rows, near_both, far_both)
    mixed = [mixed[0]] + [around_x(mixed[step], -step) for step in range(1, RING)]

    everyone = encoders + decoders
    result_near = project(False, where, context, queries, mixed, out_near)
    sent_near = relay(result_near, everyone, count)
    result_far = project(True, where, context, queries, mixed, out_far)
    sent_far = relay(result_far, everyone, count)
    ctx_new, qry_new = gather_result(
        where,
        (sent_near, other_core(sent_near)),
        (sent_far, other_core(sent_far)),
        (ctx_early, other_core(ctx_early)),
        (qry_early, other_core(qry_early)),
    )
    return ctx_new[None], qry_new[None]


def solution(mesh):
    return jax.shard_map(
        per_device,
        mesh=mesh,
        in_specs=(
            P("section", "dp", None, None),
            P("section", "dp", None, None),
            P("section", "dp"),
            P("section", None),
            P("section", "dp", None, "tensor"),
            P("section", "tensor", "dp"),
        ),
        out_specs=(P("section", "dp", None, None), P("section", "dp", None, None)),
        check_vma=False,
    )
```

```python
import functools
import math

import jax
import jax.numpy as jnp
from jax import lax
from jax.experimental import pallas as pl
from jax.experimental.pallas import tpu as pltpu
from jax.sharding import PartitionSpec as P

HEAD = 128
RING = 4
ANY = pl.BlockSpec(memory_space=pl.ANY)
SMEM = pl.BlockSpec(memory_space=pltpu.SMEM)
VMEM = pl.BlockSpec(memory_space=pltpu.VMEM)
BF16 = jnp.bfloat16
F32 = jnp.float32


def around_x(array, by):
    pairs = [
        (z * RING + x, z * RING + (x + by) % RING) for z in range(2) for x in range(RING)
    ]
    return lax.ppermute(array, "dp", pairs)


def around_x_of(array, by, sections):
    pairs = []
    for s in sections:
        for z in range(2):
            for x in range(RING):
                base = s * 2 * RING + z * RING
                pairs.append((base + x, base + (x + by) % RING))
    return lax.ppermute(array, ("section", "dp"), pairs)


def across_z(array):
    return lax.ppermute(array, "dp", [(d, (d + RING) % (2 * RING)) for d in range(2 * RING)])


def other_core(array):
    return lax.ppermute(array, "tensor", [(0, 1), (1, 0)])


def relay(array, sections, count):
    return lax.ppermute(array, "section", [(s, (s + 1) % count) for s in sections])


def after(array, *others):
    return lax.optimization_barrier((array,) + others)[0]


def copy_all(copies):
    for copy in copies:
        copy.start()
    return copies


def wait_all(copies):
    for copy in copies:
        copy.wait()


def call(kernel, outs, in_specs, out_specs, scratch=(), flops=0, moved=0, limit=16):
    return pl.pallas_call(
        kernel,
        out_shape=outs,
        in_specs=in_specs,
        out_specs=out_specs,
        scratch_shapes=list(scratch),
        compiler_params=pltpu.CompilerParams(vmem_limit_bytes=limit * 1024 * 1024),
        cost_estimate=pl.CostEstimate(flops=flops, bytes_accessed=moved, transcendentals=0),
    )


def quarter_kernel(where, weight, *pieces):
    x = where[0]
    width = pieces[0].shape[2]
    for step, piece in enumerate(pieces):
        start = pl.multiple_of(((x + step) % RING) * width, width)
        piece[...] = weight[:, :, pl.ds(start, width)]


def quarters(where, weight):
    planes, rows, columns = weight.shape
    piece = jax.ShapeDtypeStruct((planes, rows, columns // RING), BF16)
    return call(
        quarter_kernel, (piece,) * RING, [SMEM, VMEM], (VMEM,) * RING, moved=4 * weight.size
    )(where, weight)


def norm_kernel(where, context, queries, gain, ctx_out, qry_out, ctx_norm, qry_norm, *scratch):
    ctx, qry, sems = scratch
    core = where[3]
    copies = copy_all(
        [
            pltpu.make_async_copy(context.at[core], ctx, sems.at[0]),
            pltpu.make_async_copy(queries.at[core], qry, sems.at[1]),
        ]
    )
    step = 32

    def rows_of(source, raw, target):
        @pl.loop(0, source.shape[0] // step)
        def _(i):
            at = pl.ds(pl.multiple_of(i * step, step), step)
            low = source[at, :]
            wide = low.astype(F32)
            mean = jnp.mean(wide * wide, axis=-1, keepdims=True)
            target[at, :] = (wide * lax.rsqrt(mean + 1e-06) * gain[...]).astype(BF16)
            raw[at, :] = low

    copies[0].wait()
    rows_of(ctx, ctx_out, ctx_norm)
    copies[1].wait()
    rows_of(qry, qry_out, qry_norm)


def norm_scene(where, context, queries, gain):
    ctx = jax.ShapeDtypeStruct(context.shape[1:], BF16)
    qry = jax.ShapeDtypeStruct(queries.shape[1:], BF16)
    return call(
        norm_kernel,
        (ctx, qry, ctx, qry),
        [SMEM, ANY, ANY, VMEM],
        (VMEM,) * 4,
        [
            pltpu.VMEM(ctx.shape, BF16),
            pltpu.VMEM(qry.shape, BF16),
            pltpu.SemaphoreType.DMA((2,)),
        ],
        moved=6 * ctx.size,
    )(where, context, queries, gain)


def attend_kernel(where, *refs):
    lengths = refs[:4]
    ctx = refs[4:9]
    qry = refs[9:13]
    near = refs[13:21]
    far = refs[21:29]
    outs = refs[29:33]
    rows_all, qry_all, weight, q_buf, k_buf, v_buf, mixed, sems = refs[33:]
    x, z, encoder = where[0], where[1], where[2]
    mem = rows_all.shape[1]
    few = qry_all.shape[1]
    part = near[0].shape[2]
    block = near[0].shape[1]
    half = mem // 2
    copies = [
        pltpu.make_async_copy(ctx[0], rows_all.at[0], sems.at[0]),
        pltpu.make_async_copy(ctx[1], rows_all.at[1], sems.at[1]),
        pltpu.make_async_copy(ctx[2], rows_all.at[2, pl.ds(0, half)], sems.at[2]),
        pltpu.make_async_copy(ctx[3], rows_all.at[2, pl.ds(half, half)], sems.at[3]),
        pltpu.make_async_copy(ctx[4], rows_all.at[3], sems.at[4]),
    ]
    for slot in range(RING):
        copies.append(pltpu.make_async_copy(qry[slot], qry_all.at[slot], sems.at[5 + slot]))
    for side, (group, high) in enumerate(((near, z), (far, 1 - z))):
        for step in range(RING):
            first = (high * RING + (x - step + RING) % RING) * block
            first = pl.multiple_of(first, block)
            for side_core in range(2):
                copies.append(
                    pltpu.make_async_copy(
                        group[side_core * RING + step],
                        weight.at[:, pl.ds(first, block), pl.ds(side_core * part, part)],
                        sems.at[9 + side * 8 + step * 2 + side_core],
                    )
                )
    copy_all(copies)
    wait_all(copies)
    heads = 2 * part // HEAD
    scale = 1.0 / math.sqrt(HEAD)
    column = lax.broadcasted_iota(jnp.int32, (mem, mem), 1)

    @pl.loop(0, RING)
    def _(slot):
        rows = rows_all[slot]

        @pl.when(encoder == 1)
        def _():
            q_buf[...] = jnp.dot(rows, weight[0], preferred_element_type=F32).astype(BF16)

        @pl.when(encoder == 0)
        def _():
            q_buf[...] = jnp.zeros_like(q_buf)
            q_buf[pl.ds(0, few), :] = jnp.dot(
                qry_all[slot], weight[0], preferred_element_type=F32
            ).astype(BF16)

        k_buf[...] = jnp.dot(rows, weight[1], preferred_element_type=F32).astype(BF16)
        v_buf[...] = jnp.dot(rows, weight[2], preferred_element_type=F32).astype(BF16)
        length = lengths[0][0, 0]
        for other in range(1, RING):
            length = jnp.where(slot == other, lengths[other][0, 0], length)
        valid = column < length
        for head in range(heads):
            at = pl.ds(head * HEAD, HEAD)
            scores = (
                lax.dot_general(
                    q_buf[:, at],
                    k_buf[:, at],
                    (((1,), (1,)), ((), ())),
                    preferred_element_type=F32,
                )
                * scale
            )
            scores = jnp.where(valid, scores, -1e30)
            expo = jnp.exp(scores - jnp.max(scores, axis=-1, keepdims=True))
            probs = (expo / jnp.sum(expo, axis=-1, keepdims=True)).astype(BF16)
            mixed[slot, :, at] = jnp.dot(
                probs, v_buf[:, at], preferred_element_type=F32
            ).astype(BF16)

    wait_all(
        copy_all(
            [
                pltpu.make_async_copy(mixed.at[slot], outs[slot], sems.at[slot])
                for slot in range(RING)
            ]
        )
    )


def attend(where, lengths, ctx, qry, near, far):
    mem, width = ctx[0].shape
    few = qry[0].shape[0]
    planes, block, part = near[0].shape
    out = jax.ShapeDtypeStruct((mem, 2 * part), BF16)
    operands = (*ctx, *qry, *near, *far)
    return call(
        attend_kernel,
        (out,) * RING,
        [SMEM] * 5 + [ANY] * len(operands),
        (ANY,) * RING,
        [
            pltpu.VMEM((RING, mem, width), BF16),
            pltpu.VMEM((RING, few, width), BF16),
            pltpu.VMEM((planes, width, 2 * part), BF16),
            pltpu.VMEM((mem, 2 * part), BF16),
            pltpu.VMEM((mem, 2 * part), BF16),
            pltpu.VMEM((mem, 2 * part), BF16),
            pltpu.VMEM((RING, mem, 2 * part), BF16),
            pltpu.SemaphoreType.DMA((25,)),
        ],
        flops=2 * RING * mem * width * planes * 2 * part,
        moved=2 * (RING * mem * width + planes * width * 2 * part),
        limit=24,
    )(where, *lengths, *operands)


def project_kernel(crossed, where, context, queries, *refs):
    mixed = refs[:4]
    weights = refs[4:12]
    out, few_out = refs[12:14]
    heads, weight, base, sems = refs[14:]
    x, z, encoder, core = where[0], where[1], where[2], where[3]
    part = mixed[0].shape[1] // 2
    inner, block = weights[0].shape
    half = (1 - z) if crossed else z
    first = pl.multiple_of(half * RING * block, RING * block)
    few = queries.shape[1]

    @pl.when(encoder == 1)
    def _():
        pltpu.make_async_copy(
            context.at[core, :, pl.ds(first, RING * block)], base, sems.at[0]
        ).start()

    @pl.when(encoder == 0)
    def _():
        pltpu.make_async_copy(
            queries.at[core, :, pl.ds(first, RING * block)],
            base.at[pl.ds(0, few)],
            sems.at[0],
        ).start()

    copies = []
    for step in range(RING):
        for side in range(2):
            at = pl.multiple_of(side * inner + ((x + step) % RING) * part, part)
            copies.append(
                pltpu.make_async_copy(
                    mixed[step].at[:, pl.ds(side * part, part)],
                    heads.at[:, pl.ds(at, part)],
                    sems.at[1 + step * 2 + side],
                )
            )
    pieces = []
    for step in range(RING):
        for side in range(2):
            pieces.append(
                pltpu.make_async_copy(
                    weights[side * RING + step],
                    weight.at[step, pl.ds(side * inner, inner)],
                    sems.at[9 + step * 2 + side],
                )
            )
    copy_all(copies)
    copy_all(pieces)

    @pl.when(encoder == 1)
    def _():
        pltpu.make_async_copy(
            context.at[core, :, pl.ds(first, RING * block)], base, sems.at[0]
        ).wait()

    @pl.when(encoder == 0)
    def _():
        pltpu.make_async_copy(
            queries.at[core, :, pl.ds(first, RING * block)],
            base.at[pl.ds(0, few)],
            sems.at[0],
        ).wait()

    wait_all(copies)
    for step in range(RING):
        wait_all(pieces[2 * step : 2 * step + 2])
        at = pl.ds(pl.multiple_of(((x - step + RING) % RING) * block, block), block)
        update = jnp.dot(heads[...], weight[step], preferred_element_type=F32)
        result = (base[:, at].astype(F32) + update).astype(BF16)
        out[:, at] = result
        few_out[:, at] = result[:few]


def project(crossed, where, context, queries, mixed, weights):
    mem = context.shape[1]
    inner, block = weights[0].shape
    return call(
        functools.partial(project_kernel, crossed),
        (
            jax.ShapeDtypeStruct((mem, RING * block), BF16),
            jax.ShapeDtypeStruct((queries.shape[1], RING * block), BF16),
        ),
        [SMEM] + [ANY] * 14,
        (VMEM, VMEM),
        [
            pltpu.VMEM((mem, 2 * inner), BF16),
            pltpu.VMEM((RING, 2 * inner, block), BF16),
            pltpu.VMEM((mem, RING * block), BF16),
            pltpu.SemaphoreType.DMA((17,)),
        ],
        flops=2 * mem * 2 * inner * RING * block,
        moved=2 * (2 * inner * RING * block + 3 * mem * inner),
    )(where, context, queries, *mixed, *weights)


def gather_kernel(where, *refs):
    ctx_half, qry_half = (refs[0:2], refs[2:4]), (refs[4:6], refs[6:8])
    ctx_whole, qry_whole = refs[8:10], refs[10:12]
    ctx_out, qry_out, ctx, qry, sems = refs[12:]
    z, core, from_encoder = where[1], where[3], where[4]
    width = ctx_half[0][0].shape[1]

    def build(halves, target, wholes, other):
        copies = []
        for side in range(2):
            scene = core if side == 0 else 1 - core
            for i, half in enumerate((z, 1 - z)):
                at = pl.ds(pl.multiple_of(half * width, width), width)
                copies.append(
                    pltpu.make_async_copy(
                        halves[i][side], target.at[scene, :, at], sems.at[3 * side + i]
                    )
                )
            copies.append(
                pltpu.make_async_copy(wholes[side], other.at[scene], sems.at[3 * side + 2])
            )
        wait_all(copy_all(copies))

    @pl.when(from_encoder == 1)
    def _():
        build(ctx_half, ctx, qry_whole, qry)

    @pl.when(from_encoder == 0)
    def _():
        build(qry_half, qry, ctx_whole, ctx)

    wait_all(
        copy_all(
            [
                pltpu.make_async_copy(ctx, ctx_out, sems.at[0]),
                pltpu.make_async_copy(qry, qry_out, sems.at[1]),
            ]
        )
    )


def gather_result(where, ctx_half, qry_half, ctx_whole, qry_whole):
    ctx_shape = (2,) + ctx_whole[0].shape
    qry_shape = (2,) + qry_whole[0].shape
    return call(
        gather_kernel,
        (jax.ShapeDtypeStruct(ctx_shape, BF16), jax.ShapeDtypeStruct(qry_shape, BF16)),
        [SMEM] + [ANY] * 12,
        (ANY, ANY),
        [
            pltpu.VMEM(ctx_shape, BF16),
            pltpu.VMEM(qry_shape, BF16),
            pltpu.SemaphoreType.DMA((6,)),
        ],
        moved=8 * ctx_whole[0].size,
    )(where, *ctx_half[0], *ctx_half[1], *qry_half[0], *qry_half[1], *ctx_whole, *qry_whole)


def both(array):
    return array, other_core(array)


def per_device(context, queries, lengths, norm_gain, qkv_weight, out_weight):
    count = lax.axis_size("section")
    section = lax.axis_index("section")
    place = lax.axis_index("dp")
    core = lax.axis_index("tensor")
    encoders = list(range(count // 2))
    decoders = list(range(count // 2, count))
    before = (section + count - 1) % count
    where = jnp.stack(
        [
            place % RING,
            place // RING,
            (section < count // 2).astype(jnp.int32),
            core,
            (before < count // 2).astype(jnp.int32),
        ]
    ).astype(jnp.int32)
    context, queries = context[0], queries[0]

    own = quarters(where, jnp.swapaxes(qkv_weight[0], 0, 1))
    far_own = across_z(own[0])
    near = [own[0]] + [around_x(own[step], step) for step in range(1, RING)]
    near_other = [other_core(piece) for piece in near]

    ctx, qry, ctx_norm, qry_norm = norm_scene(after(where, *own), context, queries, norm_gain)
    half = ctx_norm.shape[0] // 2
    ctx_sent = after(ctx_norm, *near)
    from_left = around_x(ctx_sent, 1)
    from_right = around_x(ctx_sent, -1)
    qry_sent = after(qry_norm, *near)
    qry_rows = [qry_norm] + [around_x_of(qry_sent, step, decoders) for step in range(1, RING)]
    length = jnp.full((1, 128), lax.dynamic_index_in_dim(lengths[0], core, keepdims=False))
    length_sent = after(length, *own)
    all_lengths = [length] + [around_x(length_sent, step) for step in range(1, RING)]

    far = [far_own]
    far.append(across_z(after(near[1], far_own)))
    far.append(
        across_z(
            after(near[2], far_own, from_left, from_right, *near_other, *qry_rows, *all_lengths)
        )
    )
    far.append(across_z(after(near[3], far_own)))
    far_other = [other_core(piece) for piece in far]
    opposite = [around_x(from_left[:half], 1), around_x(from_right[half:], -1)]
    ctx_rows = [ctx_norm, from_left, *opposite, from_right]

    shard = after(out_weight[0], from_left, from_right)
    out_left, out_right = around_x(shard, 1), around_x(shard, -1)
    out_opposite = around_x(after(shard, out_left, out_right), 2)
    out_near = [shard, out_left, out_opposite, out_right]
    out_near += [other_core(piece) for piece in out_near]
    far_shard = across_z(after(out_weight[0], *far, *opposite, out_left, out_right))
    out_far = [far_shard] + [around_x(far_shard, step) for step in range(1, RING)]
    out_far += [other_core(piece) for piece in out_far]

    ctx_early = relay(after(ctx, far_shard), decoders, count)
    qry_early = relay(after(qry, far_shard), encoders, count)

    mixed = attend(where, all_lengths, ctx_rows, qry_rows, near + near_other, far + far_other)
    mixed = [mixed[0]] + [around_x(mixed[step], -step) for step in range(1, RING)]

    near_ctx, near_qry = project(False, where, context, queries, mixed, out_near)
    near_ctx = relay(near_ctx, encoders, count)
    near_qry = relay(near_qry, decoders, count)
    far_ctx, far_qry = project(True, where, context, queries, mixed, out_far)
    far_ctx = relay(far_ctx, encoders, count)
    far_qry = relay(far_qry, decoders, count)
    ctx_new, qry_new = gather_result(
        where,
        (both(near_ctx), both(far_ctx)),
        (both(near_qry), both(far_qry)),
        both(ctx_early),
        both(qry_early),
    )
    return ctx_new[None], qry_new[None]


def solution(mesh):
    return jax.shard_map(
        per_device,
        mesh=mesh,
        in_specs=(
            P("section", "dp", None, None),
            P("section", "dp", None, None),
            P("section", "dp"),
            P("section", None),
            P("section", "dp", None, "tensor"),
            P("section", "tensor", "dp"),
        ),
        out_specs=(P("section", "dp", None, None), P("section", "dp", None, None)),
        check_vma=False,
    )
```

```python
import functools
import math

import jax
import jax.numpy as jnp
from jax import lax
from jax.experimental import pallas as pl
from jax.experimental.pallas import tpu as pltpu
from jax.sharding import PartitionSpec as P

HEAD = 128
RING = 4
TAIL = 16
HBM = pl.BlockSpec(memory_space=pltpu.HBM)
SMEM = pl.BlockSpec(memory_space=pltpu.SMEM)
VMEM = pl.BlockSpec(memory_space=pltpu.VMEM)
BF16 = jnp.bfloat16
F32 = jnp.float32


def around_x(array, by):
    pairs = [
        (z * RING + x, z * RING + (x + by) % RING) for z in range(2) for x in range(RING)
    ]
    return lax.ppermute(array, "dp", pairs)


def around_x_of(array, by, sections):
    pairs = []
    for s in sections:
        for z in range(2):
            for x in range(RING):
                base = s * 2 * RING + z * RING
                pairs.append((base + x, base + (x + by) % RING))
    return lax.ppermute(array, ("section", "dp"), pairs)


def across_z(array):
    return lax.ppermute(array, "dp", [(d, (d + RING) % (2 * RING)) for d in range(2 * RING)])


def other_core(array):
    return lax.ppermute(array, "tensor", [(0, 1), (1, 0)])


def relay(array, sections, count):
    return lax.ppermute(array, "section", [(s, (s + 1) % count) for s in sections])


def round_ring(array, half):
    left, right = around_x(array, 1), around_x(array, -1)
    return [array, left, around_x(left[:half], 1), around_x(right[half:], -1), right]


def after(array, *others):
    return lax.optimization_barrier((array,) + others)[0]


def copy_all(copies):
    for copy in copies:
        copy.start()
    return copies


def wait_all(copies):
    for copy in copies:
        copy.wait()


def call(kernel, outs, in_specs, out_specs, scratch=(), flops=0, moved=0, limit=16):
    return pl.pallas_call(
        kernel,
        out_shape=outs,
        in_specs=in_specs,
        out_specs=out_specs,
        scratch_shapes=list(scratch),
        compiler_params=pltpu.CompilerParams(vmem_limit_bytes=limit * 1024 * 1024),
        cost_estimate=pl.CostEstimate(flops=flops, bytes_accessed=moved, transcendentals=0),
    )


def quarter_kernel(where, weight, *pieces):
    x = where[0]
    width = pieces[0].shape[2]
    for step, piece in enumerate(pieces):
        start = pl.multiple_of(((x + step) % RING) * width, width)
        piece[...] = weight[:, :, pl.ds(start, width)]


def quarters(where, weight):
    planes, rows, columns = weight.shape
    piece = jax.ShapeDtypeStruct((planes, rows, columns // RING), BF16)
    return call(
        quarter_kernel, (piece,) * RING, [SMEM, VMEM], (VMEM,) * RING, moved=4 * weight.size
    )(where, weight)


def norm_kernel(
    where, context, queries, gain, lengths, ctx_out, qry_out, ctx_norm, qry_norm, *scratch
):
    ctx, qry, sems = scratch
    core = where[3]
    copies = copy_all(
        [
            pltpu.make_async_copy(context.at[core], ctx, sems.at[0]),
            pltpu.make_async_copy(queries.at[core], qry, sems.at[1]),
        ]
    )
    step = 32

    def rows_of(source, raw, target):
        @pl.loop(0, source.shape[0] // step)
        def _(i):
            at = pl.ds(pl.multiple_of(i * step, step), step)
            low = source[at, :]
            wide = low.astype(F32)
            mean = jnp.mean(wide * wide, axis=-1, keepdims=True)
            target[at, :] = (wide * lax.rsqrt(mean + 1e-06) * gain[...]).astype(BF16)
            raw[at, :] = low

    tail = ctx_norm.shape[0] - ctx.shape[0]
    length = lengths[core].astype(F32)
    ctx_norm[pl.ds(ctx.shape[0], tail), :] = jnp.full((tail, ctx.shape[1]), length).astype(BF16)
    copies[0].wait()
    rows_of(ctx, ctx_out, ctx_norm)
    copies[1].wait()
    rows_of(qry, qry_out, qry_norm)


def norm_scene(where, context, queries, gain, lengths):
    ctx = jax.ShapeDtypeStruct(context.shape[1:], BF16)
    qry = jax.ShapeDtypeStruct(queries.shape[1:], BF16)
    tailed = jax.ShapeDtypeStruct((ctx.shape[0] + TAIL, ctx.shape[1]), BF16)
    return call(
        norm_kernel,
        (ctx, qry, tailed, qry),
        [SMEM, HBM, HBM, VMEM, SMEM],
        (VMEM,) * 4,
        [
            pltpu.VMEM(ctx.shape, BF16),
            pltpu.VMEM(qry.shape, BF16),
            pltpu.SemaphoreType.DMA((2,)),
        ],
        moved=6 * ctx.size,
    )(where, context, queries, gain, lengths)


def operand_copies(high, x, ctx, qry, group, rows_all, qry_all, weight, sems):
    mem, few = rows_all.shape[0] // RING, qry_all.shape[0] // RING
    half = mem // 2
    _, block, part = group[0].shape
    at = pl.ds(pl.multiple_of(high * RING * block, RING * block), RING * block)
    copies = []
    starts = (0, mem, 2 * mem, 2 * mem + half, 3 * mem)
    counts = (mem, mem, half, half, mem)
    for i, (piece, start, count) in enumerate(zip(ctx, starts, counts)):
        target = rows_all.at[pl.ds(start, count)]
        copies.append(pltpu.make_async_copy(piece.at[pl.ds(0, count), at], target, sems.at[i]))
    for slot in range(RING):
        target = qry_all.at[pl.ds(slot * few, few)]
        copies.append(pltpu.make_async_copy(qry[slot].at[:, at], target, sems.at[5 + slot]))
    for step in range(RING):
        first = pl.multiple_of(((x - step + RING) % RING) * block, block)
        for side in range(2):
            copies.append(
                pltpu.make_async_copy(
                    group[side * RING + step],
                    weight.at[:, pl.ds(first, block), pl.ds(side * part, part)],
                    sems.at[9 + step * 2 + side],
                )
            )
    return copies


def start_kernel(where, *refs):
    ctx, qry, group = refs[:5], refs[5:9], refs[9:17]
    total, rows_all, qry_all, weight, sems = refs[17:]
    wait_all(
        copy_all(
            operand_copies(where[1], where[0], ctx, qry, group, rows_all, qry_all, weight, sems)
        )
    )
    few = qry_all.shape[0]

    @pl.when(where[2] == 1)
    def _():
        total[0] = jnp.dot(rows_all[...], weight[0], preferred_element_type=F32)

    @pl.when(where[2] == 0)
    def _():
        total[0, pl.ds(0, few)] = jnp.dot(qry_all[...], weight[0], preferred_element_type=F32)

    @pl.loop(1, 3)
    def _(plane):
        total[plane] = jnp.dot(rows_all[...], weight[plane], preferred_element_type=F32)


def attend_kernel(where, *refs):
    ctx, qry, parts, total_in = refs[:5], refs[5:9], refs[9:15], refs[15]
    outs = refs[16:20]
    rows_all, qry_all, weight, total, lengths, low, mixed, sems = refs[20:]
    group = []
    for own, sides, opposite in (parts[:3], parts[3:]):
        group += [own, sides.at[0], opposite, sides.at[1]]
    copies = operand_copies(
        1 - where[1], where[0], ctx, qry, group, rows_all, qry_all, weight, sems
    )
    for slot, piece in enumerate((ctx[0], ctx[1], ctx[3], ctx[4])):
        source = piece.at[pl.ds(piece.shape[0] - TAIL, TAIL), pl.ds(0, 128)]
        copies.append(pltpu.make_async_copy(source, lengths.at[slot], sems.at[17 + slot]))
    copy_all(copies)
    totals = copy_all(
        [
            pltpu.make_async_copy(total_in.at[plane], total.at[plane], sems.at[21 + plane])
            for plane in range(3)
        ]
    )
    wait_all(copies)
    wait_all(totals)
    mem, few = rows_all.shape[0] // RING, qry_all.shape[0] // RING
    encoder = where[2]

    @pl.when(encoder == 1)
    def _():
        low[0] = (
            total[0] + jnp.dot(rows_all[...], weight[0], preferred_element_type=F32)
        ).astype(BF16)

    @pl.when(encoder == 0)
    def _():
        at = pl.ds(0, RING * few)
        low[0, at] = (
            total[0, at] + jnp.dot(qry_all[...], weight[0], preferred_element_type=F32)
        ).astype(BF16)

    @pl.loop(1, 3)
    def _(plane):
        low[plane] = (
            total[plane] + jnp.dot(rows_all[...], weight[plane], preferred_element_type=F32)
        ).astype(BF16)

    heads = low.shape[2] // HEAD
    scale = 1.0 / math.sqrt(HEAD)

    def heads_of(count):
        column = lax.broadcasted_iota(jnp.int32, (count, mem), 1)

        @pl.loop(0, RING)
        def _(slot):
            own = pl.ds(pl.multiple_of(slot * count, count), count)
            keys = pl.ds(pl.multiple_of(slot * mem, mem), mem)
            length = lengths[slot, pl.ds(0, 1), pl.ds(0, 1)].astype(F32).astype(jnp.int32)
            valid = column < length
            for head in range(heads):
                at = pl.ds(head * HEAD, HEAD)
                scores = (
                    lax.dot_general(
                        low[0, own, at],
                        low[1, keys, at],
                        (((1,), (1,)), ((), ())),
                        preferred_element_type=F32,
                    )
                    * scale
                )
                scores = jnp.where(valid, scores, -1e30)
                expo = jnp.exp(scores - jnp.max(scores, axis=-1, keepdims=True))
                probs = (expo / jnp.sum(expo, axis=-1, keepdims=True)).astype(BF16)
                mixed[slot, pl.ds(0, count), at] = jnp.dot(
                    probs, low[2, keys, at], preferred_element_type=F32
                ).astype(BF16)

    @pl.when(encoder == 1)
    def _():
        heads_of(mem)

    @pl.when(encoder == 0)
    def _():
        heads_of(few)

    wait_all(
        copy_all(
            [
                pltpu.make_async_copy(mixed.at[slot], outs[slot], sems.at[slot])
                for slot in range(RING)
            ]
        )
    )


def operand_buffers(ctx, qry, group):
    mem, width = ctx[0].shape
    mem -= TAIL
    few = qry[0].shape[0]
    planes, block, part = group[0].shape
    return [
        pltpu.VMEM((RING * mem, width // 2), BF16),
        pltpu.VMEM((RING * few, width // 2), BF16),
        pltpu.VMEM((planes, width // 2, 2 * part), BF16),
    ]


def start_projections(where, ctx, qry, group):
    mem, width = ctx[0].shape
    mem -= TAIL
    planes, block, part = group[0].shape
    operands = (*ctx, *qry, *group)
    return call(
        start_kernel,
        jax.ShapeDtypeStruct((planes, RING * mem, 2 * part), F32),
        [SMEM] + [HBM] * len(operands),
        VMEM,
        operand_buffers(ctx, qry, group) + [pltpu.SemaphoreType.DMA((17,))],
        flops=RING * mem * width * planes * 2 * part,
        moved=RING * mem * width + planes * width * 2 * part,
        limit=24,
    )(where, *operands)


def attend(where, ctx, qry, group, total):
    mem, width = ctx[0].shape
    mem -= TAIL
    planes, block, part = group[0].shape
    out = jax.ShapeDtypeStruct((mem, 2 * part), BF16)
    operands = (*ctx, *qry, *group)
    return call(
        attend_kernel,
        (out,) * RING,
        [SMEM] + [HBM] * (len(operands) + 1),
        (HBM,) * RING,
        operand_buffers(ctx, qry, group)
        + [
            pltpu.VMEM(total.shape, F32),
            pltpu.VMEM((RING, TAIL, 128), BF16),
            pltpu.VMEM((planes, RING * mem, 2 * part), BF16),
            pltpu.VMEM((RING, mem, 2 * part), BF16),
            pltpu.SemaphoreType.DMA((24,)),
        ],
        flops=RING * mem * width * planes * 2 * part,
        moved=RING * mem * width + planes * width * 2 * part,
        limit=28,
    )(where, *operands, total)


def project_kernel(crossed, where, context, queries, *refs):
    mixed = refs[:4]
    weights = refs[4:14]
    out, few_out = refs[14:16]
    heads, weight, base, sems = refs[16:]
    x, z, encoder, core = where[0], where[1], where[2], where[3]
    part = mixed[0].shape[1] // 2
    inner, block = weights[0].shape
    half = (1 - z) if crossed else z
    first = pl.multiple_of(half * RING * block, RING * block)
    few = queries.shape[1]

    @pl.when(encoder == 1)
    def _():
        pltpu.make_async_copy(
            context.at[core, :, pl.ds(first, RING * block)], base, sems.at[0]
        ).start()

    @pl.when(encoder == 0)
    def _():
        pltpu.make_async_copy(
            queries.at[core, :, pl.ds(first, RING * block)],
            base.at[pl.ds(0, few)],
            sems.at[0],
        ).start()

    copies = []
    for step in range(RING):
        for side in range(2):
            at = pl.multiple_of(side * inner + ((x + step) % RING) * part, part)
            copies.append(
                pltpu.make_async_copy(
                    mixed[step].at[:, pl.ds(side * part, part)],
                    heads.at[:, pl.ds(at, part)],
                    sems.at[1 + step * 2 + side],
                )
            )
    pieces = []
    for i, (step, start) in enumerate(((0, 0), (1, 0), (2, 0), (2, inner // 2), (3, 0))):
        for side in range(2):
            piece = weights[side * 5 + i]
            pieces.append(
                pltpu.make_async_copy(
                    piece,
                    weight.at[step, pl.ds(side * inner + start, piece.shape[0])],
                    sems.at[9 + i * 2 + side],
                )
            )
    needed = (pieces[0:2], pieces[2:4], pieces[4:8], pieces[8:10])
    copy_all(copies)
    copy_all(pieces)

    @pl.when(encoder == 1)
    def _():
        pltpu.make_async_copy(
            context.at[core, :, pl.ds(first, RING * block)], base, sems.at[0]
        ).wait()

    @pl.when(encoder == 0)
    def _():
        pltpu.make_async_copy(
            queries.at[core, :, pl.ds(first, RING * block)],
            base.at[pl.ds(0, few)],
            sems.at[0],
        ).wait()

    wait_all(copies)
    for step in range(RING):
        wait_all(needed[step])
        at = pl.ds(pl.multiple_of(((x - step + RING) % RING) * block, block), block)
        update = jnp.dot(heads[...], weight[step], preferred_element_type=F32)
        result = (base[:, at].astype(F32) + update).astype(BF16)
        out[:, at] = result
        few_out[:, at] = result[:few]


def project(crossed, where, context, queries, mixed, weights):
    mem = context.shape[1]
    inner, block = weights[0].shape
    return call(
        functools.partial(project_kernel, crossed),
        (
            jax.ShapeDtypeStruct((mem, RING * block), BF16),
            jax.ShapeDtypeStruct((queries.shape[1], RING * block), BF16),
        ),
        [SMEM] + [HBM] * 16,
        (VMEM, VMEM),
        [
            pltpu.VMEM((mem, 2 * inner), BF16),
            pltpu.VMEM((RING, 2 * inner, block), BF16),
            pltpu.VMEM((mem, RING * block), BF16),
            pltpu.SemaphoreType.DMA((19,)),
        ],
        flops=2 * mem * 2 * inner * RING * block,
        moved=2 * (2 * inner * RING * block + 3 * mem * inner),
    )(where, context, queries, *mixed, *weights)


def gather_kernel(where, *refs):
    ctx_half, qry_half = (refs[0:2], refs[2:4]), (refs[4:6], refs[6:8])
    ctx_whole, qry_whole = refs[8:10], refs[10:12]
    ctx_out, qry_out, ctx, qry, sems = refs[12:]
    z, core, from_encoder = where[1], where[3], where[4]
    width = ctx_half[0][0].shape[1]

    def build(halves, target, wholes, other):
        copies = []
        for side in range(2):
            scene = core if side == 0 else 1 - core
            for i, half in enumerate((z, 1 - z)):
                at = pl.ds(pl.multiple_of(half * width, width), width)
                copies.append(
                    pltpu.make_async_copy(
                        halves[i][side], target.at[scene, :, at], sems.at[3 * side + i]
                    )
                )
            copies.append(
                pltpu.make_async_copy(wholes[side], other.at[scene], sems.at[3 * side + 2])
            )
        wait_all(copy_all(copies))

    @pl.when(from_encoder == 1)
    def _():
        build(ctx_half, ctx, qry_whole, qry)

    @pl.when(from_encoder == 0)
    def _():
        build(qry_half, qry, ctx_whole, ctx)

    wait_all(
        copy_all(
            [
                pltpu.make_async_copy(ctx, ctx_out, sems.at[0]),
                pltpu.make_async_copy(qry, qry_out, sems.at[1]),
            ]
        )
    )


def gather_result(where, ctx_half, qry_half, ctx_whole, qry_whole):
    ctx_shape = (2,) + ctx_whole[0].shape
    qry_shape = (2,) + qry_whole[0].shape
    return call(
        gather_kernel,
        (jax.ShapeDtypeStruct(ctx_shape, BF16), jax.ShapeDtypeStruct(qry_shape, BF16)),
        [SMEM] + [HBM] * 12,
        (HBM, HBM),
        [
            pltpu.VMEM(ctx_shape, BF16),
            pltpu.VMEM(qry_shape, BF16),
            pltpu.SemaphoreType.DMA((6,)),
        ],
        moved=8 * ctx_whole[0].size,
    )(where, *ctx_half[0], *ctx_half[1], *qry_half[0], *qry_half[1], *ctx_whole, *qry_whole)


def both(array):
    return array, other_core(array)


def per_device(context, queries, lengths, norm_gain, qkv_weight, out_weight):
    count = lax.axis_size("section")
    section = lax.axis_index("section")
    place = lax.axis_index("dp")
    core = lax.axis_index("tensor")
    encoders = list(range(count // 2))
    decoders = list(range(count // 2, count))
    before = (section + count - 1) % count
    where = jnp.stack(
        [
            place % RING,
            place // RING,
            (section < count // 2).astype(jnp.int32),
            core,
            (before < count // 2).astype(jnp.int32),
        ]
    ).astype(jnp.int32)
    context, queries = context[0], queries[0]

    own = quarters(where, jnp.swapaxes(qkv_weight[0], 0, 1))
    far_own = across_z(own[0])
    near = [own[0]] + [around_x(own[step], step) for step in range(1, RING)]
    near_other = [other_core(piece) for piece in near]

    ctx, qry, ctx_norm, qry_norm = norm_scene(
        after(where, *own), context, queries, norm_gain, lengths[0]
    )
    qry_rows = [qry_norm] + [around_x_of(qry_norm, step, decoders) for step in range(1, RING)]
    ctx_rows = round_ring(after(ctx_norm, far_own, *near), ctx.shape[0] // 2)
    far_sides = across_z(after(jnp.stack([near[1], near[3]]), far_own))
    far_opposite = across_z(after(near[2], ctx_rows[1], ctx_rows[4]))

    shard = out_weight[0]
    out_near = round_ring(after(shard, far_sides, *ctx_rows[1:]), shard.shape[0] // 2)
    total = start_projections(where, ctx_rows, qry_rows, near + near_other)
    far = [far_own, far_sides, far_opposite]
    far_shard = across_z(after(shard, *far, total, out_near[1], out_near[4]))
    out_far = round_ring(far_shard, shard.shape[0] // 2)
    far += [other_core(far_own), other_core(far_sides), other_core(after(far_opposite, total))]

    mixed = attend(
        after(where, *out_near), ctx_rows, qry_rows, far, total
    )
    mixed = [mixed[0]] + [around_x(mixed[step], -step) for step in range(1, RING)]
    out_near += [other_core(piece) for piece in out_near]
    out_far += [other_core(piece) for piece in out_far]

    ctx_early = relay(after(ctx, far_shard), decoders, count)
    qry_early = relay(after(qry, far_shard), encoders, count)

    near_ctx, near_qry = project(
        False, after(where, qry_early), context, queries, mixed, out_near
    )
    near_ctx = relay(near_ctx, encoders, count)
    near_qry = relay(near_qry, decoders, count)
    far_ctx, far_qry = project(True, after(where, ctx_early), context, queries, mixed, out_far)
    far_ctx = relay(far_ctx, encoders, count)
    far_qry = relay(far_qry, decoders, count)
    near_sent = after(near_ctx, near_qry)
    ctx_new, qry_new = gather_result(
        where,
        ((near_ctx, other_core(near_sent)), (far_ctx, other_core(after(far_ctx, far_qry)))),
        (both(near_qry), both(far_qry)),
        (ctx_early, other_core(after(ctx_early, near_ctx, near_qry))),
        (qry_early, other_core(after(qry_early, near_ctx, near_qry))),
    )
    return ctx_new[None], qry_new[None]


def solution(mesh):
    return jax.shard_map(
        per_device,
        mesh=mesh,
        in_specs=(
            P("section", "dp", None, None),
            P("section", "dp", None, None),
            P("section", "dp"),
            P("section", None),
            P("section", "dp", None, "tensor"),
            P("section", "tensor", "dp"),
        ),
        out_specs=(P("section", "dp", None, None), P("section", "dp", None, None)),
        check_vma=False,
    )
```

```python
import functools
import math

import jax
import jax.numpy as jnp
from jax import lax
from jax.experimental import pallas as pl
from jax.experimental.pallas import tpu as pltpu
from jax.sharding import PartitionSpec as P

HEAD = 128
RING = 4
TAIL = 16
HBM = pl.BlockSpec(memory_space=pltpu.HBM)
SMEM = pl.BlockSpec(memory_space=pltpu.SMEM)
VMEM = pl.BlockSpec(memory_space=pltpu.VMEM)
BF16 = jnp.bfloat16
F32 = jnp.float32


def around_x(array, by):
    pairs = [
        (z * RING + x, z * RING + (x + by) % RING) for z in range(2) for x in range(RING)
    ]
    return lax.ppermute(array, "dp", pairs)


def around_x_of(array, by, sections):
    pairs = []
    for s in sections:
        for z in range(2):
            for x in range(RING):
                base = s * 2 * RING + z * RING
                pairs.append((base + x, base + (x + by) % RING))
    return lax.ppermute(array, ("section", "dp"), pairs)


def across_z(array):
    return lax.ppermute(array, "dp", [(d, (d + RING) % (2 * RING)) for d in range(2 * RING)])


def other_core(array):
    return lax.ppermute(array, "tensor", [(0, 1), (1, 0)])


def relay(array, sections, count):
    return lax.ppermute(array, "section", [(s, (s + 1) % count) for s in sections])


def round_ring(array, half):
    left, right = around_x(array, 1), around_x(array, -1)
    return [array, left, around_x(left[:half], 1), around_x(right[half:], -1), right]


def after(array, *others):
    return lax.optimization_barrier((array,) + others)[0]


def copy_all(copies):
    for copy in copies:
        copy.start()
    return copies


def wait_all(copies):
    for copy in copies:
        copy.wait()


def call(kernel, outs, in_specs, out_specs, scratch=(), flops=0, moved=0, limit=16):
    return pl.pallas_call(
        kernel,
        out_shape=outs,
        in_specs=in_specs,
        out_specs=out_specs,
        scratch_shapes=list(scratch),
        compiler_params=pltpu.CompilerParams(vmem_limit_bytes=limit * 1024 * 1024),
        cost_estimate=pl.CostEstimate(flops=flops, bytes_accessed=moved, transcendentals=0),
    )


def quarter_kernel(where, weight, *pieces):
    x = where[0]
    width = pieces[0].shape[2]
    for step, piece in enumerate(pieces):
        start = pl.multiple_of(((x + step) % RING) * width, width)
        piece[...] = weight[:, :, pl.ds(start, width)]


def quarters(where, weight):
    planes, rows, columns = weight.shape
    piece = jax.ShapeDtypeStruct((planes, rows, columns // RING), BF16)
    return call(
        quarter_kernel, (piece,) * RING, [SMEM, VMEM], (VMEM,) * RING, moved=4 * weight.size
    )(where, weight)


def norm_kernel(
    where, context, queries, gain, lengths, ctx_out, qry_out, ctx_norm, qry_norm, *scratch
):
    ctx, qry, sems = scratch
    core = where[3]
    copies = copy_all(
        [
            pltpu.make_async_copy(context.at[core], ctx, sems.at[0]),
            pltpu.make_async_copy(queries.at[core], qry, sems.at[1]),
        ]
    )
    step = 32

    def rows_of(source, raw, target):
        @pl.loop(0, source.shape[0] // step)
        def _(i):
            at = pl.ds(pl.multiple_of(i * step, step), step)
            low = source[at, :]
            wide = low.astype(F32)
            mean = jnp.mean(wide * wide, axis=-1, keepdims=True)
            target[at, :] = (wide * lax.rsqrt(mean + 1e-06) * gain[...]).astype(BF16)
            raw[at, :] = low

    tail = ctx_norm.shape[0] - ctx.shape[0]
    length = lengths[core].astype(F32)
    ctx_norm[pl.ds(ctx.shape[0], tail), :] = jnp.full((tail, ctx.shape[1]), length).astype(BF16)
    copies[0].wait()
    rows_of(ctx, ctx_out, ctx_norm)
    copies[1].wait()
    rows_of(qry, qry_out, qry_norm)


def norm_scene(where, context, queries, gain, lengths):
    ctx = jax.ShapeDtypeStruct(context.shape[1:], BF16)
    qry = jax.ShapeDtypeStruct(queries.shape[1:], BF16)
    tailed = jax.ShapeDtypeStruct((ctx.shape[0] + TAIL, ctx.shape[1]), BF16)
    return call(
        norm_kernel,
        (ctx, qry, tailed, qry),
        [SMEM, HBM, HBM, VMEM, SMEM],
        (VMEM,) * 4,
        [
            pltpu.VMEM(ctx.shape, BF16),
            pltpu.VMEM(qry.shape, BF16),
            pltpu.SemaphoreType.DMA((2,)),
        ],
        moved=6 * ctx.size,
    )(where, context, queries, gain, lengths)


def row_copies(high, ctx, rows_all, sems):
    mem, width = rows_all.shape[0] // RING, rows_all.shape[1]
    half = mem // 2
    at = pl.ds(pl.multiple_of(high * width, width), width)
    starts = (0, mem, 2 * mem, 2 * mem + half, 3 * mem)
    counts = (mem, mem, half, half, mem)
    return [
        pltpu.make_async_copy(
            piece.at[pl.ds(0, count), at], rows_all.at[pl.ds(start, count)], sems.at[i]
        )
        for i, (piece, start, count) in enumerate(zip(ctx, starts, counts))
    ]


def weight_copies(x, group, weight, sems, base, plane=None):
    copies = []
    for i, piece in enumerate(group):
        step, side = i % RING, i // RING
        _, block, part = piece.shape
        first = pl.multiple_of(((x - step + RING) % RING) * block, block)
        rows, columns = pl.ds(first, block), pl.ds(side * part, part)
        if plane is None:
            source, target = piece, weight.at[:, rows, columns]
        else:
            source, target = piece.at[plane], weight.at[rows, columns]
        copies.append(pltpu.make_async_copy(source, target, sems.at[base + i]))
    return copies


def start_kernel(where, *refs):
    ctx, group = refs[:5], refs[5:13]
    total, rows_all, weight, sems = refs[13:]
    copies = row_copies(where[1], ctx, rows_all, sems)
    copies += weight_copies(where[0], group, weight, sems, 5)
    wait_all(copy_all(copies))

    @pl.when(where[2] == 1)
    def _():
        total[0] = jnp.dot(rows_all[...], weight[0], preferred_element_type=F32)

    @pl.loop(1, 3)
    def _(plane):
        total[plane] = jnp.dot(rows_all[...], weight[plane], preferred_element_type=F32)


def attend_kernel(where, *refs):
    ctx, qry, near, parts, total_in = refs[:5], refs[5:9], refs[9:17], refs[17:21], refs[21]
    outs = refs[22:26]
    rows_all, qry_all, near_query, weight, total, lengths, low, mixed, sems = refs[26:]
    group = []
    for own, others in (parts[:2], parts[2:]):
        group += [own] + [others.at[i] for i in range(RING - 1)]
    x, z, encoder = where[0], where[1], where[2]
    mem, few = rows_all.shape[0] // RING, qry_all.shape[0] // RING
    width = rows_all.shape[1]
    copies = row_copies(1 - z, ctx, rows_all, sems)
    copies += weight_copies(x, group, weight, sems, 5)
    for slot, piece in enumerate((ctx[0], ctx[1], ctx[3], ctx[4])):
        source = piece.at[pl.ds(piece.shape[0] - TAIL, TAIL), pl.ds(0, 128)]
        copies.append(pltpu.make_async_copy(source, lengths.at[slot], sems.at[13 + slot]))
    totals = [
        pltpu.make_async_copy(total_in.at[plane], total.at[plane], sems.at[17 + plane])
        for plane in range(3)
    ]
    queries = weight_copies(x, near, near_query, sems, 20, plane=0)
    for slot in range(RING):
        target = qry_all.at[pl.ds(slot * few, few)]
        queries.append(pltpu.make_async_copy(qry[slot], target, sems.at[28 + slot]))
    copy_all(copies)
    copy_all(totals[1:])

    @pl.when(encoder == 1)
    def _():
        totals[0].start()

    @pl.when(encoder == 0)
    def _():
        copy_all(queries)

    wait_all(copies)
    wait_all(totals[1:])

    @pl.when(encoder == 1)
    def _():
        totals[0].wait()
        low[0] = (
            total[0] + jnp.dot(rows_all[...], weight[0], preferred_element_type=F32)
        ).astype(BF16)

    @pl.when(encoder == 0)
    def _():
        wait_all(queries)
        here = pl.ds(pl.multiple_of(z * width, width), width)
        there = pl.ds(pl.multiple_of((1 - z) * width, width), width)
        low[0, pl.ds(0, RING * few)] = (
            jnp.dot(qry_all[:, here], near_query[...], preferred_element_type=F32)
            + jnp.dot(qry_all[:, there], weight[0], preferred_element_type=F32)
        ).astype(BF16)

    @pl.loop(1, 3)
    def _(plane):
        low[plane] = (
            total[plane] + jnp.dot(rows_all[...], weight[plane], preferred_element_type=F32)
        ).astype(BF16)

    heads = low.shape[2] // HEAD
    scale = 1.0 / math.sqrt(HEAD)

    def heads_of(count):
        column = lax.broadcasted_iota(jnp.int32, (count, mem), 1)

        @pl.loop(0, RING)
        def _(slot):
            own = pl.ds(pl.multiple_of(slot * count, count), count)
            keys = pl.ds(pl.multiple_of(slot * mem, mem), mem)
            length = lengths[slot, pl.ds(0, 1), pl.ds(0, 1)].astype(F32).astype(jnp.int32)
            valid = column < length
            for head in range(heads):
                at = pl.ds(head * HEAD, HEAD)
                scores = (
                    lax.dot_general(
                        low[0, own, at],
                        low[1, keys, at],
                        (((1,), (1,)), ((), ())),
                        preferred_element_type=F32,
                    )
                    * scale
                )
                scores = jnp.where(valid, scores, -1e30)
                expo = jnp.exp(scores - jnp.max(scores, axis=-1, keepdims=True))
                probs = (expo / jnp.sum(expo, axis=-1, keepdims=True)).astype(BF16)
                mixed[slot, pl.ds(0, count), at] = jnp.dot(
                    probs, low[2, keys, at], preferred_element_type=F32
                ).astype(BF16)

    @pl.when(encoder == 1)
    def _():
        heads_of(mem)

    @pl.when(encoder == 0)
    def _():
        heads_of(few)

    wait_all(
        copy_all(
            [
                pltpu.make_async_copy(mixed.at[slot], outs[slot], sems.at[slot])
                for slot in range(RING)
            ]
        )
    )


def start_projections(where, ctx, group):
    mem, width = ctx[0].shape
    mem -= TAIL
    planes, block, part = group[0].shape
    return call(
        start_kernel,
        jax.ShapeDtypeStruct((planes, RING * mem, 2 * part), F32),
        [SMEM] + [HBM] * 13,
        VMEM,
        [
            pltpu.VMEM((RING * mem, width // 2), BF16),
            pltpu.VMEM((planes, width // 2, 2 * part), BF16),
            pltpu.SemaphoreType.DMA((13,)),
        ],
        flops=RING * mem * width * planes * 2 * part,
        moved=RING * mem * width + planes * width * 2 * part,
        limit=24,
    )(where, *ctx, *group)


def attend(where, ctx, qry, near, parts, total):
    mem, width = ctx[0].shape
    mem -= TAIL
    few = qry[0].shape[0]
    planes, block, part = near[0].shape
    out = jax.ShapeDtypeStruct((mem, 2 * part), BF16)
    operands = (*ctx, *qry, *near, *parts, total)
    return call(
        attend_kernel,
        (out,) * RING,
        [SMEM] + [HBM] * len(operands),
        (HBM,) * RING,
        [
            pltpu.VMEM((RING * mem, width // 2), BF16),
            pltpu.VMEM((RING * few, width), BF16),
            pltpu.VMEM((width // 2, 2 * part), BF16),
            pltpu.VMEM((planes, width // 2, 2 * part), BF16),
            pltpu.VMEM(total.shape, F32),
            pltpu.VMEM((RING, TAIL, 128), BF16),
            pltpu.VMEM((planes, RING * mem, 2 * part), BF16),
            pltpu.VMEM((RING, mem, 2 * part), BF16),
            pltpu.SemaphoreType.DMA((32,)),
        ],
        flops=RING * mem * width * planes * 2 * part,
        moved=RING * mem * width + planes * width * 2 * part,
        limit=30,
    )(where, *operands)


def project_kernel(crossed, where, context, queries, *refs):
    mixed = refs[:4]
    weights = refs[4:14]
    out, few_out = refs[14:16]
    heads, weight, base, sems = refs[16:]
    x, z, encoder, core = where[0], where[1], where[2], where[3]
    part = mixed[0].shape[1] // 2
    inner, block = weights[0].shape
    half = (1 - z) if crossed else z
    first = pl.multiple_of(half * RING * block, RING * block)
    few = queries.shape[1]

    @pl.when(encoder == 1)
    def _():
        pltpu.make_async_copy(
            context.at[core, :, pl.ds(first, RING * block)], base, sems.at[0]
        ).start()

    @pl.when(encoder == 0)
    def _():
        pltpu.make_async_copy(
            queries.at[core, :, pl.ds(first, RING * block)],
            base.at[pl.ds(0, few)],
            sems.at[0],
        ).start()

    copies = []
    for step in range(RING):
        for side in range(2):
            at = pl.multiple_of(side * inner + ((x + step) % RING) * part, part)
            copies.append(
                pltpu.make_async_copy(
                    mixed[step].at[:, pl.ds(side * part, part)],
                    heads.at[:, pl.ds(at, part)],
                    sems.at[1 + step * 2 + side],
                )
            )
    pieces = []
    for i, (step, start) in enumerate(((0, 0), (1, 0), (2, 0), (2, inner // 2), (3, 0))):
        for side in range(2):
            piece = weights[side * 5 + i]
            pieces.append(
                pltpu.make_async_copy(
                    piece,
                    weight.at[step, pl.ds(side * inner + start, piece.shape[0])],
                    sems.at[9 + i * 2 + side],
                )
            )
    needed = (pieces[0:2], pieces[2:4], pieces[4:8], pieces[8:10])
    copy_all(copies)
    copy_all(pieces)

    @pl.when(encoder == 1)
    def _():
        pltpu.make_async_copy(
            context.at[core, :, pl.ds(first, RING * block)], base, sems.at[0]
        ).wait()

    @pl.when(encoder == 0)
    def _():
        pltpu.make_async_copy(
            queries.at[core, :, pl.ds(first, RING * block)],
            base.at[pl.ds(0, few)],
            sems.at[0],
        ).wait()

    wait_all(copies)
    for step in range(RING):
        wait_all(needed[step])
        at = pl.ds(pl.multiple_of(((x - step + RING) % RING) * block, block), block)
        update = jnp.dot(heads[...], weight[step], preferred_element_type=F32)
        result = (base[:, at].astype(F32) + update).astype(BF16)
        out[:, at] = result
        few_out[:, at] = result[:few]


def project(crossed, where, context, queries, mixed, weights):
    mem = context.shape[1]
    inner, block = weights[0].shape
    return call(
        functools.partial(project_kernel, crossed),
        (
            jax.ShapeDtypeStruct((mem, RING * block), BF16),
            jax.ShapeDtypeStruct((queries.shape[1], RING * block), BF16),
        ),
        [SMEM] + [HBM] * 16,
        (VMEM, VMEM),
        [
            pltpu.VMEM((mem, 2 * inner), BF16),
            pltpu.VMEM((RING, 2 * inner, block), BF16),
            pltpu.VMEM((mem, RING * block), BF16),
            pltpu.SemaphoreType.DMA((19,)),
        ],
        flops=2 * mem * 2 * inner * RING * block,
        moved=2 * (2 * inner * RING * block + 3 * mem * inner),
    )(where, context, queries, *mixed, *weights)


def gather_kernel(where, *refs):
    ctx_half, qry_half = (refs[0:2], refs[2:4]), (refs[4:6], refs[6:8])
    ctx_whole, qry_whole = refs[8:10], refs[10:12]
    ctx_out, qry_out, ctx, qry, sems = refs[12:]
    z, core, from_encoder = where[1], where[3], where[4]
    width = ctx_half[0][0].shape[1]

    def build(halves, target, wholes, other):
        copies = []
        for side in range(2):
            scene = core if side == 0 else 1 - core
            for i, half in enumerate((z, 1 - z)):
                at = pl.ds(pl.multiple_of(half * width, width), width)
                copies.append(
                    pltpu.make_async_copy(
                        halves[i][side], target.at[scene, :, at], sems.at[3 * side + i]
                    )
                )
            copies.append(
                pltpu.make_async_copy(wholes[side], other.at[scene], sems.at[3 * side + 2])
            )
        wait_all(copy_all(copies))

    @pl.when(from_encoder == 1)
    def _():
        build(ctx_half, ctx, qry_whole, qry)

    @pl.when(from_encoder == 0)
    def _():
        build(qry_half, qry, ctx_whole, ctx)

    wait_all(
        copy_all(
            [
                pltpu.make_async_copy(ctx, ctx_out, sems.at[0]),
                pltpu.make_async_copy(qry, qry_out, sems.at[1]),
            ]
        )
    )


def gather_result(where, ctx_half, qry_half, ctx_whole, qry_whole):
    ctx_shape = (2,) + ctx_whole[0].shape
    qry_shape = (2,) + qry_whole[0].shape
    return call(
        gather_kernel,
        (jax.ShapeDtypeStruct(ctx_shape, BF16), jax.ShapeDtypeStruct(qry_shape, BF16)),
        [SMEM] + [HBM] * 12,
        (HBM, HBM),
        [
            pltpu.VMEM(ctx_shape, BF16),
            pltpu.VMEM(qry_shape, BF16),
            pltpu.SemaphoreType.DMA((6,)),
        ],
        moved=8 * ctx_whole[0].size,
    )(where, *ctx_half[0], *ctx_half[1], *qry_half[0], *qry_half[1], *ctx_whole, *qry_whole)


def both(array):
    return array, other_core(array)


def per_device(context, queries, lengths, norm_gain, qkv_weight, out_weight):
    count = lax.axis_size("section")
    section = lax.axis_index("section")
    place = lax.axis_index("dp")
    core = lax.axis_index("tensor")
    encoders = list(range(count // 2))
    decoders = list(range(count // 2, count))
    before = (section + count - 1) % count
    where = jnp.stack(
        [
            place % RING,
            place // RING,
            (section < count // 2).astype(jnp.int32),
            core,
            (before < count // 2).astype(jnp.int32),
        ]
    ).astype(jnp.int32)
    context, queries = context[0], queries[0]

    own = quarters(where, jnp.swapaxes(qkv_weight[0], 0, 1))
    far_own = across_z(own[0])
    near = [own[0]] + [around_x(own[step], step) for step in range(1, RING)]
    near_other = [other_core(piece) for piece in near]

    ctx, qry, ctx_norm, qry_norm = norm_scene(
        after(where, *own), context, queries, norm_gain, lengths[0]
    )
    ctx_rows = round_ring(after(ctx_norm, far_own, *near), ctx.shape[0] // 2)
    far_others = across_z(after(jnp.stack(near[1:]), far_own))
    qry_sent = after(qry_norm, *ctx_rows[1:])
    qry_rows = [qry_norm] + [around_x_of(qry_sent, step, decoders) for step in range(1, RING)]

    shard = out_weight[0]
    out_near = round_ring(after(shard, *ctx_rows[1:]), shard.shape[0] // 2)
    total = start_projections(where, ctx_rows, near + near_other)
    far_shard = across_z(after(shard, far_others, total, *out_near))
    far = [far_own, far_others, other_core(far_own)]
    far.append(other_core(after(far_others, total, *qry_rows)))

    mixed = attend(where, ctx_rows, qry_rows, near + near_other, far, total)
    far_shard = after(far_shard, mixed[0])
    out_far = round_ring(far_shard, shard.shape[0] // 2)
    mixed = [mixed[0]] + [around_x(mixed[step], -step) for step in range(1, RING)]
    out_near += [other_core(piece) for piece in out_near]
    out_far += [other_core(piece) for piece in out_far]

    ctx_early = relay(after(ctx, far_shard), decoders, count)
    qry_early = relay(after(qry, far_shard), encoders, count)

    near_ctx, near_qry = project(
        False, after(where, qry_early), context, queries, mixed, out_near
    )
    near_ctx = relay(near_ctx, encoders, count)
    far_ctx, far_qry = project(True, where, context, queries, mixed, out_far)
    far_ctx = relay(far_ctx, encoders, count)
    near_qry = relay(after(near_qry, far_qry), decoders, count)
    far_qry = relay(far_qry, decoders, count)
    far_sent = after(far_ctx, near_qry, far_qry)
    ctx_new, qry_new = gather_result(
        where,
        (both(near_ctx), (far_ctx, other_core(far_sent))),
        (both(near_qry), both(far_qry)),
        (ctx_early, other_core(after(ctx_early, near_ctx))),
        (qry_early, other_core(after(qry_early, near_ctx))),
    )
    return ctx_new[None], qry_new[None]


def solution(mesh):
    return jax.shard_map(
        per_device,
        mesh=mesh,
        in_specs=(
            P("section", "dp", None, None),
            P("section", "dp", None, None),
            P("section", "dp"),
            P("section", None),
            P("section", "dp", None, "tensor"),
            P("section", "tensor", "dp"),
        ),
        out_specs=(P("section", "dp", None, None), P("section", "dp", None, None)),
        check_vma=False,
    )
```

```python
import functools
import math

import jax
import jax.numpy as jnp
from jax import lax
from jax.experimental import pallas as pl
from jax.experimental.pallas import tpu as pltpu
from jax.sharding import PartitionSpec as P

HEAD = 128
RING = 4
TAIL = 16
HBM = pl.BlockSpec(memory_space=pltpu.HBM)
SMEM = pl.BlockSpec(memory_space=pltpu.SMEM)
VMEM = pl.BlockSpec(memory_space=pltpu.VMEM)
BF16 = jnp.bfloat16
F32 = jnp.float32


def around_x(array, by):
    pairs = [
        (z * RING + x, z * RING + (x + by) % RING) for z in range(2) for x in range(RING)
    ]
    return lax.ppermute(array, "dp", pairs)


def around_x_of(array, by, sections):
    pairs = []
    for s in sections:
        for z in range(2):
            for x in range(RING):
                base = s * 2 * RING + z * RING
                pairs.append((base + x, base + (x + by) % RING))
    return lax.ppermute(array, ("section", "dp"), pairs)


def across_z(array):
    return lax.ppermute(array, "dp", [(d, (d + RING) % (2 * RING)) for d in range(2 * RING)])


def other_core(array):
    return lax.ppermute(array, "tensor", [(0, 1), (1, 0)])


def relay(array, sections, count):
    return lax.ppermute(array, "section", [(s, (s + 1) % count) for s in sections])


def round_ring(array, cut):
    left, right = around_x(array, 1), around_x(array, -1)
    return left, right, left[:cut], right[cut:]


def after(array, *others):
    return lax.optimization_barrier((array,) + others)[0]


def copy_all(copies):
    for copy in copies:
        copy.start()
    return copies


def wait_all(copies):
    for copy in copies:
        copy.wait()


def call(kernel, outs, in_specs, out_specs, scratch=(), flops=0, moved=0, limit=16):
    return pl.pallas_call(
        kernel,
        out_shape=outs,
        in_specs=in_specs,
        out_specs=out_specs,
        scratch_shapes=list(scratch),
        compiler_params=pltpu.CompilerParams(vmem_limit_bytes=limit * 1024 * 1024),
        cost_estimate=pl.CostEstimate(flops=flops, bytes_accessed=moved, transcendentals=0),
    )


def quarter_kernel(where, weight, *pieces):
    x = where[0]
    width = pieces[0].shape[2]
    for step, piece in enumerate(pieces):
        start = pl.multiple_of(((x + step) % RING) * width, width)
        piece[...] = weight[:, :, pl.ds(start, width)]


def quarters(where, weight):
    planes, rows, columns = weight.shape
    piece = jax.ShapeDtypeStruct((planes, rows, columns // RING), BF16)
    return call(
        quarter_kernel, (piece,) * RING, [SMEM, VMEM], (VMEM,) * RING, moved=4 * weight.size
    )(where, weight)


def norm_kernel(where, context, queries, gain, lengths, ctx_out, qry_out, normed, *scratch):
    ctx, qry, sems = scratch
    core = where[3]
    copies = copy_all(
        [
            pltpu.make_async_copy(context.at[core], ctx, sems.at[0]),
            pltpu.make_async_copy(queries.at[core], qry, sems.at[1]),
        ]
    )
    step = 32

    def rows_of(source, raw, below):
        @pl.loop(0, source.shape[0] // step)
        def _(i):
            first = pl.multiple_of(i * step, step)
            low = source[pl.ds(first, step), :]
            wide = low.astype(F32)
            mean = jnp.mean(wide * wide, axis=-1, keepdims=True)
            normed[pl.ds(below + first, step), :] = (
                wide * lax.rsqrt(mean + 1e-06) * gain[...]
            ).astype(BF16)
            raw[pl.ds(first, step), :] = low

    length = lengths[core].astype(F32)
    normed[pl.ds(normed.shape[0] - TAIL, TAIL), :] = jnp.full(
        (TAIL, normed.shape[1]), length
    ).astype(BF16)
    copies[0].wait()
    rows_of(ctx, ctx_out, 0)
    copies[1].wait()
    rows_of(qry, qry_out, ctx.shape[0])


def norm_scene(where, context, queries, gain, lengths):
    ctx = jax.ShapeDtypeStruct(context.shape[1:], BF16)
    qry = jax.ShapeDtypeStruct(queries.shape[1:], BF16)
    rows = ctx.shape[0] + qry.shape[0] + TAIL
    return call(
        norm_kernel,
        (ctx, qry, jax.ShapeDtypeStruct((rows, ctx.shape[1]), BF16)),
        [SMEM, HBM, HBM, VMEM, SMEM],
        (VMEM,) * 3,
        [
            pltpu.VMEM(ctx.shape, BF16),
            pltpu.VMEM(qry.shape, BF16),
            pltpu.SemaphoreType.DMA((2,)),
        ],
        moved=6 * ctx.size,
    )(where, context, queries, gain, lengths)


def slot_copies(rows, slot, first, count, columns, target, sems, base):
    if slot != 2:
        pieces = [(rows[slot if slot < 2 else 4], first, count, 0)]
    else:
        cut = rows[2].shape[0]
        pieces = []
        if first < cut:
            pieces.append((rows[2], first, min(count, cut - first), 0))
        if first + count > cut:
            skip = max(cut - first, 0)
            pieces.append((rows[3], first + skip - cut, count - skip, skip))
    return [
        pltpu.make_async_copy(
            piece.at[pl.ds(start, size), columns], target.at[pl.ds(at, size)], sems.at[base + i]
        )
        for i, (piece, start, size, at) in enumerate(pieces)
    ]


def row_copies(high, rows, rows_all, sems):
    mem, width = rows_all.shape[0] // RING, rows_all.shape[1]
    columns = pl.ds(pl.multiple_of(high * width, width), width)
    copies = []
    for slot in range(RING):
        target = rows_all.at[pl.ds(slot * mem, mem)]
        copies += slot_copies(rows, slot, 0, mem, columns, target, sems, len(copies))
    return copies


def weight_copies(x, group, weight, sems, base, plane=None):
    copies = []
    for i, piece in enumerate(group):
        step, side = i % RING, i // RING
        _, block, part = piece.shape
        first = pl.multiple_of(((x - step + RING) % RING) * block, block)
        rows, columns = pl.ds(first, block), pl.ds(side * part, part)
        if plane is None:
            source, target = piece, weight.at[:, rows, columns]
        else:
            source, target = piece.at[plane], weight.at[rows, columns]
        copies.append(pltpu.make_async_copy(source, target, sems.at[base + i]))
    return copies


def pieces_of(parts):
    pieces = []
    for own, sides, opposite in (parts[:3], parts[3:]):
        pieces += [own, sides.at[0], opposite, sides.at[1]]
    return pieces


def start_kernel(where, *refs):
    rows, parts = refs[:5], refs[5:11]
    total, rows_all, weight, sems = refs[11:]
    group = pieces_of(parts)
    copies = row_copies(where[1], rows, rows_all, sems)
    copies += weight_copies(where[0], group, weight, sems, 5)
    wait_all(copy_all(copies))

    @pl.when(where[2] == 1)
    def _():
        total[0] = jnp.dot(rows_all[...], weight[0], preferred_element_type=F32)

    @pl.loop(1, 3)
    def _(plane):
        total[plane] = jnp.dot(rows_all[...], weight[plane], preferred_element_type=F32)


def attend_kernel(where, *refs):
    rows, near, far, total_in = refs[:5], refs[5:11], refs[11:17], refs[17]
    outs = refs[18:22]
    rows_all, qry_all, near_query, weight, total, lengths, low, mixed, sems = refs[22:]
    x, z, encoder = where[0], where[1], where[2]
    mem, few = rows_all.shape[0] // RING, qry_all.shape[0] // RING
    width = rows_all.shape[1]
    copies = row_copies(1 - z, rows, rows_all, sems)
    copies += weight_copies(x, pieces_of(far), weight, sems, 5)
    for slot in range(RING):
        copies += slot_copies(
            rows, slot, mem + few, TAIL, pl.ds(0, 128), lengths.at[slot], sems, 13 + slot
        )
    totals = [
        pltpu.make_async_copy(total_in.at[plane], total.at[plane], sems.at[17 + plane])
        for plane in range(3)
    ]
    queries = weight_copies(x, pieces_of(near), near_query, sems, 20, plane=0)
    for slot in range(RING):
        target = qry_all.at[pl.ds(slot * few, few)]
        queries += slot_copies(
            rows, slot, mem, few, pl.ds(0, 2 * width), target, sems, 28 + slot
        )
    copy_all(copies)
    copy_all(totals[1:])

    @pl.when(encoder == 1)
    def _():
        totals[0].start()

    @pl.when(encoder == 0)
    def _():
        copy_all(queries)

    wait_all(copies)
    wait_all(totals[1:])

    @pl.when(encoder == 1)
    def _():
        totals[0].wait()
        low[0] = (
            total[0] + jnp.dot(rows_all[...], weight[0], preferred_element_type=F32)
        ).astype(BF16)

    @pl.when(encoder == 0)
    def _():
        wait_all(queries)
        here = pl.ds(pl.multiple_of(z * width, width), width)
        there = pl.ds(pl.multiple_of((1 - z) * width, width), width)
        low[0, pl.ds(0, RING * few)] = (
            jnp.dot(qry_all[:, here], near_query[...], preferred_element_type=F32)
            + jnp.dot(qry_all[:, there], weight[0], preferred_element_type=F32)
        ).astype(BF16)

    @pl.loop(1, 3)
    def _(plane):
        low[plane] = (
            total[plane] + jnp.dot(rows_all[...], weight[plane], preferred_element_type=F32)
        ).astype(BF16)

    heads = low.shape[2] // HEAD
    scale = 1.0 / math.sqrt(HEAD)

    def heads_of(count):
        column = lax.broadcasted_iota(jnp.int32, (count, mem), 1)

        @pl.loop(0, RING)
        def _(slot):
            own = pl.ds(pl.multiple_of(slot * count, count), count)
            keys = pl.ds(pl.multiple_of(slot * mem, mem), mem)
            length = lengths[slot, pl.ds(0, 1), pl.ds(0, 1)].astype(F32).astype(jnp.int32)
            valid = column < length
            for head in range(heads):
                at = pl.ds(head * HEAD, HEAD)
                scores = (
                    lax.dot_general(
                        low[0, own, at],
                        low[1, keys, at],
                        (((1,), (1,)), ((), ())),
                        preferred_element_type=F32,
                    )
                    * scale
                )
                scores = jnp.where(valid, scores, -1e30)
                expo = jnp.exp(scores - jnp.max(scores, axis=-1, keepdims=True))
                probs = (expo / jnp.sum(expo, axis=-1, keepdims=True)).astype(BF16)
                mixed[slot, pl.ds(0, count), at] = jnp.dot(
                    probs, low[2, keys, at], preferred_element_type=F32
                ).astype(BF16)

    @pl.when(encoder == 1)
    def _():
        heads_of(mem)

    @pl.when(encoder == 0)
    def _():
        heads_of(few)

    wait_all(
        copy_all(
            [
                pltpu.make_async_copy(mixed.at[slot], outs[slot], sems.at[slot])
                for slot in range(RING)
            ]
        )
    )


def start_projections(where, mem, rows, parts):
    width = rows[0].shape[1]
    planes, block, part = parts[0].shape
    return call(
        start_kernel,
        jax.ShapeDtypeStruct((planes, RING * mem, 2 * part), F32),
        [SMEM] + [HBM] * 11,
        VMEM,
        [
            pltpu.VMEM((RING * mem, width // 2), BF16),
            pltpu.VMEM((planes, width // 2, 2 * part), BF16),
            pltpu.SemaphoreType.DMA((13,)),
        ],
        flops=RING * mem * width * planes * 2 * part,
        moved=RING * mem * width + planes * width * 2 * part,
        limit=24,
    )(where, *rows, *parts)


def attend(where, mem, few, rows, near, far, total):
    width = rows[0].shape[1]
    planes, block, part = near[0].shape
    out = jax.ShapeDtypeStruct((mem, 2 * part), BF16)
    operands = (*rows, *near, *far, total)
    return call(
        attend_kernel,
        (out,) * RING,
        [SMEM] + [HBM] * len(operands),
        (HBM,) * RING,
        [
            pltpu.VMEM((RING * mem, width // 2), BF16),
            pltpu.VMEM((RING * few, width), BF16),
            pltpu.VMEM((width // 2, 2 * part), BF16),
            pltpu.VMEM((planes, width // 2, 2 * part), BF16),
            pltpu.VMEM(total.shape, F32),
            pltpu.VMEM((RING, TAIL, 128), BF16),
            pltpu.VMEM((planes, RING * mem, 2 * part), BF16),
            pltpu.VMEM((RING, mem, 2 * part), BF16),
            pltpu.SemaphoreType.DMA((32,)),
        ],
        flops=RING * mem * width * planes * 2 * part,
        moved=RING * mem * width + planes * width * 2 * part,
        limit=30,
    )(where, *operands)


def project_kernel(part, where, context, queries, *refs):
    mixed = refs[:4]
    weights = refs[4:6]
    few_in = refs[6] if part else None
    out, few_out = refs[6 + part : 8 + part]
    heads, weight, base, sems = refs[8 + part :]
    x, encoder, core = where[0], where[2], where[3]
    quarter = mixed[0].shape[1] // 2
    _, inner, block = weights[0].shape
    few = queries.shape[1]
    columns = pl.ds(part * RING * block, RING * block)
    rows_base = pltpu.make_async_copy(context.at[core, :, columns], base, sems.at[0])
    few_base = pltpu.make_async_copy(
        queries.at[core, :, columns], base.at[pl.ds(0, few)], sems.at[0]
    )
    copies = []
    for step in range(RING):
        for side in range(2):
            at = pl.multiple_of(side * inner + ((x + step) % RING) * quarter, quarter)
            copies.append(
                pltpu.make_async_copy(
                    mixed[step].at[:, pl.ds(side * quarter, quarter)],
                    heads.at[:, pl.ds(at, quarter)],
                    sems.at[1 + step * 2 + side],
                )
            )
    pieces = []
    for i in range(RING):
        for side in range(2):
            pieces.append(
                pltpu.make_async_copy(
                    weights[side].at[part * RING + i],
                    weight.at[i, pl.ds(side * inner, inner)],
                    sems.at[9 + i * 2 + side],
                )
            )

    @pl.when(encoder == 1)
    def _():
        rows_base.start()

    @pl.when(encoder == 0)
    def _():
        few_base.start()

    copy_all(copies)
    copy_all(pieces)

    @pl.when(encoder == 1)
    def _():
        rows_base.wait()

    @pl.when(encoder == 0)
    def _():
        few_base.wait()

    if part:
        few_out[:, pl.ds(0, RING * block)] = few_in[...]
    wait_all(copies)
    for i in range(RING):
        wait_all(pieces[2 * i : 2 * i + 2])
        at = pl.ds(i * block, block)
        update = jnp.dot(heads[...], weight[i], preferred_element_type=F32)
        result = (base[:, at].astype(F32) + update).astype(BF16)
        out[:, at] = result
        few_out[:, pl.ds((part * RING + i) * block, block)] = result[:few]


def project(part, where, context, queries, mixed, weights, few_in=()):
    mem, few = context.shape[1], queries.shape[1]
    _, inner, block = weights[0].shape
    return call(
        functools.partial(project_kernel, part),
        (
            jax.ShapeDtypeStruct((mem, RING * block), BF16),
            jax.ShapeDtypeStruct((few, (1 + part) * RING * block), BF16),
        ),
        [SMEM] + [HBM] * 8 + [VMEM] * part,
        (VMEM, VMEM),
        [
            pltpu.VMEM((mem, 2 * inner), BF16),
            pltpu.VMEM((RING, 2 * inner, block), BF16),
            pltpu.VMEM((mem, RING * block), BF16),
            pltpu.SemaphoreType.DMA((17,)),
        ],
        flops=2 * mem * 2 * inner * RING * block,
        moved=2 * (2 * inner * RING * block + 3 * mem * inner),
    )(where, context, queries, *mixed, *weights, *few_in)


def gather_kernel(where, *refs):
    halves = (refs[0:2], refs[2:4])
    ctx_early, qry_early, qry_late = refs[4:6], refs[6:8], refs[8:10]
    ctx_out, qry_out, ctx, qry, sems = refs[10:]
    core, from_encoder = where[3], where[4]
    width = halves[0][0].shape[1]

    def build(rows, few):
        copies = []
        for side in range(2):
            scene = core if side == 0 else 1 - core
            for piece, at in rows[side]:
                target = ctx.at[scene, :, at]
                copies.append(pltpu.make_async_copy(piece, target, sems.at[len(copies)]))
            copies.append(
                pltpu.make_async_copy(few[side], qry.at[scene], sems.at[len(copies)])
            )
        wait_all(copy_all(copies))

    @pl.when(from_encoder == 1)
    def _():
        build(
            [[(halves[i][side], pl.ds(i * width, width)) for i in range(2)] for side in range(2)],
            qry_early,
        )

    @pl.when(from_encoder == 0)
    def _():
        build([[(ctx_early[side], pl.ds(0, 2 * width))] for side in range(2)], qry_late)

    wait_all(
        copy_all(
            [
                pltpu.make_async_copy(ctx, ctx_out, sems.at[0]),
                pltpu.make_async_copy(qry, qry_out, sems.at[1]),
            ]
        )
    )


def gather_result(where, first, second, ctx_early, qry_early, qry_late):
    ctx_shape = (2,) + ctx_early[0].shape
    qry_shape = (2,) + qry_early[0].shape
    return call(
        gather_kernel,
        (jax.ShapeDtypeStruct(ctx_shape, BF16), jax.ShapeDtypeStruct(qry_shape, BF16)),
        [SMEM] + [HBM] * 10,
        (HBM, HBM),
        [
            pltpu.VMEM(ctx_shape, BF16),
            pltpu.VMEM(qry_shape, BF16),
            pltpu.SemaphoreType.DMA((6,)),
        ],
        moved=8 * ctx_early[0].size,
    )(where, *first, *second, *ctx_early, *qry_early, *qry_late)


def both(array):
    return array, other_core(array)


def per_device(context, queries, lengths, norm_gain, qkv_weight, out_weight):
    count = lax.axis_size("section")
    section = lax.axis_index("section")
    place = lax.axis_index("dp")
    core = lax.axis_index("tensor")
    encoders = list(range(count // 2))
    decoders = list(range(count // 2, count))
    before = (section + count - 1) % count
    where = jnp.stack(
        [
            place % RING,
            place // RING,
            (section < count // 2).astype(jnp.int32),
            core,
            (before < count // 2).astype(jnp.int32),
        ]
    ).astype(jnp.int32)
    context, queries = context[0], queries[0]

    mem, few = context.shape[1], queries.shape[1]
    out_all = lax.all_gather(out_weight[0], "dp")

    own = quarters(where, jnp.swapaxes(qkv_weight[0], 0, 1))
    own_other = other_core(own[0])
    far_own = across_z(own[0])
    left, opposite, right = [around_x(own[step], step) for step in range(1, RING)]
    sides = jnp.stack([left, right])

    ctx, qry, normed = norm_scene(
        after(where, *own), context, queries, norm_gain, lengths[0]
    )
    cut = (normed.shape[0] // 32 + 1) * 16
    from_left, from_right, send_left, send_right = round_ring(
        after(normed, far_own, sides, opposite, own_other), cut
    )
    far_sides = across_z(after(sides, far_own))
    far_opposite = across_z(after(opposite, from_left, from_right))
    rows = (
        normed,
        from_left,
        around_x(after(send_left, far_sides), 1),
        around_x(after(send_right, far_sides), -1),
        from_right,
    )
    near = (own[0], sides, opposite, own_other, other_core(sides), other_core(opposite))
    total = start_projections(where, mem, rows, near)
    far = (far_own, far_sides, far_opposite)
    far += (
        other_core(after(far_own, far_sides)),
        other_core(far_sides),
        other_core(after(far_opposite, total)),
    )
    ctx_early = relay(after(ctx, far_opposite), decoders, count)
    qry_early = relay(after(qry, far_opposite), encoders, count)

    mixed = attend(where, mem, few, rows, near, far, total)
    weights = both(after(out_all, mixed[0]))
    mixed = [mixed[0]] + [around_x(mixed[step], -step) for step in range(1, RING)]

    first, few_first = project(0, where, context, queries, mixed, weights)
    first = relay(first, encoders, count)
    second, few_new = project(1, where, context, queries, mixed, weights, (few_first,))
    second = relay(second, encoders, count)
    few_new = relay(few_new, decoders, count)
    ctx_new, qry_new = gather_result(
        where,
        both(first),
        (second, other_core(after(second, few_new))),
        (ctx_early, other_core(after(ctx_early, first))),
        (qry_early, other_core(after(qry_early, first))),
        both(few_new),
    )
    return ctx_new[None], qry_new[None]


def solution(mesh):
    return jax.shard_map(
        per_device,
        mesh=mesh,
        in_specs=(
            P("section", "dp", None, None),
            P("section", "dp", None, None),
            P("section", "dp"),
            P("section", None),
            P("section", "dp", None, "tensor"),
            P("section", "tensor", "dp"),
        ),
        out_specs=(P("section", "dp", None, None), P("section", "dp", None, None)),
        check_vma=False,
    )
```

```python
import functools
import math

import jax
import jax.numpy as jnp
from jax import lax
from jax.experimental import pallas as pl
from jax.experimental.pallas import tpu as pltpu
from jax.sharding import PartitionSpec as P

HEAD = 128
RING = 4
TAIL = 16
HBM = pl.BlockSpec(memory_space=pltpu.HBM)
SMEM = pl.BlockSpec(memory_space=pltpu.SMEM)
VMEM = pl.BlockSpec(memory_space=pltpu.VMEM)
BF16 = jnp.bfloat16
F32 = jnp.float32


def around_x(array, by):
    pairs = [
        (z * RING + x, z * RING + (x + by) % RING) for z in range(2) for x in range(RING)
    ]
    return lax.ppermute(array, "dp", pairs)


def around_x_of(array, by, sections):
    pairs = []
    for s in sections:
        for z in range(2):
            for x in range(RING):
                base = s * 2 * RING + z * RING
                pairs.append((base + x, base + (x + by) % RING))
    return lax.ppermute(array, ("section", "dp"), pairs)


def across_z(array):
    return lax.ppermute(array, "dp", [(d, (d + RING) % (2 * RING)) for d in range(2 * RING)])


def other_core(array):
    return lax.ppermute(array, "tensor", [(0, 1), (1, 0)])


def relay(array, sections, count):
    return lax.ppermute(array, "section", [(s, (s + 1) % count) for s in sections])


def round_ring(array):
    return around_x(array, 1), around_x(array, -1)


def after(array, *others):
    return lax.optimization_barrier((array,) + others)[0]


def copy_all(copies):
    for copy in copies:
        copy.start()
    return copies


def wait_all(copies):
    for copy in copies:
        copy.wait()


def call(kernel, outs, in_specs, out_specs, scratch=(), flops=0, moved=0, limit=16):
    return pl.pallas_call(
        kernel,
        out_shape=outs,
        in_specs=in_specs,
        out_specs=out_specs,
        scratch_shapes=list(scratch),
        compiler_params=pltpu.CompilerParams(vmem_limit_bytes=limit * 1024 * 1024),
        cost_estimate=pl.CostEstimate(flops=1, bytes_accessed=1, transcendentals=0),
    )


def quarter_kernel(where, weight, *pieces):
    x = where[0]
    width = pieces[0].shape[2]
    for step, piece in enumerate(pieces):
        start = pl.multiple_of(((x + step) % RING) * width, width)
        piece[...] = weight[:, :, pl.ds(start, width)]


def quarters(where, weight):
    planes, rows, columns = weight.shape
    piece = jax.ShapeDtypeStruct((planes, rows, columns // RING), BF16)
    return call(
        quarter_kernel, (piece,) * RING, [SMEM, VMEM], (VMEM,) * RING, moved=4 * weight.size
    )(where, weight)


def norm_kernel(where, context, queries, gain, lengths, ctx_out, qry_out, normed, *scratch):
    ctx, qry, sems = scratch
    core = where[3]
    copies = copy_all(
        [
            pltpu.make_async_copy(context.at[core], ctx, sems.at[0]),
            pltpu.make_async_copy(queries.at[core], qry, sems.at[1]),
        ]
    )
    step = 32

    def rows_of(source, raw, below):
        @pl.loop(0, source.shape[0] // step)
        def _(i):
            first = pl.multiple_of(i * step, step)
            low = source[pl.ds(first, step), :]
            wide = low.astype(F32)
            mean = jnp.mean(wide * wide, axis=-1, keepdims=True)
            normed[pl.ds(below + first, step), :] = (
                wide * lax.rsqrt(mean + 1e-06) * gain[...]
            ).astype(BF16)
            raw[pl.ds(first, step), :] = low

    length = lengths[core].astype(F32)
    normed[pl.ds(normed.shape[0] - TAIL, TAIL), :] = jnp.full(
        (TAIL, normed.shape[1]), length
    ).astype(BF16)
    copies[0].wait()
    rows_of(ctx, ctx_out, 0)
    copies[1].wait()
    rows_of(qry, qry_out, ctx.shape[0])


def norm_scene(where, context, queries, gain, lengths):
    ctx = jax.ShapeDtypeStruct(context.shape[1:], BF16)
    qry = jax.ShapeDtypeStruct(queries.shape[1:], BF16)
    rows = ctx.shape[0] + qry.shape[0] + TAIL
    return call(
        norm_kernel,
        (ctx, qry, jax.ShapeDtypeStruct((rows, ctx.shape[1]), BF16)),
        [SMEM, HBM, HBM, VMEM, SMEM],
        (VMEM,) * 3,
        [
            pltpu.VMEM(ctx.shape, BF16),
            pltpu.VMEM(qry.shape, BF16),
            pltpu.SemaphoreType.DMA((2,)),
        ],
        moved=6 * ctx.size,
    )(where, context, queries, gain, lengths)


def slot_copies(rows, slot, first, count, columns, target, sems, base):
    if slot != 2:
        pieces = [(rows[slot if slot < 2 else 4], first, count, 0)]
    else:
        cut = rows[2].shape[0]
        pieces = []
        if first < cut:
            pieces.append((rows[2], first, min(count, cut - first), 0))
        if first + count > cut:
            skip = max(cut - first, 0)
            pieces.append((rows[3], first + skip - cut, count - skip, skip))
    return [
        pltpu.make_async_copy(
            piece.at[pl.ds(start, size), columns], target.at[pl.ds(at, size)], sems.at[base + i]
        )
        for i, (piece, start, size, at) in enumerate(pieces)
    ]


def row_copies(high, rows, rows_all, sems):
    mem, width = rows_all.shape[0] // RING, rows_all.shape[1]
    columns = pl.ds(pl.multiple_of(high * width, width), width)
    copies = []
    for slot in range(RING):
        target = rows_all.at[pl.ds(slot * mem, mem)]
        copies += slot_copies(rows, slot, 0, mem, columns, target, sems, len(copies))
    return copies


def weight_copies(x, group, weight, sems, base, plane=None):
    copies = []
    for i, piece in enumerate(group):
        step, side = i % RING, i // RING
        _, block, part = piece.shape
        first = pl.multiple_of(((x - step + RING) % RING) * block, block)
        rows, columns = pl.ds(first, block), pl.ds(side * part, part)
        if plane is None:
            source, target = piece, weight.at[:, rows, columns]
        else:
            source, target = piece.at[plane], weight.at[rows, columns]
        copies.append(pltpu.make_async_copy(source, target, sems.at[base + i]))
    return copies


def pieces_of(parts):
    return [part.at[step] for part in parts for step in range(part.shape[0])]


def start_kernel(where, *refs):
    rows, parts = refs[:5], refs[5:7]
    total, rows_all, weight, sems = refs[7:]
    group = pieces_of(parts)
    copies = row_copies(where[1], rows, rows_all, sems)
    copies += weight_copies(where[0], group, weight, sems, 5)
    wait_all(copy_all(copies))

    @pl.when(where[2] == 1)
    def _():
        total[0] = jnp.dot(rows_all[...], weight[0], preferred_element_type=F32)

    @pl.loop(1, 3)
    def _(plane):
        total[plane] = jnp.dot(rows_all[...], weight[plane], preferred_element_type=F32)


def attend_kernel(where, *refs):
    rows, near, far, total_in = refs[:5], refs[5:7], refs[7:10], refs[10]
    outs = refs[11:15]
    rows_all, qry_all, near_query, weight, total, lengths, low, mixed, sems = refs[15:]
    x, z, encoder = where[0], where[1], where[2]
    mem, few = rows_all.shape[0] // RING, qry_all.shape[0] // RING
    width = rows_all.shape[1]
    copies = row_copies(1 - z, rows, rows_all, sems)
    copies += weight_copies(x, pieces_of(far), weight, sems, 5)
    for slot in range(RING):
        copies += slot_copies(
            rows, slot, mem + few, TAIL, pl.ds(0, 128), lengths.at[slot], sems, 13 + slot
        )
    totals = [
        pltpu.make_async_copy(total_in.at[plane], total.at[plane], sems.at[17 + plane])
        for plane in range(3)
    ]
    queries = weight_copies(x, pieces_of(near), near_query, sems, 20, plane=0)
    for slot in range(RING):
        target = qry_all.at[pl.ds(slot * few, few)]
        queries += slot_copies(
            rows, slot, mem, few, pl.ds(0, 2 * width), target, sems, 28 + slot
        )
    copy_all(copies)
    copy_all(totals[1:])

    @pl.when(encoder == 1)
    def _():
        totals[0].start()

    @pl.when(encoder == 0)
    def _():
        copy_all(queries)

    wait_all(copies)
    wait_all(totals[1:])

    @pl.when(encoder == 1)
    def _():
        totals[0].wait()
        low[0] = (
            total[0] + jnp.dot(rows_all[...], weight[0], preferred_element_type=F32)
        ).astype(BF16)

    @pl.when(encoder == 0)
    def _():
        wait_all(queries)
        here = pl.ds(pl.multiple_of(z * width, width), width)
        there = pl.ds(pl.multiple_of((1 - z) * width, width), width)
        low[0, pl.ds(0, RING * few)] = (
            jnp.dot(qry_all[:, here], near_query[...], preferred_element_type=F32)
            + jnp.dot(qry_all[:, there], weight[0], preferred_element_type=F32)
        ).astype(BF16)

    @pl.loop(1, 3)
    def _(plane):
        low[plane] = (
            total[plane] + jnp.dot(rows_all[...], weight[plane], preferred_element_type=F32)
        ).astype(BF16)

    heads = low.shape[2] // HEAD
    scale = 1.0 / math.sqrt(HEAD)

    def heads_of(count):
        column = lax.broadcasted_iota(jnp.int32, (count, mem), 1)

        @pl.loop(0, RING)
        def _(slot):
            own = pl.ds(pl.multiple_of(slot * count, count), count)
            keys = pl.ds(pl.multiple_of(slot * mem, mem), mem)
            length = lengths[slot, pl.ds(0, 1), pl.ds(0, 1)].astype(F32).astype(jnp.int32)
            valid = column < length
            for head in range(heads):
                at = pl.ds(head * HEAD, HEAD)
                scores = (
                    lax.dot_general(
                        low[0, own, at],
                        low[1, keys, at],
                        (((1,), (1,)), ((), ())),
                        preferred_element_type=F32,
                    )
                    * scale
                )
                scores = jnp.where(valid, scores, -1e30)
                expo = jnp.exp(scores - jnp.max(scores, axis=-1, keepdims=True))
                probs = (expo / jnp.sum(expo, axis=-1, keepdims=True)).astype(BF16)
                mixed[slot, pl.ds(0, count), at] = jnp.dot(
                    probs, low[2, keys, at], preferred_element_type=F32
                ).astype(BF16)

    @pl.when(encoder == 1)
    def _():
        heads_of(mem)

    @pl.when(encoder == 0)
    def _():
        heads_of(few)

    wait_all(
        copy_all(
            [
                pltpu.make_async_copy(mixed.at[slot], outs[slot], sems.at[slot])
                for slot in range(RING)
            ]
        )
    )


def start_projections(where, mem, rows, parts):
    width = rows[0].shape[1]
    _, planes, block, part = parts[0].shape
    return call(
        start_kernel,
        jax.ShapeDtypeStruct((planes, RING * mem, 2 * part), F32),
        [SMEM] + [HBM] * 7,
        VMEM,
        [
            pltpu.VMEM((RING * mem, width // 2), BF16),
            pltpu.VMEM((planes, width // 2, 2 * part), BF16),
            pltpu.SemaphoreType.DMA((13,)),
        ],
        flops=RING * mem * width * planes * 2 * part,
        moved=RING * mem * width + planes * width * 2 * part,
        limit=24,
    )(where, *rows, *parts)


def attend(where, mem, few, rows, near, far, total):
    width = rows[0].shape[1]
    _, planes, block, part = near[0].shape
    out = jax.ShapeDtypeStruct((mem, 2 * part), BF16)
    operands = (*rows, *near, *far, total)
    return call(
        attend_kernel,
        (out,) * RING,
        [SMEM] + [HBM] * len(operands),
        (HBM,) * RING,
        [
            pltpu.VMEM((RING * mem, width // 2), BF16),
            pltpu.VMEM((RING * few, width), BF16),
            pltpu.VMEM((width // 2, 2 * part), BF16),
            pltpu.VMEM((planes, width // 2, 2 * part), BF16),
            pltpu.VMEM(total.shape, F32),
            pltpu.VMEM((RING, TAIL, 128), BF16),
            pltpu.VMEM((planes, RING * mem, 2 * part), BF16),
            pltpu.VMEM((RING, mem, 2 * part), BF16),
            pltpu.SemaphoreType.DMA((32,)),
        ],
        flops=RING * mem * width * planes * 2 * part,
        moved=RING * mem * width + planes * width * 2 * part,
        limit=30,
    )(where, *operands)


def project_kernel(part, where, context, queries, *refs):
    mixed = refs[:4]
    weights = refs[4:6]
    few_in = refs[6] if part else None
    out, few_out = refs[6 + part : 8 + part]
    heads, weight, base, sems = refs[8 + part :]
    x, z, encoder, core = where[0], where[1], where[2], where[3]
    quarter = mixed[0].shape[1] // 2
    inner = quarter * RING
    block = weights[0].shape[1]
    few = queries.shape[1]
    columns = pl.ds(part * RING * block, RING * block)
    rows_base = pltpu.make_async_copy(context.at[core, :, columns], base, sems.at[0])
    few_base = pltpu.make_async_copy(
        queries.at[core, :, columns], base.at[pl.ds(0, few)], sems.at[0]
    )
    copies = []
    for step in range(RING):
        for side in range(2):
            at = pl.multiple_of(side * inner + ((x + step) % RING) * quarter, quarter)
            copies.append(
                pltpu.make_async_copy(
                    mixed[step].at[:, pl.ds(side * quarter, quarter)],
                    heads.at[:, pl.ds(at, quarter)],
                    sems.at[1 + step * 2 + side],
                )
            )
    pieces = []
    crossed = z if part == 0 else 1 - z
    for i in range(RING):
        for side in range(2):
            start = pl.multiple_of((2 * i + crossed) * inner, inner)
            pieces.append(
                pltpu.make_async_copy(
                    weights[side].at[pl.ds(start, inner)],
                    weight.at[i, pl.ds(side * inner, inner)],
                    sems.at[9 + i * 2 + side],
                )
            )

    @pl.when(encoder == 1)
    def _():
        rows_base.start()

    @pl.when(encoder == 0)
    def _():
        few_base.start()

    copy_all(copies)
    copy_all(pieces)

    @pl.when(encoder == 1)
    def _():
        rows_base.wait()

    @pl.when(encoder == 0)
    def _():
        few_base.wait()

    if part:
        few_out[:, pl.ds(0, RING * block)] = few_in[...]
    wait_all(copies)
    for i in range(RING):
        wait_all(pieces[2 * i : 2 * i + 2])
        place = (x - i + RING) % RING
        at = pl.ds(pl.multiple_of(place * block, block), block)
        update = jnp.dot(heads[...], weight[i], preferred_element_type=F32)
        result = (base[:, at].astype(F32) + update).astype(BF16)
        out[:, at] = result
        at = pl.ds(pl.multiple_of((part * RING + place) * block, block), block)
        few_out[:, at] = result[:few]


def project(part, where, context, queries, mixed, weights, few_in=()):
    mem, few = context.shape[1], queries.shape[1]
    inner, block = mixed[0].shape[1] // 2 * RING, weights[0].shape[1]
    return call(
        functools.partial(project_kernel, part),
        (
            jax.ShapeDtypeStruct((mem, RING * block), BF16),
            jax.ShapeDtypeStruct((few, (1 + part) * RING * block), BF16),
        ),
        [SMEM] + [HBM] * 8 + [VMEM] * part,
        (VMEM, VMEM),
        [
            pltpu.VMEM((mem, 2 * inner), BF16),
            pltpu.VMEM((RING, 2 * inner, block), BF16),
            pltpu.VMEM((mem, RING * block), BF16),
            pltpu.SemaphoreType.DMA((17,)),
        ],
        flops=2 * mem * 2 * inner * RING * block,
        moved=2 * (2 * inner * RING * block + 3 * mem * inner),
    )(where, context, queries, *mixed, *weights, *few_in)


def gather_kernel(where, *refs):
    halves = (refs[0:2], refs[2:4])
    ctx_early, qry_early, qry_late = refs[4:6], refs[6:8], refs[8:10]
    ctx_out, qry_out, ctx, qry, sems = refs[10:]
    core, from_encoder = where[3], where[4]
    width = halves[0][0].shape[1]

    def build(rows, few):
        copies = []
        for side in range(2):
            scene = core if side == 0 else 1 - core
            for piece, at in rows[side]:
                target = ctx.at[scene, :, at]
                copies.append(pltpu.make_async_copy(piece, target, sems.at[len(copies)]))
            copies.append(
                pltpu.make_async_copy(few[side], qry.at[scene], sems.at[len(copies)])
            )
        wait_all(copy_all(copies))

    @pl.when(from_encoder == 1)
    def _():
        build(
            [[(halves[i][side], pl.ds(i * width, width)) for i in range(2)] for side in range(2)],
            qry_early,
        )

    @pl.when(from_encoder == 0)
    def _():
        build([[(ctx_early[side], pl.ds(0, 2 * width))] for side in range(2)], qry_late)

    wait_all(
        copy_all(
            [
                pltpu.make_async_copy(ctx, ctx_out, sems.at[0]),
                pltpu.make_async_copy(qry, qry_out, sems.at[1]),
            ]
        )
    )


def gather_result(where, first, second, ctx_early, qry_early, qry_late):
    ctx_shape = (2,) + ctx_early[0].shape
    qry_shape = (2,) + qry_early[0].shape
    return call(
        gather_kernel,
        (jax.ShapeDtypeStruct(ctx_shape, BF16), jax.ShapeDtypeStruct(qry_shape, BF16)),
        [SMEM] + [HBM] * 10,
        (HBM, HBM),
        [
            pltpu.VMEM(ctx_shape, BF16),
            pltpu.VMEM(qry_shape, BF16),
            pltpu.SemaphoreType.DMA((6,)),
        ],
        moved=8 * ctx_early[0].size,
    )(where, *first, *second, *ctx_early, *qry_early, *qry_late)


def both(array):
    return array, other_core(array)


def per_device(context, queries, lengths, norm_gain, qkv_weight, out_weight):
    count = lax.axis_size("section")
    section = lax.axis_index("section")
    place = lax.axis_index("dp")
    core = lax.axis_index("tensor")
    encoders = list(range(count // 2))
    decoders = list(range(count // 2, count))
    before = (section + count - 1) % count
    where = jnp.stack(
        [
            place % RING,
            place // RING,
            (section < count // 2).astype(jnp.int32),
            core,
            (before < count // 2).astype(jnp.int32),
        ]
    ).astype(jnp.int32)
    context, queries = context[0], queries[0]

    mem, few = context.shape[1], queries.shape[1]
    out_shard = out_weight[0]
    out_far = across_z(out_shard)
    own = quarters(where, jnp.swapaxes(qkv_weight[0], 0, 1))
    near = jnp.stack([own[0]] + [around_x(own[step], step) for step in range(1, RING)])
    far = across_z(after(near, out_far))
    near = (near, other_core(near))

    ctx, qry, normed = norm_scene(
        after(where, *own), context, queries, norm_gain, lengths[0]
    )
    cut = (normed.shape[0] // 32 + 1) * 16
    left, right = round_ring(after(normed, near[0], out_far))
    rows = (normed, left, around_x(left[:cut], 1), around_x(right[cut:], -1), right)
    total = start_projections(where, mem, rows, near)

    out_pair = after(jnp.concatenate([out_shard, out_far]), *rows, total)
    cut = out_shard.shape[0]
    left, right = round_ring(out_pair)
    opposite = [around_x(left[:cut], 1), around_x(right[cut:], -1)]
    far = (far, other_core(after(far[:2], total)), other_core(after(far[2:], total)))
    ctx_early = relay(after(ctx, *far), decoders, count)
    qry_early = relay(after(qry, *far), encoders, count)

    mixed = attend(after(where, left, right), mem, few, rows, near, far, total)
    weights = both(jnp.concatenate([out_pair, left, *after(tuple(opposite), mixed[0]), right]))
    mixed = [mixed[0]] + [around_x(mixed[step], -step) for step in range(1, RING)]

    first, few_first = project(0, where, context, queries, mixed, weights)
    first = relay(first, encoders, count)
    second, few_new = project(1, where, context, queries, mixed, weights, (few_first,))
    second = relay(second, encoders, count)
    few_new = relay(few_new, decoders, count)
    ctx_new, qry_new = gather_result(
        where,
        both(first),
        (second, other_core(after(second, few_new))),
        (ctx_early, other_core(after(ctx_early, first))),
        (qry_early, other_core(after(qry_early, first))),
        both(few_new),
    )
    return ctx_new[None], qry_new[None]


def solution(mesh):
    return jax.shard_map(
        per_device,
        mesh=mesh,
        in_specs=(
            P("section", "dp", None, None),
            P("section", "dp", None, None),
            P("section", "dp"),
            P("section", None),
            P("section", "dp", None, "tensor"),
            P("section", "tensor", "dp"),
        ),
        out_specs=(P("section", "dp", None, None), P("section", "dp", None, None)),
        check_vma=False,
    )
```

```python
import functools
import math

import jax
import jax.numpy as jnp
from jax import lax
from jax.experimental import pallas as pl
from jax.experimental.pallas import tpu as pltpu
from jax.sharding import PartitionSpec as P

HEAD = 128
RING = 4
TAIL = 16
HBM = pl.BlockSpec(memory_space=pltpu.HBM)
SMEM = pl.BlockSpec(memory_space=pltpu.SMEM)
VMEM = pl.BlockSpec(memory_space=pltpu.VMEM)
BF16 = jnp.bfloat16
F32 = jnp.float32


def around_x(array, by):
    pairs = [
        (z * RING + x, z * RING + (x + by) % RING) for z in range(2) for x in range(RING)
    ]
    return lax.ppermute(array, "dp", pairs)


def around_x_of(array, by, sections):
    pairs = []
    for s in sections:
        for z in range(2):
            for x in range(RING):
                base = s * 2 * RING + z * RING
                pairs.append((base + x, base + (x + by) % RING))
    return lax.ppermute(array, ("section", "dp"), pairs)


def across_z(array):
    return lax.ppermute(array, "dp", [(d, (d + RING) % (2 * RING)) for d in range(2 * RING)])


def other_core(array):
    return lax.ppermute(array, "tensor", [(0, 1), (1, 0)])


def relay(array, sections, count):
    return lax.ppermute(array, "section", [(s, (s + 1) % count) for s in sections])


def round_ring(array):
    return (array,) + tuple(around_x(array, step) for step in range(1, RING))


def after(array, *others):
    return lax.optimization_barrier((array,) + others)[0]


def copy_all(copies):
    for copy in copies:
        copy.start()
    return copies


def wait_all(copies):
    for copy in copies:
        copy.wait()


def call(kernel, outs, in_specs, out_specs, scratch=(), flops=0, moved=0, limit=16):
    return pl.pallas_call(
        kernel,
        out_shape=outs,
        in_specs=in_specs,
        out_specs=out_specs,
        scratch_shapes=list(scratch),
        compiler_params=pltpu.CompilerParams(vmem_limit_bytes=limit * 1024 * 1024),
        cost_estimate=pl.CostEstimate(flops=1, bytes_accessed=1, transcendentals=0),
    )


def quarter_kernel(where, weight, *pieces):
    x = where[0]
    width = pieces[0].shape[2]
    for step, piece in enumerate(pieces):
        start = pl.multiple_of(((x + step) % RING) * width, width)
        piece[...] = weight[:, :, pl.ds(start, width)]


def quarters(where, weight):
    planes, rows, columns = weight.shape
    piece = jax.ShapeDtypeStruct((planes, rows, columns // RING), BF16)
    return call(
        quarter_kernel, (piece,) * RING, [SMEM, VMEM], (VMEM,) * RING, moved=4 * weight.size
    )(where, weight)


def norm_kernel(where, context, queries, gain, lengths, ctx_out, qry_out, normed, *scratch):
    ctx, qry, sems = scratch
    core = where[3]
    copies = copy_all(
        [
            pltpu.make_async_copy(context.at[core], ctx, sems.at[0]),
            pltpu.make_async_copy(queries.at[core], qry, sems.at[1]),
        ]
    )
    step = 32

    def rows_of(source, raw, below):
        @pl.loop(0, source.shape[0] // step)
        def _(i):
            first = pl.multiple_of(i * step, step)
            low = source[pl.ds(first, step), :]
            wide = low.astype(F32)
            mean = jnp.mean(wide * wide, axis=-1, keepdims=True)
            normed[pl.ds(below + first, step), :] = (
                wide * lax.rsqrt(mean + 1e-06) * gain[...]
            ).astype(BF16)
            raw[pl.ds(first, step), :] = low

    length = lengths[core].astype(F32)
    normed[pl.ds(normed.shape[0] - TAIL, TAIL), :] = jnp.full(
        (TAIL, normed.shape[1]), length
    ).astype(BF16)
    copies[0].wait()
    rows_of(ctx, ctx_out, 0)
    copies[1].wait()
    rows_of(qry, qry_out, ctx.shape[0])


def norm_scene(where, context, queries, gain, lengths):
    ctx = jax.ShapeDtypeStruct(context.shape[1:], BF16)
    qry = jax.ShapeDtypeStruct(queries.shape[1:], BF16)
    rows = ctx.shape[0] + qry.shape[0] + TAIL
    return call(
        norm_kernel,
        (ctx, qry, jax.ShapeDtypeStruct((rows, ctx.shape[1]), BF16)),
        [SMEM, HBM, HBM, VMEM, SMEM],
        (VMEM,) * 3,
        [
            pltpu.VMEM(ctx.shape, BF16),
            pltpu.VMEM(qry.shape, BF16),
            pltpu.SemaphoreType.DMA((2,)),
        ],
        moved=6 * ctx.size,
    )(where, context, queries, gain, lengths)


def start_kernel(where, *refs):
    rows, parts = refs[:4], refs[4:6]
    total, far_rows, far_qry, lengths, near_rows, near_qry, weight, sems = refs[6:]
    x, z = where[0], where[1]
    mem, few = far_rows.shape[0] // RING, far_qry.shape[0] // RING
    width = far_rows.shape[1]
    copies = []

    def take(slot, first, count, columns, target):
        source = rows[slot].at[pl.ds(first, count), columns]
        copies.append(pltpu.make_async_copy(source, target, sems.at[len(copies)]))

    for part, first in ((parts[0], 0), (parts[1], parts[0].shape[3])):
        for step in range(RING):
            _, _, block, columns = part.shape
            at = pl.multiple_of(((x - step + RING) % RING) * block, block)
            target = weight.at[:, pl.ds(at, block), pl.ds(first, columns)]
            copies.append(
                pltpu.make_async_copy(part.at[step], target, sems.at[len(copies)])
            )
    for slot in range(RING):
        columns = pl.ds(pl.multiple_of(z * width, width), width)
        take(slot, 0, mem, columns, near_rows.at[pl.ds(slot * mem, mem)])
        take(slot, mem, few, columns, near_qry.at[pl.ds(slot * few, few)])
        take(slot, mem + few, TAIL, pl.ds(0, 128), lengths.at[slot])
    for step in range(RING):
        at = ((1 - z) * RING + (x - step + RING) % RING) * block
        columns = pl.ds(pl.multiple_of(at, block), block)
        here = pl.ds(step * block, block)
        for slot in range(RING):
            take(slot, 0, mem, columns, far_rows.at[pl.ds(slot * mem, mem), here])
            take(slot, mem, few, columns, far_qry.at[pl.ds(slot * few, few), here])
    wait_all(copy_all(copies))

    @pl.when(where[2] == 1)
    def _():
        total[0] = jnp.dot(near_rows[...], weight[0], preferred_element_type=F32)

    @pl.when(where[2] == 0)
    def _():
        total[0, pl.ds(0, RING * few)] = jnp.dot(
            near_qry[...], weight[0], preferred_element_type=F32
        )

    @pl.loop(1, 3)
    def _(plane):
        total[plane] = jnp.dot(near_rows[...], weight[plane], preferred_element_type=F32)


def attend_kernel(where, total, rows, qry, lengths, *refs):
    sides = (refs[:1], refs[1:3])
    outs = refs[3:7]
    low, mixed = refs[7:]
    mem, few = mixed.shape[1], qry.shape[0] // RING
    encoder = where[2]

    def add_half(plane, source, count):
        for side, pieces in enumerate(sides):
            part = pieces[0].shape[3]
            at = pl.ds(side * part, part)
            result = total[plane, pl.ds(0, count), at]
            first = 0
            for piece in pieces:
                depth = piece.shape[0] * piece.shape[2]
                result += jnp.dot(
                    source[:, pl.ds(first, depth)],
                    piece[:, plane].reshape(depth, part),
                    preferred_element_type=F32,
                )
                first += depth
            low[plane, pl.ds(0, count), at] = result.astype(BF16)

    @pl.when(encoder == 1)
    def _():
        add_half(0, rows, RING * mem)

    @pl.when(encoder == 0)
    def _():
        add_half(0, qry, RING * few)

    @pl.loop(1, 3)
    def _(plane):
        add_half(plane, rows, RING * mem)

    heads = low.shape[2] // HEAD
    scale = 1.0 / math.sqrt(HEAD)

    def heads_of(count):
        column = lax.broadcasted_iota(jnp.int32, (count, mem), 1)

        @pl.loop(0, RING)
        def _(slot):
            own = pl.ds(pl.multiple_of(slot * count, count), count)
            keys = pl.ds(pl.multiple_of(slot * mem, mem), mem)
            length = lengths[slot, pl.ds(0, 1), pl.ds(0, 1)].astype(F32).astype(jnp.int32)
            valid = column < length
            for head in range(heads):
                at = pl.ds(head * HEAD, HEAD)
                scores = (
                    lax.dot_general(
                        low[0, own, at],
                        low[1, keys, at],
                        (((1,), (1,)), ((), ())),
                        preferred_element_type=F32,
                    )
                    * scale
                )
                scores = jnp.where(valid, scores, -1e30)
                expo = jnp.exp(scores - jnp.max(scores, axis=-1, keepdims=True))
                probs = (expo / jnp.sum(expo, axis=-1, keepdims=True)).astype(BF16)
                mixed[slot, pl.ds(0, count), at] = jnp.dot(
                    probs, low[2, keys, at], preferred_element_type=F32
                ).astype(BF16)

    @pl.when(encoder == 1)
    def _():
        heads_of(mem)

    @pl.when(encoder == 0)
    def _():
        heads_of(few)

    for slot in range(RING):
        outs[slot][...] = mixed[slot]


def start_projections(where, mem, few, rows, parts):
    width = rows[0].shape[1]
    _, planes, block, part = parts[0].shape
    half = width // 2
    return call(
        start_kernel,
        (
            jax.ShapeDtypeStruct((planes, RING * mem, 2 * part), F32),
            jax.ShapeDtypeStruct((RING * mem, half), BF16),
            jax.ShapeDtypeStruct((RING * few, half), BF16),
            jax.ShapeDtypeStruct((RING, TAIL, 128), BF16),
        ),
        [SMEM] + [HBM] * 6,
        (VMEM,) * 4,
        [
            pltpu.VMEM((RING * mem, half), BF16),
            pltpu.VMEM((RING * few, half), BF16),
            pltpu.VMEM((planes, half, 2 * part), BF16),
            pltpu.SemaphoreType.DMA((64,)),
        ],
        limit=14,
    )(where, *rows, *parts)


def attend(where, mem, started, far):
    total = started[0]
    planes, _, columns = total.shape
    out = jax.ShapeDtypeStruct((mem, columns), BF16)
    return call(
        attend_kernel,
        (out,) * RING,
        [SMEM] + [VMEM] * 7,
        (VMEM,) * RING,
        [
            pltpu.VMEM((planes, RING * mem, columns), BF16),
            pltpu.VMEM((RING, mem, columns), BF16),
        ],
        limit=14,
    )(where, *started, *far)


def project_kernel(part, where, context, queries, *refs):
    mixed = refs[:4]
    weights = refs[4:6]
    few_in = refs[6] if part else None
    out, few_out = refs[6 + part : 8 + part]
    heads, weight, base, sems = refs[8 + part :]
    x, z, encoder, core = where[0], where[1], where[2], where[3]
    quarter = mixed[0].shape[1] // 2
    inner = quarter * RING
    block = weights[0].shape[1]
    few = queries.shape[1]
    columns = pl.ds(part * RING * block, RING * block)
    rows_base = pltpu.make_async_copy(context.at[core, :, columns], base, sems.at[0])
    few_base = pltpu.make_async_copy(
        queries.at[core, :, columns], base.at[pl.ds(0, few)], sems.at[0]
    )
    copies = []
    for step in range(RING):
        for side in range(2):
            at = pl.multiple_of(side * inner + ((x + step) % RING) * quarter, quarter)
            copies.append(
                pltpu.make_async_copy(
                    mixed[step].at[:, pl.ds(side * quarter, quarter)],
                    heads.at[:, pl.ds(at, quarter)],
                    sems.at[1 + step * 2 + side],
                )
            )
    pieces = []
    crossed = z if part == 0 else 1 - z
    for i in range(RING):
        for side in range(2):
            start = pl.multiple_of((2 * i + crossed) * inner, inner)
            pieces.append(
                pltpu.make_async_copy(
                    weights[side].at[pl.ds(start, inner)],
                    weight.at[i, pl.ds(side * inner, inner)],
                    sems.at[9 + i * 2 + side],
                )
            )

    @pl.when(encoder == 1)
    def _():
        rows_base.start()

    @pl.when(encoder == 0)
    def _():
        few_base.start()

    copy_all(copies)
    copy_all(pieces)

    @pl.when(encoder == 1)
    def _():
        rows_base.wait()

    @pl.when(encoder == 0)
    def _():
        few_base.wait()

    if part:
        few_out[:, pl.ds(0, RING * block)] = few_in[...]
    wait_all(copies)
    for i in range(RING):
        wait_all(pieces[2 * i : 2 * i + 2])
        place = (x - i + RING) % RING
        at = pl.ds(pl.multiple_of(place * block, block), block)
        update = jnp.dot(heads[...], weight[i], preferred_element_type=F32)
        result = (base[:, at].astype(F32) + update).astype(BF16)
        out[:, at] = result
        at = pl.ds(pl.multiple_of((part * RING + place) * block, block), block)
        few_out[:, at] = result[:few]


def project(part, where, context, queries, mixed, weights, few_in=()):
    mem, few = context.shape[1], queries.shape[1]
    inner, block = mixed[0].shape[1] // 2 * RING, weights[0].shape[1]
    return call(
        functools.partial(project_kernel, part),
        (
            jax.ShapeDtypeStruct((mem, RING * block), BF16),
            jax.ShapeDtypeStruct((few, (1 + part) * RING * block), BF16),
        ),
        [SMEM] + [HBM] * 8 + [VMEM] * part,
        (VMEM, VMEM),
        [
            pltpu.VMEM((mem, 2 * inner), BF16),
            pltpu.VMEM((RING, 2 * inner, block), BF16),
            pltpu.VMEM((mem, RING * block), BF16),
            pltpu.SemaphoreType.DMA((17,)),
        ],
        flops=2 * mem * 2 * inner * RING * block,
        moved=2 * (2 * inner * RING * block + 3 * mem * inner),
    )(where, context, queries, *mixed, *weights, *few_in)


def gather_kernel(where, *refs):
    halves = (refs[0:2], refs[2:4])
    ctx_early, qry_early, qry_late = refs[4:6], refs[6:8], refs[8:10]
    ctx_out, qry_out, ctx, qry, sems = refs[10:]
    core, from_encoder = where[3], where[4]
    width = halves[0][0].shape[1]

    def build(rows, few):
        copies = []
        for side in range(2):
            scene = core if side == 0 else 1 - core
            for piece, at in rows[side]:
                target = ctx.at[scene, :, at]
                copies.append(pltpu.make_async_copy(piece, target, sems.at[len(copies)]))
            copies.append(
                pltpu.make_async_copy(few[side], qry.at[scene], sems.at[len(copies)])
            )
        wait_all(copy_all(copies))

    @pl.when(from_encoder == 1)
    def _():
        build(
            [[(halves[i][side], pl.ds(i * width, width)) for i in range(2)] for side in range(2)],
            qry_early,
        )

    @pl.when(from_encoder == 0)
    def _():
        build([[(ctx_early[side], pl.ds(0, 2 * width))] for side in range(2)], qry_late)

    wait_all(
        copy_all(
            [
                pltpu.make_async_copy(ctx, ctx_out, sems.at[0]),
                pltpu.make_async_copy(qry, qry_out, sems.at[1]),
            ]
        )
    )


def gather_result(where, first, second, ctx_early, qry_early, qry_late):
    ctx_shape = (2,) + ctx_early[0].shape
    qry_shape = (2,) + qry_early[0].shape
    return call(
        gather_kernel,
        (jax.ShapeDtypeStruct(ctx_shape, BF16), jax.ShapeDtypeStruct(qry_shape, BF16)),
        [SMEM] + [HBM] * 10,
        (HBM, HBM),
        [
            pltpu.VMEM(ctx_shape, BF16),
            pltpu.VMEM(qry_shape, BF16),
            pltpu.SemaphoreType.DMA((6,)),
        ],
        moved=8 * ctx_early[0].size,
    )(where, *first, *second, *ctx_early, *qry_early, *qry_late)


def both(array):
    return array, other_core(array)


def per_device(context, queries, lengths, norm_gain, qkv_weight, out_weight):
    count = lax.axis_size("section")
    section = lax.axis_index("section")
    place = lax.axis_index("dp")
    core = lax.axis_index("tensor")
    encoders = list(range(count // 2))
    decoders = list(range(count // 2, count))
    before = (section + count - 1) % count
    where = jnp.stack(
        [
            place % RING,
            place // RING,
            (section < count // 2).astype(jnp.int32),
            core,
            (before < count // 2).astype(jnp.int32),
        ]
    ).astype(jnp.int32)
    context, queries = context[0], queries[0]

    mem, few = context.shape[1], queries.shape[1]
    out_shard = out_weight[0]
    out_far = across_z(out_shard)
    own = quarters(where, jnp.swapaxes(qkv_weight[0], 0, 1))
    out_pair = jnp.concatenate([out_shard, out_far])
    near = [own[0]] + [around_x(own[step], step) for step in range(1, RING)]
    arrived = near[1:]
    near = jnp.stack(near)
    far = across_z(after(near, out_pair))

    ctx, qry, normed = norm_scene(
        after(where, *own), context, queries, norm_gain, lengths[0]
    )
    rows = round_ring(after(normed, out_pair, *arrived))
    started = start_projections(where, mem, few, rows, (near, other_core(near)))

    weights = round_ring(after(out_pair, *rows, started[0]))
    far = (
        far,
        other_core(after(far[:2], started[0], *weights)),
        other_core(after(far[2:], started[0], *weights)),
    )
    weights = both(jnp.concatenate(after(weights, *far)))

    mixed = attend(where, mem, started, far)
    ctx_early = relay(after(ctx, mixed[0]), decoders, count)
    qry_early = relay(after(qry, mixed[0]), encoders, count)
    mixed = [mixed[0]] + [around_x(mixed[step], -step) for step in range(1, RING)]

    first, few_first = project(
        0, after(where, qry_early), context, queries, mixed, weights
    )
    first = relay(first, encoders, count)
    second, few_new = project(1, where, context, queries, mixed, weights, (few_first,))
    qry_early = (qry_early, other_core(qry_early))
    second = relay(after(second, qry_early[1]), encoders, count)
    few_new = relay(few_new, decoders, count)
    ctx_new, qry_new = gather_result(
        where,
        both(first),
        (second, other_core(after(second, few_new))),
        (ctx_early, other_core(after(ctx_early, first))),
        qry_early,
        both(few_new),
    )
    return ctx_new[None], qry_new[None]


def solution(mesh):
    return jax.shard_map(
        per_device,
        mesh=mesh,
        in_specs=(
            P("section", "dp", None, None),
            P("section", "dp", None, None),
            P("section", "dp"),
            P("section", None),
            P("section", "dp", None, "tensor"),
            P("section", "tensor", "dp"),
        ),
        out_specs=(P("section", "dp", None, None), P("section", "dp", None, None)),
        check_vma=False,
    )
```

```python
import functools
import math

import jax
import jax.numpy as jnp
from jax import lax
from jax.experimental import pallas as pl
from jax.experimental.pallas import tpu as pltpu
from jax.sharding import PartitionSpec as P

HEAD = 128
RING = 4
TAIL = 16
HBM = pl.BlockSpec(memory_space=pltpu.HBM)
SMEM = pl.BlockSpec(memory_space=pltpu.SMEM)
VMEM = pl.BlockSpec(memory_space=pltpu.VMEM)
BF16 = jnp.bfloat16
F32 = jnp.float32


def around_x(array, by):
    pairs = [
        (z * RING + x, z * RING + (x + by) % RING) for z in range(2) for x in range(RING)
    ]
    return lax.ppermute(array, "dp", pairs)


def around_x_of(array, by, sections):
    pairs = []
    for s in sections:
        for z in range(2):
            for x in range(RING):
                base = s * 2 * RING + z * RING
                pairs.append((base + x, base + (x + by) % RING))
    return lax.ppermute(array, ("section", "dp"), pairs)


def across_z(array):
    return lax.ppermute(array, "dp", [(d, (d + RING) % (2 * RING)) for d in range(2 * RING)])


def other_core(array):
    return lax.ppermute(array, "tensor", [(0, 1), (1, 0)])


def relay(array, sections, count):
    return lax.ppermute(array, "section", [(s, (s + 1) % count) for s in sections])


def round_ring(array, cut):
    left, right = around_x(array, 1), around_x(array, -1)
    return array, left, around_x(left[:cut], 1), around_x(right[cut:], -1), right


def after(array, *others):
    return lax.optimization_barrier((array,) + others)[0]


def copy_all(copies):
    for copy in copies:
        copy.start()
    return copies


def wait_all(copies):
    for copy in copies:
        copy.wait()


def call(kernel, outs, in_specs, out_specs, scratch=(), flops=0, moved=0, limit=16):
    return pl.pallas_call(
        kernel,
        out_shape=outs,
        in_specs=in_specs,
        out_specs=out_specs,
        scratch_shapes=list(scratch),
        compiler_params=pltpu.CompilerParams(vmem_limit_bytes=limit * 1024 * 1024),
        cost_estimate=pl.CostEstimate(flops=1, bytes_accessed=1, transcendentals=0),
    )


def quarter_kernel(where, weight, *pieces):
    x = where[0]
    width = pieces[0].shape[2]
    for step, piece in enumerate(pieces):
        start = pl.multiple_of(((x + step) % RING) * width, width)
        piece[...] = weight[:, :, pl.ds(start, width)]


def quarters(where, weight):
    planes, rows, columns = weight.shape
    piece = jax.ShapeDtypeStruct((planes, rows, columns // RING), BF16)
    return call(
        quarter_kernel, (piece,) * RING, [SMEM, VMEM], (VMEM,) * RING, moved=4 * weight.size
    )(where, weight)


def norm_kernel(where, context, queries, gain, lengths, ctx_out, qry_out, normed, *scratch):
    ctx, qry, sems = scratch
    core = where[3]
    copies = copy_all(
        [
            pltpu.make_async_copy(context.at[core], ctx, sems.at[0]),
            pltpu.make_async_copy(queries.at[core], qry, sems.at[1]),
        ]
    )
    step = 32

    def rows_of(source, raw, below):
        @pl.loop(0, source.shape[0] // step)
        def _(i):
            first = pl.multiple_of(i * step, step)
            low = source[pl.ds(first, step), :]
            wide = low.astype(F32)
            mean = jnp.mean(wide * wide, axis=-1, keepdims=True)
            normed[pl.ds(below + first, step), :] = (
                wide * lax.rsqrt(mean + 1e-06) * gain[...]
            ).astype(BF16)
            raw[pl.ds(first, step), :] = low

    length = lengths[core].astype(F32)
    normed[pl.ds(normed.shape[0] - TAIL, TAIL), :] = jnp.full(
        (TAIL, normed.shape[1]), length
    ).astype(BF16)
    copies[0].wait()
    rows_of(ctx, ctx_out, 0)
    copies[1].wait()
    rows_of(qry, qry_out, ctx.shape[0])


def norm_scene(where, context, queries, gain, lengths):
    ctx = jax.ShapeDtypeStruct(context.shape[1:], BF16)
    qry = jax.ShapeDtypeStruct(queries.shape[1:], BF16)
    rows = ctx.shape[0] + qry.shape[0] + TAIL
    return call(
        norm_kernel,
        (ctx, qry, jax.ShapeDtypeStruct((rows, ctx.shape[1]), BF16)),
        [SMEM, HBM, HBM, VMEM, SMEM],
        (VMEM,) * 3,
        [
            pltpu.VMEM(ctx.shape, BF16),
            pltpu.VMEM(qry.shape, BF16),
            pltpu.SemaphoreType.DMA((2,)),
        ],
        moved=6 * ctx.size,
    )(where, context, queries, gain, lengths)


def start_kernel(where, *refs):
    rows, parts = refs[:5], refs[5:7]
    total, far_rows, far_qry, lengths, near_rows, near_qry, weight, sems = refs[7:]
    x, z = where[0], where[1]
    mem, few = far_rows.shape[0] // RING, far_qry.shape[0] // RING
    width = far_rows.shape[1]
    copies = []

    def take(slot, first, count, columns, target):
        cut = rows[2].shape[0]
        pieces = [(rows[slot if slot < 2 else 4], first, count, 0)]
        if slot == 2:
            low = min(max(cut - first, 0), count)
            pieces = [(rows[2], first, low, 0), (rows[3], first + low - cut, count - low, low)]
        for source, start, size, at in pieces:
            if size > 0:
                copies.append(
                    pltpu.make_async_copy(
                        source.at[pl.ds(start, size), columns],
                        target.at[pl.ds(at, size)],
                        sems.at[len(copies)],
                    )
                )

    for part, first in ((parts[0], 0), (parts[1], parts[0].shape[3])):
        for step in range(RING):
            _, _, block, columns = part.shape
            at = pl.multiple_of(((x - step + RING) % RING) * block, block)
            target = weight.at[:, pl.ds(at, block), pl.ds(first, columns)]
            copies.append(
                pltpu.make_async_copy(part.at[step], target, sems.at[len(copies)])
            )
    for slot in range(RING):
        columns = pl.ds(pl.multiple_of(z * width, width), width)
        take(slot, 0, mem, columns, near_rows.at[pl.ds(slot * mem, mem)])
        take(slot, mem, few, columns, near_qry.at[pl.ds(slot * few, few)])
        take(slot, mem + few, TAIL, pl.ds(0, 128), lengths.at[slot])
    for step in range(RING):
        at = ((1 - z) * RING + (x - step + RING) % RING) * block
        columns = pl.ds(pl.multiple_of(at, block), block)
        here = pl.ds(step * block, block)
        for slot in range(RING):
            take(slot, 0, mem, columns, far_rows.at[pl.ds(slot * mem, mem), here])
            take(slot, mem, few, columns, far_qry.at[pl.ds(slot * few, few), here])
    wait_all(copy_all(copies))

    @pl.when(where[2] == 1)
    def _():
        total[0] = jnp.dot(near_rows[...], weight[0], preferred_element_type=F32)

    @pl.when(where[2] == 0)
    def _():
        total[0, pl.ds(0, RING * few)] = jnp.dot(
            near_qry[...], weight[0], preferred_element_type=F32
        )

    @pl.loop(1, 3)
    def _(plane):
        total[plane] = jnp.dot(near_rows[...], weight[plane], preferred_element_type=F32)


def attend_kernel(where, total, rows, qry, lengths, *refs):
    sides = (refs[:1], refs[1:5])
    outs = refs[5:9]
    low, mixed = refs[9:]
    mem, few = mixed.shape[1], qry.shape[0] // RING
    encoder = where[2]

    def add_half(plane, source, count):
        for side, pieces in enumerate(sides):
            part = pieces[0].shape[3]
            at = pl.ds(side * part, part)
            result = total[plane, pl.ds(0, count), at]
            first = 0
            for piece in pieces:
                depth = piece.shape[0] * piece.shape[2]
                result += jnp.dot(
                    source[:, pl.ds(first, depth)],
                    piece[:, plane].reshape(depth, part),
                    preferred_element_type=F32,
                )
                first += depth
            low[plane, pl.ds(0, count), at] = result.astype(BF16)

    @pl.when(encoder == 1)
    def _():
        add_half(0, rows, RING * mem)

    @pl.when(encoder == 0)
    def _():
        add_half(0, qry, RING * few)

    @pl.loop(1, 3)
    def _(plane):
        add_half(plane, rows, RING * mem)

    heads = low.shape[2] // HEAD
    scale = 1.0 / math.sqrt(HEAD)

    def heads_of(count):
        column = lax.broadcasted_iota(jnp.int32, (count, mem), 1)

        @pl.loop(0, RING)
        def _(slot):
            own = pl.ds(pl.multiple_of(slot * count, count), count)
            keys = pl.ds(pl.multiple_of(slot * mem, mem), mem)
            length = lengths[slot, pl.ds(0, 1), pl.ds(0, 1)].astype(F32).astype(jnp.int32)
            valid = column < length
            for head in range(heads):
                at = pl.ds(head * HEAD, HEAD)
                scores = (
                    lax.dot_general(
                        low[0, own, at],
                        low[1, keys, at],
                        (((1,), (1,)), ((), ())),
                        preferred_element_type=F32,
                    )
                    * scale
                )
                scores = jnp.where(valid, scores, -1e30)
                expo = jnp.exp(scores - jnp.max(scores, axis=-1, keepdims=True))
                probs = (expo / jnp.sum(expo, axis=-1, keepdims=True)).astype(BF16)
                mixed[slot, pl.ds(0, count), at] = jnp.dot(
                    probs, low[2, keys, at], preferred_element_type=F32
                ).astype(BF16)

    @pl.when(encoder == 1)
    def _():
        heads_of(mem)

    @pl.when(encoder == 0)
    def _():
        heads_of(few)

    for slot in range(RING):
        outs[slot][...] = mixed[slot]


def start_projections(where, mem, few, rows, parts):
    width = rows[0].shape[1]
    _, planes, block, part = parts[0].shape
    half = width // 2
    return call(
        start_kernel,
        (
            jax.ShapeDtypeStruct((planes, RING * mem, 2 * part), F32),
            jax.ShapeDtypeStruct((RING * mem, half), BF16),
            jax.ShapeDtypeStruct((RING * few, half), BF16),
            jax.ShapeDtypeStruct((RING, TAIL, 128), BF16),
        ),
        [SMEM] + [HBM] * 7,
        (VMEM,) * 4,
        [
            pltpu.VMEM((RING * mem, half), BF16),
            pltpu.VMEM((RING * few, half), BF16),
            pltpu.VMEM((planes, half, 2 * part), BF16),
            pltpu.SemaphoreType.DMA((64,)),
        ],
        limit=14,
    )(where, *rows, *parts)


def attend(where, mem, started, far):
    total = started[0]
    planes, _, columns = total.shape
    out = jax.ShapeDtypeStruct((mem, columns), BF16)
    return call(
        attend_kernel,
        (out,) * RING,
        [SMEM] + [VMEM] * 9,
        (VMEM,) * RING,
        [
            pltpu.VMEM((planes, RING * mem, columns), BF16),
            pltpu.VMEM((RING, mem, columns), BF16),
        ],
        limit=14,
    )(where, *started, *far)


def project_kernel(part, where, context, queries, *refs):
    mixed = refs[:4]
    weights = refs[4:6]
    few_in = refs[6] if part else None
    out, few_out = refs[6 + part : 8 + part]
    heads, weight, base, sems = refs[8 + part :]
    x, z, encoder, core = where[0], where[1], where[2], where[3]
    quarter = mixed[0].shape[1] // 2
    inner = quarter * RING
    block = weights[0].shape[1]
    few = queries.shape[1]
    columns = pl.ds(part * RING * block, RING * block)
    rows_base = pltpu.make_async_copy(context.at[core, :, columns], base, sems.at[0])
    few_base = pltpu.make_async_copy(
        queries.at[core, :, columns], base.at[pl.ds(0, few)], sems.at[0]
    )
    copies = []
    for step in range(RING):
        for side in range(2):
            at = pl.multiple_of(side * inner + ((x + step) % RING) * quarter, quarter)
            copies.append(
                pltpu.make_async_copy(
                    mixed[step].at[:, pl.ds(side * quarter, quarter)],
                    heads.at[:, pl.ds(at, quarter)],
                    sems.at[1 + step * 2 + side],
                )
            )
    pieces = []
    crossed = z if part == 0 else 1 - z
    for i in range(RING):
        for side in range(2):
            start = pl.multiple_of((2 * i + crossed) * inner, inner)
            pieces.append(
                pltpu.make_async_copy(
                    weights[side].at[pl.ds(start, inner)],
                    weight.at[i, pl.ds(side * inner, inner)],
                    sems.at[9 + i * 2 + side],
                )
            )

    @pl.when(encoder == 1)
    def _():
        rows_base.start()

    @pl.when(encoder == 0)
    def _():
        few_base.start()

    copy_all(copies)
    copy_all(pieces)

    @pl.when(encoder == 1)
    def _():
        rows_base.wait()

    @pl.when(encoder == 0)
    def _():
        few_base.wait()

    if part:
        few_out[:, pl.ds(0, RING * block)] = few_in[...]
    wait_all(copies)
    for i in range(RING):
        wait_all(pieces[2 * i : 2 * i + 2])
        place = (x - i + RING) % RING
        at = pl.ds(pl.multiple_of(place * block, block), block)
        update = jnp.dot(heads[...], weight[i], preferred_element_type=F32)
        result = (base[:, at].astype(F32) + update).astype(BF16)
        out[:, at] = result
        at = pl.ds(pl.multiple_of((part * RING + place) * block, block), block)
        few_out[:, at] = result[:few]


def project(part, where, context, queries, mixed, weights, few_in=()):
    mem, few = context.shape[1], queries.shape[1]
    inner, block = mixed[0].shape[1] // 2 * RING, weights[0].shape[1]
    return call(
        functools.partial(project_kernel, part),
        (
            jax.ShapeDtypeStruct((mem, RING * block), BF16),
            jax.ShapeDtypeStruct((few, (1 + part) * RING * block), BF16),
        ),
        [SMEM] + [HBM] * 8 + [VMEM] * part,
        (VMEM, VMEM),
        [
            pltpu.VMEM((mem, 2 * inner), BF16),
            pltpu.VMEM((RING, 2 * inner, block), BF16),
            pltpu.VMEM((mem, RING * block), BF16),
            pltpu.SemaphoreType.DMA((17,)),
        ],
        flops=2 * mem * 2 * inner * RING * block,
        moved=2 * (2 * inner * RING * block + 3 * mem * inner),
    )(where, context, queries, *mixed, *weights, *few_in)


def gather_kernel(where, *refs):
    halves = (refs[0:2], refs[2:4])
    ctx_early, qry_early, qry_late = refs[4:6], refs[6:8], refs[8:10]
    ctx_out, qry_out, ctx, qry, sems = refs[10:]
    core, from_encoder = where[3], where[4]
    width = halves[0][0].shape[1]

    def build(rows, few):
        copies = []
        for side in range(2):
            scene = core if side == 0 else 1 - core
            for piece, at in rows[side]:
                target = ctx.at[scene, :, at]
                copies.append(pltpu.make_async_copy(piece, target, sems.at[len(copies)]))
            copies.append(
                pltpu.make_async_copy(few[side], qry.at[scene], sems.at[len(copies)])
            )
        wait_all(copy_all(copies))

    @pl.when(from_encoder == 1)
    def _():
        build(
            [[(halves[i][side], pl.ds(i * width, width)) for i in range(2)] for side in range(2)],
            qry_early,
        )

    @pl.when(from_encoder == 0)
    def _():
        build([[(ctx_early[side], pl.ds(0, 2 * width))] for side in range(2)], qry_late)

    wait_all(
        copy_all(
            [
                pltpu.make_async_copy(ctx, ctx_out, sems.at[0]),
                pltpu.make_async_copy(qry, qry_out, sems.at[1]),
            ]
        )
    )


def gather_result(where, first, second, ctx_early, qry_early, qry_late):
    ctx_shape = (2,) + ctx_early[0].shape
    qry_shape = (2,) + qry_early[0].shape
    return call(
        gather_kernel,
        (jax.ShapeDtypeStruct(ctx_shape, BF16), jax.ShapeDtypeStruct(qry_shape, BF16)),
        [SMEM] + [HBM] * 10,
        (HBM, HBM),
        [
            pltpu.VMEM(ctx_shape, BF16),
            pltpu.VMEM(qry_shape, BF16),
            pltpu.SemaphoreType.DMA((6,)),
        ],
        moved=8 * ctx_early[0].size,
    )(where, *first, *second, *ctx_early, *qry_early, *qry_late)


def both(array):
    return array, other_core(array)


def per_device(context, queries, lengths, norm_gain, qkv_weight, out_weight):
    count = lax.axis_size("section")
    section = lax.axis_index("section")
    place = lax.axis_index("dp")
    core = lax.axis_index("tensor")
    encoders = list(range(count // 2))
    decoders = list(range(count // 2, count))
    before = (section + count - 1) % count
    where = jnp.stack(
        [
            place % RING,
            place // RING,
            (section < count // 2).astype(jnp.int32),
            core,
            (before < count // 2).astype(jnp.int32),
        ]
    ).astype(jnp.int32)
    context, queries = context[0], queries[0]

    mem, few = context.shape[1], queries.shape[1]
    out_shard = out_weight[0]
    out_far = across_z(out_shard)
    own = quarters(where, jnp.swapaxes(qkv_weight[0], 0, 1))
    out_pair = jnp.concatenate([out_shard, out_far])
    near = [own[0]] + [around_x(own[step], step) for step in range(1, RING)]
    arrived = near[1:]
    near = jnp.stack(near)
    far = across_z(after(near, out_pair))

    ctx, qry, normed = norm_scene(
        after(where, *own), context, queries, norm_gain, lengths[0]
    )
    cut = (normed.shape[0] // 32 + 1) * 16
    rows = round_ring(after(normed, out_pair, *arrived), cut)
    started = start_projections(where, mem, few, rows, (near, other_core(near)))

    weights = round_ring(after(out_pair, *rows, started[0]), out_shard.shape[0])
    far_other = [other_core(after(far[step : step + 1], started[0])) for step in range(RING)]

    mixed = attend(after(where, weights[1], weights[4]), mem, started, (far, *far_other))
    weights = both(jnp.concatenate(after(weights, mixed[0])))
    mixed = [mixed[0]] + [around_x(mixed[step], -step) for step in range(1, RING)]
    ctx_early = relay(after(ctx, *mixed), decoders, count)
    qry_early = relay(after(qry, *mixed), encoders, count)

    first, few_first = project(0, where, context, queries, mixed, weights)
    first = relay(first, encoders, count)
    second, few_new = project(1, where, context, queries, mixed, weights, (few_first,))
    qry_early = (qry_early, other_core(qry_early))
    second = relay(after(second, qry_early[1]), encoders, count)
    few_new = relay(few_new, decoders, count)
    ctx_new, qry_new = gather_result(
        where,
        both(first),
        (second, other_core(after(second, few_new))),
        (ctx_early, other_core(after(ctx_early, first))),
        qry_early,
        both(few_new),
    )
    return ctx_new[None], qry_new[None]


def solution(mesh):
    return jax.shard_map(
        per_device,
        mesh=mesh,
        in_specs=(
            P("section", "dp", None, None),
            P("section", "dp", None, None),
            P("section", "dp"),
            P("section", None),
            P("section", "dp", None, "tensor"),
            P("section", "tensor", "dp"),
        ),
        out_specs=(P("section", "dp", None, None), P("section", "dp", None, None)),
        check_vma=False,
    )
```

```python
import functools
import math

import jax
import jax.numpy as jnp
from jax import lax
from jax.experimental import pallas as pl
from jax.experimental.pallas import tpu as pltpu
from jax.sharding import PartitionSpec as P

HEAD = 128
RING = 4
TAIL = 16
HBM = pl.BlockSpec(memory_space=pltpu.HBM)
SMEM = pl.BlockSpec(memory_space=pltpu.SMEM)
VMEM = pl.BlockSpec(memory_space=pltpu.VMEM)
BF16 = jnp.bfloat16
F32 = jnp.float32


def around_x(array, by):
    pairs = [
        (z * RING + x, z * RING + (x + by) % RING) for z in range(2) for x in range(RING)
    ]
    return lax.ppermute(array, "dp", pairs)


def around_x_of(array, by, sections):
    pairs = []
    for s in sections:
        for z in range(2):
            for x in range(RING):
                base = s * 2 * RING + z * RING
                pairs.append((base + x, base + (x + by) % RING))
    return lax.ppermute(array, ("section", "dp"), pairs)


def across_z(array):
    return lax.ppermute(array, "dp", [(d, (d + RING) % (2 * RING)) for d in range(2 * RING)])


def other_core(array):
    return lax.ppermute(array, "tensor", [(0, 1), (1, 0)])


def relay(array, sections, count):
    return lax.ppermute(array, "section", [(s, (s + 1) % count) for s in sections])


def round_ring(array, cut):
    left, right = around_x(array, 1), around_x(array, -1)
    return array, left, around_x(left[:cut], 1), around_x(right[cut:], -1), right


def after(array, *others):
    return lax.optimization_barrier((array,) + others)[0]


def copy_all(copies):
    for copy in copies:
        copy.start()
    return copies


def wait_all(copies):
    for copy in copies:
        copy.wait()


def call(kernel, outs, in_specs, out_specs, scratch=(), limit=16):
    return pl.pallas_call(
        kernel,
        out_shape=outs,
        in_specs=in_specs,
        out_specs=out_specs,
        scratch_shapes=list(scratch),
        compiler_params=pltpu.CompilerParams(vmem_limit_bytes=limit * 1024 * 1024),
        cost_estimate=pl.CostEstimate(flops=1, bytes_accessed=1, transcendentals=0),
    )


def quarter_kernel(where, weight, *pieces):
    x = where[0]
    width = pieces[0].shape[2]
    for step, piece in enumerate(pieces):
        start = pl.multiple_of(((x + step) % RING) * width, width)
        piece[...] = weight[:, :, pl.ds(start, width)]


def quarters(where, weight):
    planes, rows, columns = weight.shape
    piece = jax.ShapeDtypeStruct((planes, rows, columns // RING), BF16)
    return call(
        quarter_kernel, (piece,) * RING, [SMEM, VMEM], (VMEM,) * RING
    )(where, weight)


def norm_kernel(
    where, context, queries, gain, lengths, ctx_out, qry_out, normed, qry_normed, *scratch
):
    ctx, qry, sems = scratch
    core = where[3]
    copies = copy_all(
        [
            pltpu.make_async_copy(context.at[core], ctx, sems.at[0]),
            pltpu.make_async_copy(queries.at[core], qry, sems.at[1]),
        ]
    )
    step = 32

    def rows_of(source, raw, target):
        @pl.loop(0, source.shape[0] // step)
        def _(i):
            first = pl.multiple_of(i * step, step)
            low = source[pl.ds(first, step), :]
            wide = low.astype(F32)
            mean = jnp.mean(wide * wide, axis=-1, keepdims=True)
            target[pl.ds(first, step), :] = (
                wide * lax.rsqrt(mean + 1e-06) * gain[...]
            ).astype(BF16)
            raw[pl.ds(first, step), :] = low

    length = lengths[core].astype(F32)
    normed[pl.ds(normed.shape[0] - TAIL, TAIL), :] = jnp.full(
        (TAIL, normed.shape[1]), length
    ).astype(BF16)
    copies[0].wait()
    rows_of(ctx, ctx_out, normed)
    copies[1].wait()
    rows_of(qry, qry_out, qry_normed)


def norm_scene(where, context, queries, gain, lengths):
    ctx = jax.ShapeDtypeStruct(context.shape[1:], BF16)
    qry = jax.ShapeDtypeStruct(queries.shape[1:], BF16)
    rows = ctx.shape[0] + TAIL
    return call(
        norm_kernel,
        (ctx, qry, jax.ShapeDtypeStruct((rows, ctx.shape[1]), BF16), qry),
        [SMEM, HBM, HBM, VMEM, SMEM],
        (VMEM,) * 4,
        [
            pltpu.VMEM(ctx.shape, BF16),
            pltpu.VMEM(qry.shape, BF16),
            pltpu.SemaphoreType.DMA((2,)),
        ],
    )(where, context, queries, gain, lengths)


def start_kernel(where, *refs):
    rows, queries, parts = refs[:5], refs[5:9], refs[9:11]
    total, far_rows, far_qry, lengths, near_rows, near_qry, weight, sems = refs[11:]
    x, z = where[0], where[1]
    mem, few = far_rows.shape[0] // RING, far_qry.shape[0] // RING
    width = far_rows.shape[1]
    copies = []

    def take_queries(slot, columns, target):
        source = queries[slot].at[:, columns]
        copies.append(pltpu.make_async_copy(source, target, sems.at[len(copies)]))

    def take(slot, first, count, columns, target):
        cut = rows[2].shape[0]
        pieces = [(rows[slot if slot < 2 else 4], first, count, 0)]
        if slot == 2:
            low = min(max(cut - first, 0), count)
            pieces = [(rows[2], first, low, 0), (rows[3], first + low - cut, count - low, low)]
        for source, start, size, at in pieces:
            if size > 0:
                copies.append(
                    pltpu.make_async_copy(
                        source.at[pl.ds(start, size), columns],
                        target.at[pl.ds(at, size)],
                        sems.at[len(copies)],
                    )
                )

    for part, first in ((parts[0], 0), (parts[1], parts[0].shape[3])):
        for step in range(RING):
            _, _, block, columns = part.shape
            at = pl.multiple_of(((x - step + RING) % RING) * block, block)
            target = weight.at[:, pl.ds(at, block), pl.ds(first, columns)]
            copies.append(
                pltpu.make_async_copy(part.at[step], target, sems.at[len(copies)])
            )
    for slot in range(RING):
        columns = pl.ds(pl.multiple_of(z * width, width), width)
        take(slot, 0, mem, columns, near_rows.at[pl.ds(slot * mem, mem)])
        take_queries(slot, columns, near_qry.at[pl.ds(slot * few, few)])
        take(slot, mem, TAIL, pl.ds(0, 128), lengths.at[slot])
    for step in range(RING):
        at = ((1 - z) * RING + (x - step + RING) % RING) * block
        columns = pl.ds(pl.multiple_of(at, block), block)
        here = pl.ds(step * block, block)
        for slot in range(RING):
            take(slot, 0, mem, columns, far_rows.at[pl.ds(slot * mem, mem), here])
            take_queries(slot, columns, far_qry.at[pl.ds(slot * few, few), here])
    wait_all(copy_all(copies))

    @pl.when(where[2] == 1)
    def _():
        total[0] = jnp.dot(near_rows[...], weight[0], preferred_element_type=F32)

    @pl.when(where[2] == 0)
    def _():
        total[0, pl.ds(0, RING * few)] = jnp.dot(
            near_qry[...], weight[0], preferred_element_type=F32
        )

    @pl.loop(1, 3)
    def _(plane):
        total[plane] = jnp.dot(near_rows[...], weight[plane], preferred_element_type=F32)


def attend_kernel(where, total, rows, qry, lengths, *refs):
    sides = (refs[:1], refs[1:3])
    outs = refs[3:7]
    low, mixed = refs[7:]
    mem, few = mixed.shape[1], qry.shape[0] // RING
    encoder = where[2]

    def add_half(plane, source, count):
        for side, pieces in enumerate(sides):
            part = pieces[0].shape[3]
            at = pl.ds(side * part, part)
            result = total[plane, pl.ds(0, count), at]
            first = 0
            for piece in pieces:
                depth = piece.shape[0] * piece.shape[2]
                result += jnp.dot(
                    source[:, pl.ds(first, depth)],
                    piece[:, plane].reshape(depth, part),
                    preferred_element_type=F32,
                )
                first += depth
            low[plane, pl.ds(0, count), at] = result.astype(BF16)

    @pl.when(encoder == 1)
    def _():
        add_half(0, rows, RING * mem)

    @pl.when(encoder == 0)
    def _():
        add_half(0, qry, RING * few)

    @pl.loop(1, 3)
    def _(plane):
        add_half(plane, rows, RING * mem)

    heads = low.shape[2] // HEAD
    scale = 1.0 / math.sqrt(HEAD)

    def heads_of(count):
        column = lax.broadcasted_iota(jnp.int32, (count, mem), 1)

        @pl.loop(0, RING)
        def _(slot):
            own = pl.ds(pl.multiple_of(slot * count, count), count)
            keys = pl.ds(pl.multiple_of(slot * mem, mem), mem)
            length = lengths[slot, pl.ds(0, 1), pl.ds(0, 1)].astype(F32).astype(jnp.int32)
            valid = column < length
            for head in range(heads):
                at = pl.ds(head * HEAD, HEAD)
                scores = (
                    lax.dot_general(
                        low[0, own, at],
                        low[1, keys, at],
                        (((1,), (1,)), ((), ())),
                        preferred_element_type=F32,
                    )
                    * scale
                )
                scores = jnp.where(valid, scores, -1e30)
                expo = jnp.exp(scores - jnp.max(scores, axis=-1, keepdims=True))
                probs = (expo / jnp.sum(expo, axis=-1, keepdims=True)).astype(BF16)
                mixed[slot, pl.ds(0, count), at] = jnp.dot(
                    probs, low[2, keys, at], preferred_element_type=F32
                ).astype(BF16)

    @pl.when(encoder == 1)
    def _():
        heads_of(mem)

    @pl.when(encoder == 0)
    def _():
        heads_of(few)

    for slot in range(RING):
        outs[slot][...] = mixed[slot]


def start_projections(where, mem, few, rows, queries, parts):
    width = rows[0].shape[1]
    _, planes, block, part = parts[0].shape
    half = width // 2
    return call(
        start_kernel,
        (
            jax.ShapeDtypeStruct((planes, RING * mem, 2 * part), F32),
            jax.ShapeDtypeStruct((RING * mem, half), BF16),
            jax.ShapeDtypeStruct((RING * few, half), BF16),
            jax.ShapeDtypeStruct((RING, TAIL, 128), BF16),
        ),
        [SMEM] + [HBM] * 11,
        (VMEM,) * 4,
        [
            pltpu.VMEM((RING * mem, half), BF16),
            pltpu.VMEM((RING * few, half), BF16),
            pltpu.VMEM((planes, half, 2 * part), BF16),
            pltpu.SemaphoreType.DMA((64,)),
        ],
        limit=14,
    )(where, *rows, *queries, *parts)


def attend(where, mem, started, far):
    total = started[0]
    planes, _, columns = total.shape
    out = jax.ShapeDtypeStruct((mem, columns), BF16)
    return call(
        attend_kernel,
        (out,) * RING,
        [SMEM] + [VMEM] * 7,
        (VMEM,) * RING,
        [
            pltpu.VMEM((planes, RING * mem, columns), BF16),
            pltpu.VMEM((RING, mem, columns), BF16),
        ],
        limit=14,
    )(where, *started, *far)


def project_kernel(part, where, context, queries, *refs):
    mixed = refs[:4]
    weights = refs[4:6]
    few_in = refs[6] if part else None
    out, few_out = refs[6 + part : 8 + part]
    heads, base, sems = refs[8 + part :]
    x, z, encoder, core = where[0], where[1], where[2], where[3]
    quarter = mixed[0].shape[1] // 2
    inner = quarter * RING
    block = weights[0].shape[1]
    few = queries.shape[1]
    columns = pl.ds(part * RING * block, RING * block)
    rows_base = pltpu.make_async_copy(context.at[core, :, columns], base, sems.at[0])
    few_base = pltpu.make_async_copy(
        queries.at[core, :, columns], base.at[pl.ds(0, few)], sems.at[0]
    )
    copies = []
    for step in range(RING):
        for side in range(2):
            at = pl.multiple_of(side * inner + ((x + step) % RING) * quarter, quarter)
            copies.append(
                pltpu.make_async_copy(
                    mixed[step].at[:, pl.ds(side * quarter, quarter)],
                    heads.at[:, pl.ds(at, quarter)],
                    sems.at[1 + step * 2 + side],
                )
            )
    crossed = z if part == 0 else 1 - z

    @pl.when(encoder == 1)
    def _():
        rows_base.start()

    @pl.when(encoder == 0)
    def _():
        few_base.start()

    copy_all(copies)

    @pl.when(encoder == 1)
    def _():
        rows_base.wait()

    @pl.when(encoder == 0)
    def _():
        few_base.wait()

    if part:
        few_out[:, pl.ds(0, RING * block)] = few_in[...]
    wait_all(copies)
    for i in range(RING):
        place = (x - i + RING) % RING
        start = pl.ds(pl.multiple_of((2 * i + crossed) * inner, inner), inner)
        at = pl.ds(pl.multiple_of(place * block, block), block)
        update = sum(
            jnp.dot(
                heads[:, pl.ds(side * inner, inner)],
                weights[side][start, :],
                preferred_element_type=F32,
            )
            for side in range(2)
        )
        result = (base[:, at].astype(F32) + update).astype(BF16)
        out[:, at] = result
        at = pl.ds(pl.multiple_of((part * RING + place) * block, block), block)
        few_out[:, at] = result[:few]


def project(part, where, context, queries, mixed, weights, few_in=()):
    mem, few = context.shape[1], queries.shape[1]
    inner, block = mixed[0].shape[1] // 2 * RING, weights[0].shape[1]
    return call(
        functools.partial(project_kernel, part),
        (
            jax.ShapeDtypeStruct((mem, RING * block), BF16),
            jax.ShapeDtypeStruct((few, (1 + part) * RING * block), BF16),
        ),
        [SMEM] + [HBM] * 6 + [VMEM] * (2 + part),
        (VMEM, VMEM),
        [
            pltpu.VMEM((mem, 2 * inner), BF16),
            pltpu.VMEM((mem, RING * block), BF16),
            pltpu.SemaphoreType.DMA((9,)),
        ],
    )(where, context, queries, *mixed, *weights, *few_in)


def gather_kernel(where, *refs):
    halves = (refs[0:2], refs[2:4])
    ctx_early, qry_early, qry_late = refs[4:6], refs[6:8], refs[8:10]
    ctx_out, qry_out, ctx, qry, sems = refs[10:]
    core, from_encoder = where[3], where[4]
    width = halves[0][0].shape[1]

    def build(rows, few):
        copies = []
        for side in range(2):
            scene = core if side == 0 else 1 - core
            for piece, at in rows[side]:
                target = ctx.at[scene, :, at]
                copies.append(pltpu.make_async_copy(piece, target, sems.at[len(copies)]))
            copies.append(
                pltpu.make_async_copy(few[side], qry.at[scene], sems.at[len(copies)])
            )
        wait_all(copy_all(copies))

    @pl.when(from_encoder == 1)
    def _():
        build(
            [[(halves[i][side], pl.ds(i * width, width)) for i in range(2)] for side in range(2)],
            qry_early,
        )

    @pl.when(from_encoder == 0)
    def _():
        build([[(ctx_early[side], pl.ds(0, 2 * width))] for side in range(2)], qry_late)

    wait_all(
        copy_all(
            [
                pltpu.make_async_copy(ctx, ctx_out, sems.at[0]),
                pltpu.make_async_copy(qry, qry_out, sems.at[1]),
            ]
        )
    )


def gather_result(where, first, second, ctx_early, qry_early, qry_late):
    ctx_shape = (2,) + ctx_early[0].shape
    qry_shape = (2,) + qry_early[0].shape
    return call(
        gather_kernel,
        (jax.ShapeDtypeStruct(ctx_shape, BF16), jax.ShapeDtypeStruct(qry_shape, BF16)),
        [SMEM] + [HBM] * 10,
        (HBM, HBM),
        [
            pltpu.VMEM(ctx_shape, BF16),
            pltpu.VMEM(qry_shape, BF16),
            pltpu.SemaphoreType.DMA((6,)),
        ],
    )(where, *first, *second, *ctx_early, *qry_early, *qry_late)


def both(array):
    return array, other_core(array)


def per_device(context, queries, lengths, norm_gain, qkv_weight, out_weight):
    count = lax.axis_size("section")
    section = lax.axis_index("section")
    place = lax.axis_index("dp")
    core = lax.axis_index("tensor")
    encoders = list(range(count // 2))
    decoders = list(range(count // 2, count))
    before = (section + count - 1) % count
    where = jnp.stack(
        [
            place % RING,
            place // RING,
            (section < count // 2).astype(jnp.int32),
            core,
            (before < count // 2).astype(jnp.int32),
        ]
    ).astype(jnp.int32)
    context, queries = context[0], queries[0]

    mem, few = context.shape[1], queries.shape[1]
    out_shard = out_weight[0]
    out_far = across_z(out_shard)
    own = quarters(where, jnp.swapaxes(qkv_weight[0], 0, 1))
    out_pair = jnp.concatenate([out_shard, out_far])
    near = [own[0]] + [around_x(own[step], step) for step in range(1, RING)]
    arrived = near[1:]
    near = jnp.stack(near)
    far = across_z(after(near, out_pair))

    ctx, qry, normed, qry_normed = norm_scene(
        after(where, *own), context, queries, norm_gain, lengths[0]
    )
    cut = (normed.shape[0] // 32 + 1) * 16
    rows = round_ring(after(normed, out_pair, *arrived), cut)
    qry_sent = after(qry_normed, rows[1], rows[4])
    qry_rows = [qry_normed] + [around_x_of(qry_sent, step, decoders) for step in range(1, RING)]
    started = start_projections(where, mem, few, rows, qry_rows, (near, other_core(near)))

    weights = round_ring(after(out_pair, *rows, started[0]), out_shard.shape[0])
    far_other = [other_core(after(far[i : i + 2], started[0])) for i in (0, 2)]

    mixed = attend(after(where, weights[1], weights[4]), mem, started, (far, *far_other))
    weights = both(jnp.concatenate(after(weights, mixed[0])))
    mixed = [mixed[0]] + [around_x(mixed[step], -step) for step in range(1, RING)]
    ctx_early = relay(after(ctx, *mixed), decoders, count)
    qry_early = relay(after(qry, *mixed), encoders, count)

    first, few_first = project(0, where, context, queries, mixed, weights)
    first = relay(first, encoders, count)
    second, few_new = project(1, where, context, queries, mixed, weights, (few_first,))
    qry_early = (qry_early, other_core(qry_early))
    second = relay(after(second, qry_early[1]), encoders, count)
    few_new = relay(few_new, decoders, count)
    ctx_new, qry_new = gather_result(
        where,
        both(first),
        (second, other_core(after(second, few_new))),
        (ctx_early, other_core(after(ctx_early, first))),
        qry_early,
        both(few_new),
    )
    return ctx_new[None], qry_new[None]


def solution(mesh):
    return jax.shard_map(
        per_device,
        mesh=mesh,
        in_specs=(
            P("section", "dp", None, None),
            P("section", "dp", None, None),
            P("section", "dp"),
            P("section", None),
            P("section", "dp", None, "tensor"),
            P("section", "tensor", "dp"),
        ),
        out_specs=(P("section", "dp", None, None), P("section", "dp", None, None)),
        check_vma=False,
    )
```

```python
import functools
import math

import jax
import jax.numpy as jnp
from jax import lax
from jax.experimental import pallas as pl
from jax.experimental.pallas import tpu as pltpu
from jax.sharding import PartitionSpec as P

HEAD = 128
RING = 4
TAIL = 16
HBM = pl.BlockSpec(memory_space=pltpu.HBM)
SMEM = pl.BlockSpec(memory_space=pltpu.SMEM)
VMEM = pl.BlockSpec(memory_space=pltpu.VMEM)
BF16 = jnp.bfloat16
F32 = jnp.float32


def around_x(array, by):
    pairs = [
        (z * RING + x, z * RING + (x + by) % RING) for z in range(2) for x in range(RING)
    ]
    return lax.ppermute(array, "dp", pairs)


def across_z(array):
    return lax.ppermute(array, "dp", [(d, (d + RING) % (2 * RING)) for d in range(2 * RING)])


def other_core(array):
    return lax.ppermute(array, "tensor", [(0, 1), (1, 0)])


def relay(array, sections, count):
    return lax.ppermute(array, "section", [(s, (s + 1) % count) for s in sections])


def round_ring(array, cut, *before_right):
    left, right = around_x(array, 1), around_x(after(array, *before_right), -1)
    return array, left, around_x(left[:cut], 1), around_x(right[cut:], -1), right


def after(array, *others):
    return lax.optimization_barrier((array,) + others)[0]


def copy_all(copies):
    for copy in copies:
        copy.start()
    return copies


def wait_all(copies):
    for copy in copies:
        copy.wait()


def call(kernel, outs, in_specs, out_specs, scratch=(), limit=16):
    return pl.pallas_call(
        kernel,
        out_shape=outs,
        in_specs=in_specs,
        out_specs=out_specs,
        scratch_shapes=list(scratch),
        compiler_params=pltpu.CompilerParams(vmem_limit_bytes=limit * 1024 * 1024),
        cost_estimate=pl.CostEstimate(flops=1, bytes_accessed=1, transcendentals=0),
    )


def quarter_kernel(where, weight, *pieces):
    x = where[0]
    width = pieces[0].shape[2]
    for step, piece in enumerate(pieces):
        start = pl.multiple_of(((x + step) % RING) * width, width)
        piece[...] = weight[:, :, pl.ds(start, width)]


def quarters(where, weight):
    planes, rows, columns = weight.shape
    piece = jax.ShapeDtypeStruct((planes, rows, columns // RING), BF16)
    return call(
        quarter_kernel, (piece,) * RING, [SMEM, VMEM], (VMEM,) * RING
    )(where, weight)


def norm_kernel(where, context, queries, gain, lengths, ctx_out, qry_out, normed, *scratch):
    ctx, qry, sems = scratch
    core = where[3]
    copies = copy_all(
        [
            pltpu.make_async_copy(context.at[core], ctx, sems.at[0]),
            pltpu.make_async_copy(queries.at[core], qry, sems.at[1]),
        ]
    )
    step = 32

    def rows_of(source, raw, below):
        @pl.loop(0, source.shape[0] // step)
        def _(i):
            first = pl.multiple_of(i * step, step)
            low = source[pl.ds(first, step), :]
            wide = low.astype(F32)
            mean = jnp.mean(wide * wide, axis=-1, keepdims=True)
            normed[pl.ds(below + first, step), :] = (
                wide * lax.rsqrt(mean + 1e-06) * gain[...]
            ).astype(BF16)
            raw[pl.ds(first, step), :] = low

    length = lengths[core].astype(F32)
    normed[pl.ds(normed.shape[0] - TAIL, TAIL), :] = jnp.full(
        (TAIL, normed.shape[1]), length
    ).astype(BF16)
    copies[0].wait()
    rows_of(ctx, ctx_out, 0)
    copies[1].wait()
    rows_of(qry, qry_out, ctx.shape[0])


def norm_scene(where, context, queries, gain, lengths):
    ctx = jax.ShapeDtypeStruct(context.shape[1:], BF16)
    qry = jax.ShapeDtypeStruct(queries.shape[1:], BF16)
    rows = ctx.shape[0] + qry.shape[0] + TAIL
    return call(
        norm_kernel,
        (ctx, qry, jax.ShapeDtypeStruct((rows, ctx.shape[1]), BF16)),
        [SMEM, HBM, HBM, VMEM, SMEM],
        (VMEM,) * 3,
        [
            pltpu.VMEM(ctx.shape, BF16),
            pltpu.VMEM(qry.shape, BF16),
            pltpu.SemaphoreType.DMA((2,)),
        ],
    )(where, context, queries, gain, lengths)


def start_kernel(where, *refs):
    rows, parts = refs[:5], refs[5:7]
    total, far_rows, far_qry, lengths, near_rows, near_qry, weight, sems = refs[7:]
    x, z = where[0], where[1]
    mem, few = far_rows.shape[0] // RING, far_qry.shape[0] // RING
    width = far_rows.shape[1]
    copies = []

    def take(slot, first, count, columns, target):
        cut = rows[2].shape[0]
        pieces = [(rows[slot if slot < 2 else 4], first, count, 0)]
        if slot == 2:
            low = min(max(cut - first, 0), count)
            pieces = [(rows[2], first, low, 0), (rows[3], first + low - cut, count - low, low)]
        for source, start, size, at in pieces:
            if size > 0:
                copies.append(
                    pltpu.make_async_copy(
                        source.at[pl.ds(start, size), columns],
                        target.at[pl.ds(at, size)],
                        sems.at[len(copies)],
                    )
                )

    for part, first in ((parts[0], 0), (parts[1], parts[0].shape[3])):
        for step in range(RING):
            _, _, block, columns = part.shape
            at = pl.multiple_of(((x - step + RING) % RING) * block, block)
            target = weight.at[:, pl.ds(at, block), pl.ds(first, columns)]
            copies.append(
                pltpu.make_async_copy(part.at[step], target, sems.at[len(copies)])
            )
    for slot in range(RING):
        columns = pl.ds(pl.multiple_of(z * width, width), width)
        take(slot, 0, mem, columns, near_rows.at[pl.ds(slot * mem, mem)])
        take(slot, mem, few, columns, near_qry.at[pl.ds(slot * few, few)])
        take(slot, mem + few, TAIL, pl.ds(0, 128), lengths.at[slot])
    for step in range(RING):
        at = ((1 - z) * RING + (x - step + RING) % RING) * block
        columns = pl.ds(pl.multiple_of(at, block), block)
        here = pl.ds(step * block, block)
        for slot in range(RING):
            take(slot, 0, mem, columns, far_rows.at[pl.ds(slot * mem, mem), here])
            take(slot, mem, few, columns, far_qry.at[pl.ds(slot * few, few), here])
    wait_all(copy_all(copies))

    @pl.when(where[2] == 1)
    def _():
        total[0] = jnp.dot(near_rows[...], weight[0], preferred_element_type=F32)

    @pl.when(where[2] == 0)
    def _():
        total[0, pl.ds(0, RING * few)] = jnp.dot(
            near_qry[...], weight[0], preferred_element_type=F32
        )

    @pl.loop(1, 3)
    def _(plane):
        total[plane] = jnp.dot(near_rows[...], weight[plane], preferred_element_type=F32)


def attend_kernel(where, total, rows, qry, lengths, *refs):
    sides = (refs[:1], refs[1:3])
    outs = refs[3:7]
    low, mixed = refs[7:]
    mem, few = mixed.shape[1], qry.shape[0] // RING
    encoder = where[2]

    def add_half(plane, source, count):
        for side, pieces in enumerate(sides):
            part = pieces[0].shape[3]
            at = pl.ds(side * part, part)
            result = total[plane, pl.ds(0, count), at]
            first = 0
            for piece in pieces:
                depth = piece.shape[0] * piece.shape[2]
                result += jnp.dot(
                    source[:, pl.ds(first, depth)],
                    piece[:, plane].reshape(depth, part),
                    preferred_element_type=F32,
                )
                first += depth
            low[plane, pl.ds(0, count), at] = result.astype(BF16)

    @pl.when(encoder == 1)
    def _():
        add_half(0, rows, RING * mem)

    @pl.when(encoder == 0)
    def _():
        add_half(0, qry, RING * few)

    @pl.loop(1, 3)
    def _(plane):
        add_half(plane, rows, RING * mem)

    heads = low.shape[2] // HEAD
    scale = 1.0 / math.sqrt(HEAD)

    def heads_of(count):
        column = lax.broadcasted_iota(jnp.int32, (count, mem), 1)

        @pl.loop(0, RING)
        def _(slot):
            own = pl.ds(pl.multiple_of(slot * count, count), count)
            keys = pl.ds(pl.multiple_of(slot * mem, mem), mem)
            length = lengths[slot, pl.ds(0, 1), pl.ds(0, 1)].astype(F32).astype(jnp.int32)
            valid = column < length
            for head in range(heads):
                at = pl.ds(head * HEAD, HEAD)
                scores = (
                    lax.dot_general(
                        low[0, own, at],
                        low[1, keys, at],
                        (((1,), (1,)), ((), ())),
                        preferred_element_type=F32,
                    )
                    * scale
                )
                scores = jnp.where(valid, scores, -1e30)
                expo = jnp.exp(scores - jnp.max(scores, axis=-1, keepdims=True))
                probs = (expo / jnp.sum(expo, axis=-1, keepdims=True)).astype(BF16)
                mixed[slot, pl.ds(0, count), at] = jnp.dot(
                    probs, low[2, keys, at], preferred_element_type=F32
                ).astype(BF16)

    @pl.when(encoder == 1)
    def _():
        heads_of(mem)

    @pl.when(encoder == 0)
    def _():
        heads_of(few)

    for slot in range(RING):
        outs[slot][...] = mixed[slot]


def start_projections(where, mem, few, rows, parts):
    width = rows[0].shape[1]
    _, planes, block, part = parts[0].shape
    half = width // 2
    return call(
        start_kernel,
        (
            jax.ShapeDtypeStruct((planes, RING * mem, 2 * part), F32),
            jax.ShapeDtypeStruct((RING * mem, half), BF16),
            jax.ShapeDtypeStruct((RING * few, half), BF16),
            jax.ShapeDtypeStruct((RING, TAIL, 128), BF16),
        ),
        [SMEM] + [HBM] * 7,
        (VMEM,) * 4,
        [
            pltpu.VMEM((RING * mem, half), BF16),
            pltpu.VMEM((RING * few, half), BF16),
            pltpu.VMEM((planes, half, 2 * part), BF16),
            pltpu.SemaphoreType.DMA((64,)),
        ],
        limit=14,
    )(where, *rows, *parts)


def attend(where, mem, started, far):
    total = started[0]
    planes, _, columns = total.shape
    out = jax.ShapeDtypeStruct((mem, columns), BF16)
    return call(
        attend_kernel,
        (out,) * RING,
        [SMEM] + [VMEM] * 7,
        (VMEM,) * RING,
        [
            pltpu.VMEM((planes, RING * mem, columns), BF16),
            pltpu.VMEM((RING, mem, columns), BF16),
        ],
        limit=14,
    )(where, *started, *far)


def project_kernel(part, where, context, queries, *refs):
    mixed = refs[:4]
    weights = refs[4:6]
    few_in = refs[6] if part else None
    out, few_out = refs[6 + part : 8 + part]
    heads, base, sems = refs[8 + part :]
    x, z, encoder, core = where[0], where[1], where[2], where[3]
    quarter = mixed[0].shape[1] // 2
    inner = quarter * RING
    block = weights[0].shape[1]
    few = queries.shape[1]
    columns = pl.ds(part * RING * block, RING * block)
    rows_base = pltpu.make_async_copy(context.at[core, :, columns], base, sems.at[0])
    few_base = pltpu.make_async_copy(
        queries.at[core, :, columns], base.at[pl.ds(0, few)], sems.at[0]
    )
    copies = []
    for step in range(RING):
        for side in range(2):
            at = pl.multiple_of(side * inner + ((x + step) % RING) * quarter, quarter)
            copies.append(
                pltpu.make_async_copy(
                    mixed[step].at[:, pl.ds(side * quarter, quarter)],
                    heads.at[:, pl.ds(at, quarter)],
                    sems.at[1 + step * 2 + side],
                )
            )
    crossed = z if part == 0 else 1 - z

    @pl.when(encoder == 1)
    def _():
        rows_base.start()

    @pl.when(encoder == 0)
    def _():
        few_base.start()

    copy_all(copies)

    @pl.when(encoder == 1)
    def _():
        rows_base.wait()

    @pl.when(encoder == 0)
    def _():
        few_base.wait()

    if part:
        few_out[:, pl.ds(0, RING * block)] = few_in[...]
    wait_all(copies)
    for i in range(RING):
        place = (x - i + RING) % RING
        start = pl.ds(pl.multiple_of((2 * i + crossed) * inner, inner), inner)
        at = pl.ds(pl.multiple_of(place * block, block), block)
        update = sum(
            jnp.dot(
                heads[:, pl.ds(side * inner, inner)],
                weights[side][start, :],
                preferred_element_type=F32,
            )
            for side in range(2)
        )
        result = (base[:, at].astype(F32) + update).astype(BF16)
        out[:, at] = result
        at = pl.ds(pl.multiple_of((part * RING + place) * block, block), block)
        few_out[:, at] = result[:few]


def project(part, where, context, queries, mixed, weights, few_in=()):
    mem, few = context.shape[1], queries.shape[1]
    inner, block = mixed[0].shape[1] // 2 * RING, weights[0].shape[1]
    return call(
        functools.partial(project_kernel, part),
        (
            jax.ShapeDtypeStruct((mem, RING * block), BF16),
            jax.ShapeDtypeStruct((few, (1 + part) * RING * block), BF16),
        ),
        [SMEM] + [HBM] * 6 + [VMEM] * (2 + part),
        (VMEM, VMEM),
        [
            pltpu.VMEM((mem, 2 * inner), BF16),
            pltpu.VMEM((mem, RING * block), BF16),
            pltpu.SemaphoreType.DMA((9,)),
        ],
    )(where, context, queries, *mixed, *weights, *few_in)


def gather_kernel(where, *refs):
    halves = (refs[0:2], refs[2:4])
    ctx_early, qry_early, qry_late = refs[4:6], refs[6:8], refs[8:10]
    ctx_out, qry_out, ctx, qry, sems = refs[10:]
    core, from_encoder = where[3], where[4]
    width = halves[0][0].shape[1]

    def build(rows, few):
        copies = []
        for side in range(2):
            scene = core if side == 0 else 1 - core
            for piece, at in rows[side]:
                target = ctx.at[scene, :, at]
                copies.append(pltpu.make_async_copy(piece, target, sems.at[len(copies)]))
            copies.append(
                pltpu.make_async_copy(few[side], qry.at[scene], sems.at[len(copies)])
            )
        wait_all(copy_all(copies))

    @pl.when(from_encoder == 1)
    def _():
        build(
            [[(halves[i][side], pl.ds(i * width, width)) for i in range(2)] for side in range(2)],
            qry_early,
        )

    @pl.when(from_encoder == 0)
    def _():
        build([[(ctx_early[side], pl.ds(0, 2 * width))] for side in range(2)], qry_late)

    wait_all(
        copy_all(
            [
                pltpu.make_async_copy(ctx, ctx_out, sems.at[0]),
                pltpu.make_async_copy(qry, qry_out, sems.at[1]),
            ]
        )
    )


def gather_result(where, first, second, ctx_early, qry_early, qry_late):
    ctx_shape = (2,) + ctx_early[0].shape
    qry_shape = (2,) + qry_early[0].shape
    return call(
        gather_kernel,
        (jax.ShapeDtypeStruct(ctx_shape, BF16), jax.ShapeDtypeStruct(qry_shape, BF16)),
        [SMEM] + [HBM] * 10,
        (HBM, HBM),
        [
            pltpu.VMEM(ctx_shape, BF16),
            pltpu.VMEM(qry_shape, BF16),
            pltpu.SemaphoreType.DMA((6,)),
        ],
    )(where, *first, *second, *ctx_early, *qry_early, *qry_late)


def both(array):
    return array, other_core(array)


def per_device(context, queries, lengths, norm_gain, qkv_weight, out_weight):
    count = lax.axis_size("section")
    section = lax.axis_index("section")
    place = lax.axis_index("dp")
    core = lax.axis_index("tensor")
    encoders = list(range(count // 2))
    decoders = list(range(count // 2, count))
    before = (section + count - 1) % count
    where = jnp.stack(
        [
            place % RING,
            place // RING,
            (section < count // 2).astype(jnp.int32),
            core,
            (before < count // 2).astype(jnp.int32),
        ]
    ).astype(jnp.int32)
    context, queries = context[0], queries[0]

    mem, few = context.shape[1], queries.shape[1]
    out_shard = out_weight[0]
    out_far = across_z(out_shard)
    own = quarters(where, jnp.swapaxes(qkv_weight[0], 0, 1))
    out_pair = jnp.concatenate([out_shard, out_far])
    near = [own[0]] + [around_x(own[step], step) for step in range(1, RING)]
    arrived = near[1:]
    near = jnp.stack(near)
    far = across_z(after(near, out_pair))

    ctx, qry, normed = norm_scene(
        after(where, *own), context, queries, norm_gain, lengths[0]
    )
    cut = (normed.shape[0] // 32 + 1) * 16
    rows = round_ring(after(normed, out_pair, *arrived), cut)
    started = start_projections(where, mem, few, rows, (near, other_core(near)))

    weights = round_ring(after(out_pair, *rows), out_shard.shape[0], started[0])
    far_other = [other_core(after(far[i : i + 2], started[0])) for i in (0, 2)]

    mixed = attend(after(where, weights[1], weights[4]), mem, started, (far, *far_other))
    weights = both(jnp.concatenate(after(weights, mixed[0])))
    mixed = [mixed[0]] + [around_x(mixed[step], -step) for step in range(1, RING)]
    ctx_early = relay(after(ctx, *mixed), decoders, count)
    qry_early = relay(after(qry, *mixed), encoders, count)

    first, few_first = project(0, where, context, queries, mixed, weights)
    first = relay(first, encoders, count)
    second, few_new = project(1, where, context, queries, mixed, weights, (few_first,))
    qry_early = (qry_early, other_core(qry_early))
    second = relay(after(second, qry_early[1]), encoders, count)
    few_new = relay(few_new, decoders, count)
    ctx_new, qry_new = gather_result(
        where,
        both(first),
        (second, other_core(after(second, few_new))),
        (ctx_early, other_core(after(ctx_early, first))),
        qry_early,
        both(few_new),
    )
    return ctx_new[None], qry_new[None]


def solution(mesh):
    return jax.shard_map(
        per_device,
        mesh=mesh,
        in_specs=(
            P("section", "dp", None, None),
            P("section", "dp", None, None),
            P("section", "dp"),
            P("section", None),
            P("section", "dp", None, "tensor"),
            P("section", "tensor", "dp"),
        ),
        out_specs=(P("section", "dp", None, None), P("section", "dp", None, None)),
        check_vma=False,
    )
```

```python
import functools
import math

import jax
import jax.numpy as jnp
from jax import lax
from jax.experimental import pallas as pl
from jax.experimental.pallas import tpu as pltpu
from jax.sharding import PartitionSpec as P

HEAD = 128
RING = 4
TAIL = 16
HBM = pl.BlockSpec(memory_space=pltpu.HBM)
SMEM = pl.BlockSpec(memory_space=pltpu.SMEM)
VMEM = pl.BlockSpec(memory_space=pltpu.VMEM)
BF16 = jnp.bfloat16
F32 = jnp.float32


def around_x(array, by):
    pairs = [
        (z * RING + x, z * RING + (x + by) % RING) for z in range(2) for x in range(RING)
    ]
    return lax.ppermute(array, "dp", pairs)


def across_z(array):
    return lax.ppermute(array, "dp", [(d, (d + RING) % (2 * RING)) for d in range(2 * RING)])


def other_core(array):
    return lax.ppermute(array, "tensor", [(0, 1), (1, 0)])


def relay(array, sections, count):
    return lax.ppermute(array, "section", [(s, (s + 1) % count) for s in sections])


def round_ring(array, cut, *before_right):
    left, right = around_x(array, 1), around_x(after(array, *before_right), -1)
    return array, left, around_x(left[:cut], 1), around_x(right[cut:], -1), right


def after(array, *others):
    return lax.optimization_barrier((array,) + others)[0]


def copy_all(copies):
    for copy in copies:
        copy.start()
    return copies


def wait_all(copies):
    for copy in copies:
        copy.wait()


def call(kernel, outs, in_specs, out_specs, scratch=(), limit=16):
    return pl.pallas_call(
        kernel,
        out_shape=outs,
        in_specs=in_specs,
        out_specs=out_specs,
        scratch_shapes=list(scratch),
        compiler_params=pltpu.CompilerParams(vmem_limit_bytes=limit * 1024 * 1024),
        cost_estimate=pl.CostEstimate(flops=1, bytes_accessed=1, transcendentals=0),
    )


def quarter_kernel(where, weight, *pieces):
    x = where[0]
    width = pieces[0].shape[2]
    for step, piece in enumerate(pieces):
        start = pl.multiple_of(((x + step) % RING) * width, width)
        piece[...] = weight[:, :, pl.ds(start, width)]


def quarters(where, weight):
    planes, rows, columns = weight.shape
    piece = jax.ShapeDtypeStruct((planes, rows, columns // RING), BF16)
    return call(
        quarter_kernel, (piece,) * RING, [SMEM, VMEM], (VMEM,) * RING
    )(where, weight)


def norm_kernel(where, context, queries, gain, lengths, ctx_out, qry_out, normed, *scratch):
    ctx, qry, sems = scratch
    core = where[3]
    copies = copy_all(
        [
            pltpu.make_async_copy(context.at[core], ctx, sems.at[0]),
            pltpu.make_async_copy(queries.at[core], qry, sems.at[1]),
        ]
    )
    step = 32

    def rows_of(source, raw, below):
        @pl.loop(0, source.shape[0] // step)
        def _(i):
            first = pl.multiple_of(i * step, step)
            low = source[pl.ds(first, step), :]
            wide = low.astype(F32)
            mean = jnp.mean(wide * wide, axis=-1, keepdims=True)
            normed[pl.ds(below + first, step), :] = (
                wide * lax.rsqrt(mean + 1e-06) * gain[...]
            ).astype(BF16)
            raw[pl.ds(first, step), :] = low

    length = lengths[core].astype(F32)
    normed[pl.ds(normed.shape[0] - TAIL, TAIL), :] = jnp.full(
        (TAIL, normed.shape[1]), length
    ).astype(BF16)
    copies[0].wait()
    rows_of(ctx, ctx_out, 0)
    copies[1].wait()
    rows_of(qry, qry_out, ctx.shape[0])


def norm_scene(where, context, queries, gain, lengths):
    ctx = jax.ShapeDtypeStruct(context.shape[1:], BF16)
    qry = jax.ShapeDtypeStruct(queries.shape[1:], BF16)
    rows = ctx.shape[0] + qry.shape[0] + TAIL
    return call(
        norm_kernel,
        (ctx, qry, jax.ShapeDtypeStruct((rows, ctx.shape[1]), BF16)),
        [SMEM, HBM, HBM, VMEM, SMEM],
        (VMEM,) * 3,
        [
            pltpu.VMEM(ctx.shape, BF16),
            pltpu.VMEM(qry.shape, BF16),
            pltpu.SemaphoreType.DMA((2,)),
        ],
    )(where, context, queries, gain, lengths)


def start_kernel(where, *refs):
    rows, parts = refs[:5], refs[5:7]
    total, far_rows, far_qry, lengths, near_rows, near_qry, weight, sems = refs[7:]
    x, z = where[0], where[1]
    mem, few = far_rows.shape[0] // RING, far_qry.shape[0] // RING
    width = far_rows.shape[1]
    copies = []

    def take(slot, first, count, columns, target):
        cut = rows[2].shape[0]
        pieces = [(rows[slot if slot < 2 else 4], first, count, 0)]
        if slot == 2:
            low = min(max(cut - first, 0), count)
            pieces = [(rows[2], first, low, 0), (rows[3], first + low - cut, count - low, low)]
        for source, start, size, at in pieces:
            if size > 0:
                copies.append(
                    pltpu.make_async_copy(
                        source.at[pl.ds(start, size), columns],
                        target.at[pl.ds(at, size)],
                        sems.at[len(copies)],
                    )
                )

    for part, first in ((parts[0], 0), (parts[1], parts[0].shape[3])):
        for step in range(RING):
            _, _, block, columns = part.shape
            at = pl.multiple_of(((x - step + RING) % RING) * block, block)
            target = weight.at[:, pl.ds(at, block), pl.ds(first, columns)]
            copies.append(
                pltpu.make_async_copy(part.at[step], target, sems.at[len(copies)])
            )
    for slot in range(RING):
        columns = pl.ds(pl.multiple_of(z * width, width), width)
        take(slot, 0, mem, columns, near_rows.at[pl.ds(slot * mem, mem)])
        take(slot, mem, few, columns, near_qry.at[pl.ds(slot * few, few)])
        take(slot, mem + few, TAIL, pl.ds(0, 128), lengths.at[slot])
    for step in range(RING):
        at = ((1 - z) * RING + (x - step + RING) % RING) * block
        columns = pl.ds(pl.multiple_of(at, block), block)
        here = pl.ds(step * block, block)
        for slot in range(RING):
            take(slot, 0, mem, columns, far_rows.at[pl.ds(slot * mem, mem), here])
            take(slot, mem, few, columns, far_qry.at[pl.ds(slot * few, few), here])
    wait_all(copy_all(copies))

    @pl.when(where[2] == 1)
    def _():
        total[0] = jnp.dot(near_rows[...], weight[0], preferred_element_type=F32)

    @pl.when(where[2] == 0)
    def _():
        total[0, pl.ds(0, RING * few)] = jnp.dot(
            near_qry[...], weight[0], preferred_element_type=F32
        )

    @pl.loop(1, 3)
    def _(plane):
        total[plane] = jnp.dot(near_rows[...], weight[plane], preferred_element_type=F32)


def attend_kernel(where, total, rows, qry, lengths, *refs):
    sides = (refs[:1], refs[1:3])
    outs = refs[3:7]
    low, mixed = refs[7:]
    mem, few = mixed.shape[1], qry.shape[0] // RING
    encoder = where[2]

    def add_half(plane, source, count):
        for side, pieces in enumerate(sides):
            part = pieces[0].shape[3]
            at = pl.ds(side * part, part)
            result = total[plane, pl.ds(0, count), at]
            first = 0
            for piece in pieces:
                depth = piece.shape[0] * piece.shape[2]
                result += jnp.dot(
                    source[:, pl.ds(first, depth)],
                    piece[:, plane].reshape(depth, part),
                    preferred_element_type=F32,
                )
                first += depth
            low[plane, pl.ds(0, count), at] = result.astype(BF16)

    @pl.when(encoder == 1)
    def _():
        add_half(0, rows, RING * mem)

    @pl.when(encoder == 0)
    def _():
        add_half(0, qry, RING * few)

    @pl.loop(1, 3)
    def _(plane):
        add_half(plane, rows, RING * mem)

    heads = low.shape[2] // HEAD
    scale = 1.0 / math.sqrt(HEAD)

    def heads_of(count):
        column = lax.broadcasted_iota(jnp.int32, (count, mem), 1)

        @pl.loop(0, RING)
        def _(slot):
            own = pl.ds(pl.multiple_of(slot * count, count), count)
            keys = pl.ds(pl.multiple_of(slot * mem, mem), mem)
            length = lengths[slot, pl.ds(0, 1), pl.ds(0, 1)].astype(F32).astype(jnp.int32)
            valid = column < length
            for head in range(heads):
                at = pl.ds(head * HEAD, HEAD)
                scores = (
                    lax.dot_general(
                        low[0, own, at],
                        low[1, keys, at],
                        (((1,), (1,)), ((), ())),
                        preferred_element_type=F32,
                    )
                    * scale
                )
                scores = jnp.where(valid, scores, -1e30)
                expo = jnp.exp(scores - jnp.max(scores, axis=-1, keepdims=True))
                probs = (expo / jnp.sum(expo, axis=-1, keepdims=True)).astype(BF16)
                mixed[slot, pl.ds(0, count), at] = jnp.dot(
                    probs, low[2, keys, at], preferred_element_type=F32
                ).astype(BF16)

    @pl.when(encoder == 1)
    def _():
        heads_of(mem)

    @pl.when(encoder == 0)
    def _():
        heads_of(few)

    for slot in range(RING):
        outs[slot][...] = mixed[slot]


def start_projections(where, mem, few, rows, parts):
    width = rows[0].shape[1]
    _, planes, block, part = parts[0].shape
    half = width // 2
    return call(
        start_kernel,
        (
            jax.ShapeDtypeStruct((planes, RING * mem, 2 * part), F32),
            jax.ShapeDtypeStruct((RING * mem, half), BF16),
            jax.ShapeDtypeStruct((RING * few, half), BF16),
            jax.ShapeDtypeStruct((RING, TAIL, 128), BF16),
        ),
        [SMEM] + [HBM] * 7,
        (VMEM,) * 4,
        [
            pltpu.VMEM((RING * mem, half), BF16),
            pltpu.VMEM((RING * few, half), BF16),
            pltpu.VMEM((planes, half, 2 * part), BF16),
            pltpu.SemaphoreType.DMA((64,)),
        ],
        limit=14,
    )(where, *rows, *parts)


def attend(where, mem, started, far):
    total = started[0]
    planes, _, columns = total.shape
    out = jax.ShapeDtypeStruct((mem, columns), BF16)
    return call(
        attend_kernel,
        (out,) * RING,
        [SMEM] + [VMEM] * 7,
        (VMEM,) * RING,
        [
            pltpu.VMEM((planes, RING * mem, columns), BF16),
            pltpu.VMEM((RING, mem, columns), BF16),
        ],
        limit=14,
    )(where, *started, *far)


def project_kernel(part, where, context, queries, *refs):
    mixed = refs[:4]
    weights = refs[4:6]
    few_in = refs[6] if part else None
    out, few_out = refs[6 + part : 8 + part]
    heads, base, sems = refs[8 + part :]
    x, z, encoder, core = where[0], where[1], where[2], where[3]
    quarter = mixed[0].shape[1] // 2
    inner = quarter * RING
    block = weights[0].shape[1]
    few = queries.shape[1]
    columns = pl.ds(part * RING * block, RING * block)
    rows_base = pltpu.make_async_copy(context.at[core, :, columns], base, sems.at[0])
    few_base = pltpu.make_async_copy(
        queries.at[core, :, columns], base.at[pl.ds(0, few)], sems.at[0]
    )
    copies = []
    for step in range(RING):
        for side in range(2):
            at = pl.multiple_of(side * inner + ((x + step) % RING) * quarter, quarter)
            copies.append(
                pltpu.make_async_copy(
                    mixed[step].at[:, pl.ds(side * quarter, quarter)],
                    heads.at[:, pl.ds(at, quarter)],
                    sems.at[1 + step * 2 + side],
                )
            )
    crossed = z if part == 0 else 1 - z

    @pl.when(encoder == 1)
    def _():
        rows_base.start()

    @pl.when(encoder == 0)
    def _():
        few_base.start()

    copy_all(copies)

    @pl.when(encoder == 1)
    def _():
        rows_base.wait()

    @pl.when(encoder == 0)
    def _():
        few_base.wait()

    if part:
        few_out[:, pl.ds(0, RING * block)] = few_in[...]
    wait_all(copies)
    for i in range(RING):
        place = (x - i + RING) % RING
        start = pl.ds(pl.multiple_of((2 * i + crossed) * inner, inner), inner)
        at = pl.ds(pl.multiple_of(place * block, block), block)
        update = sum(
            jnp.dot(
                heads[:, pl.ds(side * inner, inner)],
                weights[side][start, :],
                preferred_element_type=F32,
            )
            for side in range(2)
        )
        result = (base[:, at].astype(F32) + update).astype(BF16)
        out[:, at] = result
        at = pl.ds(pl.multiple_of((part * RING + place) * block, block), block)
        few_out[:, at] = result[:few]


def project(part, where, context, queries, mixed, weights, few_in=()):
    mem, few = context.shape[1], queries.shape[1]
    inner, block = mixed[0].shape[1] // 2 * RING, weights[0].shape[1]
    return call(
        functools.partial(project_kernel, part),
        (
            jax.ShapeDtypeStruct((mem, RING * block), BF16),
            jax.ShapeDtypeStruct((few, (1 + part) * RING * block), BF16),
        ),
        [SMEM] + [HBM] * 6 + [VMEM] * (2 + part),
        (VMEM, VMEM),
        [
            pltpu.VMEM((mem, 2 * inner), BF16),
            pltpu.VMEM((mem, RING * block), BF16),
            pltpu.SemaphoreType.DMA((9,)),
        ],
    )(where, context, queries, *mixed, *weights, *few_in)


def gather_kernel(where, *refs):
    halves = (refs[0:2], refs[2:4])
    ctx_early, qry_early, qry_late = refs[4:6], refs[6:8], refs[8:10]
    ctx_out, qry_out, ctx, qry, sems = refs[10:]
    core, from_encoder = where[3], where[4]
    width = halves[0][0].shape[1]

    def build(rows, few):
        copies = []
        for side in range(2):
            scene = core if side == 0 else 1 - core
            for piece, at in rows[side]:
                target = ctx.at[scene, :, at]
                copies.append(pltpu.make_async_copy(piece, target, sems.at[len(copies)]))
            copies.append(
                pltpu.make_async_copy(few[side], qry.at[scene], sems.at[len(copies)])
            )
        wait_all(copy_all(copies))

    @pl.when(from_encoder == 1)
    def _():
        build(
            [[(halves[i][side], pl.ds(i * width, width)) for i in range(2)] for side in range(2)],
            qry_early,
        )

    @pl.when(from_encoder == 0)
    def _():
        build([[(ctx_early[side], pl.ds(0, 2 * width))] for side in range(2)], qry_late)

    wait_all(
        copy_all(
            [
                pltpu.make_async_copy(ctx, ctx_out, sems.at[0]),
                pltpu.make_async_copy(qry, qry_out, sems.at[1]),
            ]
        )
    )


def gather_result(where, first, second, ctx_early, qry_early, qry_late):
    ctx_shape = (2,) + ctx_early[0].shape
    qry_shape = (2,) + qry_early[0].shape
    return call(
        gather_kernel,
        (jax.ShapeDtypeStruct(ctx_shape, BF16), jax.ShapeDtypeStruct(qry_shape, BF16)),
        [SMEM] + [HBM] * 10,
        (HBM, HBM),
        [
            pltpu.VMEM(ctx_shape, BF16),
            pltpu.VMEM(qry_shape, BF16),
            pltpu.SemaphoreType.DMA((6,)),
        ],
    )(where, *first, *second, *ctx_early, *qry_early, *qry_late)


def both(array):
    return array, other_core(array)


def per_device(context, queries, lengths, norm_gain, qkv_weight, out_weight):
    count = lax.axis_size("section")
    section = lax.axis_index("section")
    place = lax.axis_index("dp")
    core = lax.axis_index("tensor")
    encoders = list(range(count // 2))
    decoders = list(range(count // 2, count))
    before = (section + count - 1) % count
    where = jnp.stack(
        [
            place % RING,
            place // RING,
            (section < count // 2).astype(jnp.int32),
            core,
            (before < count // 2).astype(jnp.int32),
        ]
    ).astype(jnp.int32)
    context, queries = context[0], queries[0]

    mem, few = context.shape[1], queries.shape[1]
    out_shard = out_weight[0]
    out_far = across_z(out_shard)
    own = quarters(where, jnp.swapaxes(qkv_weight[0], 0, 1))
    out_pair = jnp.concatenate([out_shard, out_far])
    near = [own[0]] + [around_x(own[step], step) for step in range(1, RING)]
    arrived = near[1:]
    near = jnp.stack(near)
    far = across_z(after(near, out_pair))

    ctx, qry, normed = norm_scene(
        after(where, *own), context, queries, norm_gain, lengths[0]
    )
    cut = (normed.shape[0] // 32 + 1) * 16
    rows = round_ring(after(normed, out_pair, *arrived), cut)
    started = start_projections(where, mem, few, rows, (near, other_core(near)))

    weights = round_ring(after(out_pair, *rows), out_shard.shape[0], started[0])
    far_other = [other_core(after(far[i : i + 2], started[0])) for i in (0, 2)]

    ctx_early = relay(after(ctx, *far_other), decoders, count)
    mixed = attend(after(where, weights[1], weights[4]), mem, started, (far, *far_other))
    weights = both(jnp.concatenate(after(weights, mixed[0])))
    mixed = [mixed[0]] + [around_x(mixed[step], -step) for step in range(1, RING)]
    qry_early = relay(after(qry, *mixed), encoders, count)

    first, few_first = project(0, where, context, queries, mixed, weights)
    first = relay(first, encoders, count)
    second, few_new = project(1, where, context, queries, mixed, weights, (few_first,))
    qry_early = (qry_early, other_core(qry_early))
    second = relay(after(second, qry_early[1]), encoders, count)
    few_new = relay(few_new, decoders, count)
    ctx_new, qry_new = gather_result(
        where,
        both(first),
        (second, other_core(after(second, few_new))),
        (ctx_early, other_core(after(ctx_early, few_new))),
        qry_early,
        both(few_new),
    )
    return ctx_new[None], qry_new[None]


def solution(mesh):
    return jax.shard_map(
        per_device,
        mesh=mesh,
        in_specs=(
            P("section", "dp", None, None),
            P("section", "dp", None, None),
            P("section", "dp"),
            P("section", None),
            P("section", "dp", None, "tensor"),
            P("section", "tensor", "dp"),
        ),
        out_specs=(P("section", "dp", None, None), P("section", "dp", None, None)),
        check_vma=False,
    )
```

```python
import functools
import math

import jax
import jax.numpy as jnp
from jax import lax
from jax.experimental import pallas as pl
from jax.experimental.pallas import tpu as pltpu
from jax.sharding import PartitionSpec as P

HEAD = 128
RING = 4
TAIL = 16
HBM = pl.BlockSpec(memory_space=pltpu.HBM)
SMEM = pl.BlockSpec(memory_space=pltpu.SMEM)
VMEM = pl.BlockSpec(memory_space=pltpu.VMEM)
BF16 = jnp.bfloat16
F32 = jnp.float32


def around_x(array, by):
    pairs = [
        (z * RING + x, z * RING + (x + by) % RING) for z in range(2) for x in range(RING)
    ]
    return lax.ppermute(array, "dp", pairs)


def across_z(array):
    return lax.ppermute(array, "dp", [(d, (d + RING) % (2 * RING)) for d in range(2 * RING)])


def other_core(array):
    return lax.ppermute(array, "tensor", [(0, 1), (1, 0)])


def relay(array, sections, count):
    return lax.ppermute(array, "section", [(s, (s + 1) % count) for s in sections])


def round_ring(array, cut, *before_right):
    left, right = around_x(array, 1), around_x(after(array, *before_right), -1)
    return array, left, around_x(left[:cut], 1), around_x(right[cut:], -1), right


def after(array, *others):
    return lax.optimization_barrier((array,) + others)[0]


def copy_all(copies):
    for copy in copies:
        copy.start()
    return copies


def wait_all(copies):
    for copy in copies:
        copy.wait()


def call(kernel, outs, in_specs, out_specs, scratch=(), limit=16):
    return pl.pallas_call(
        kernel,
        out_shape=outs,
        in_specs=in_specs,
        out_specs=out_specs,
        scratch_shapes=list(scratch),
        compiler_params=pltpu.CompilerParams(vmem_limit_bytes=limit * 1024 * 1024),
        cost_estimate=pl.CostEstimate(flops=1, bytes_accessed=1, transcendentals=0),
    )


def quarter_kernel(where, weight, *pieces):
    x = where[0]
    width = pieces[0].shape[2]
    for step, piece in enumerate(pieces):
        start = pl.multiple_of(((x + step) % RING) * width, width)
        piece[...] = weight[:, :, pl.ds(start, width)]


def quarters(where, weight):
    planes, rows, columns = weight.shape
    piece = jax.ShapeDtypeStruct((planes, rows, columns // RING), BF16)
    return call(
        quarter_kernel, (piece,) * RING, [SMEM, VMEM], (VMEM,) * RING
    )(where, weight)


def norm_kernel(where, context, queries, gain, lengths, ctx_out, qry_out, normed, *scratch):
    ctx, qry, sems = scratch
    core = where[3]
    copies = copy_all(
        [
            pltpu.make_async_copy(context.at[core], ctx, sems.at[0]),
            pltpu.make_async_copy(queries.at[core], qry, sems.at[1]),
        ]
    )
    step = 32

    def rows_of(source, raw, below):
        @pl.loop(0, source.shape[0] // step)
        def _(i):
            first = pl.multiple_of(i * step, step)
            low = source[pl.ds(first, step), :]
            wide = low.astype(F32)
            mean = jnp.mean(wide * wide, axis=-1, keepdims=True)
            normed[pl.ds(below + first, step), :] = (
                wide * lax.rsqrt(mean + 1e-06) * gain[...]
            ).astype(BF16)
            raw[pl.ds(first, step), :] = low

    length = lengths[core].astype(F32)
    normed[pl.ds(normed.shape[0] - TAIL, TAIL), :] = jnp.full(
        (TAIL, normed.shape[1]), length
    ).astype(BF16)
    copies[0].wait()
    rows_of(ctx, ctx_out, 0)
    copies[1].wait()
    rows_of(qry, qry_out, ctx.shape[0])


def norm_scene(where, context, queries, gain, lengths):
    ctx = jax.ShapeDtypeStruct(context.shape[1:], BF16)
    qry = jax.ShapeDtypeStruct(queries.shape[1:], BF16)
    rows = ctx.shape[0] + qry.shape[0] + TAIL
    return call(
        norm_kernel,
        (ctx, qry, jax.ShapeDtypeStruct((rows, ctx.shape[1]), BF16)),
        [SMEM, HBM, HBM, VMEM, SMEM],
        (VMEM,) * 3,
        [
            pltpu.VMEM(ctx.shape, BF16),
            pltpu.VMEM(qry.shape, BF16),
            pltpu.SemaphoreType.DMA((2,)),
        ],
    )(where, context, queries, gain, lengths)


def start_kernel(where, *refs):
    rows, parts = refs[:5], refs[5:7]
    total, far_rows, far_qry, lengths, near_rows, near_qry, weight, sems = refs[7:]
    x, z = where[0], where[1]
    mem, few = far_rows.shape[0] // RING, far_qry.shape[0] // RING
    width = far_rows.shape[1]
    copies = []

    def take(slot, first, count, columns, target):
        cut = rows[2].shape[0]
        pieces = [(rows[slot if slot < 2 else 4], first, count, 0)]
        if slot == 2:
            low = min(max(cut - first, 0), count)
            pieces = [(rows[2], first, low, 0), (rows[3], first + low - cut, count - low, low)]
        for source, start, size, at in pieces:
            if size > 0:
                copies.append(
                    pltpu.make_async_copy(
                        source.at[pl.ds(start, size), columns],
                        target.at[pl.ds(at, size)],
                        sems.at[len(copies)],
                    )
                )

    for part, first in ((parts[0], 0), (parts[1], parts[0].shape[3])):
        for step in range(RING):
            _, _, block, columns = part.shape
            at = pl.multiple_of(((x - step + RING) % RING) * block, block)
            target = weight.at[:, pl.ds(at, block), pl.ds(first, columns)]
            copies.append(
                pltpu.make_async_copy(part.at[step], target, sems.at[len(copies)])
            )
    for slot in range(RING):
        columns = pl.ds(pl.multiple_of(z * width, width), width)
        take(slot, 0, mem, columns, near_rows.at[pl.ds(slot * mem, mem)])
        take(slot, mem, few, columns, near_qry.at[pl.ds(slot * few, few)])
        take(slot, mem + few, TAIL, pl.ds(0, 128), lengths.at[slot])
    for step in range(RING):
        at = ((1 - z) * RING + (x - step + RING) % RING) * block
        columns = pl.ds(pl.multiple_of(at, block), block)
        here = pl.ds(step * block, block)
        for slot in range(RING):
            take(slot, 0, mem, columns, far_rows.at[pl.ds(slot * mem, mem), here])
            take(slot, mem, few, columns, far_qry.at[pl.ds(slot * few, few), here])
    wait_all(copy_all(copies))

    @pl.when(where[2] == 1)
    def _():
        total[0] = jnp.dot(near_rows[...], weight[0], preferred_element_type=F32)

    @pl.when(where[2] == 0)
    def _():
        total[0, pl.ds(0, RING * few)] = jnp.dot(
            near_qry[...], weight[0], preferred_element_type=F32
        )

    @pl.loop(1, 3)
    def _(plane):
        total[plane] = jnp.dot(near_rows[...], weight[plane], preferred_element_type=F32)


def attend_kernel(where, total, rows, qry, lengths, *refs):
    sides = (refs[:1], refs[1:3])
    outs = refs[3:7]
    low, mixed = refs[7:]
    mem, few = mixed.shape[1], qry.shape[0] // RING
    encoder = where[2]

    def add_half(plane, source, count):
        for side, pieces in enumerate(sides):
            part = pieces[0].shape[3]
            at = pl.ds(side * part, part)
            result = total[plane, pl.ds(0, count), at]
            first = 0
            for piece in pieces:
                depth = piece.shape[0] * piece.shape[2]
                result += jnp.dot(
                    source[:, pl.ds(first, depth)],
                    piece[:, plane].reshape(depth, part),
                    preferred_element_type=F32,
                )
                first += depth
            low[plane, pl.ds(0, count), at] = result.astype(BF16)

    @pl.when(encoder == 1)
    def _():
        add_half(0, rows, RING * mem)

    @pl.when(encoder == 0)
    def _():
        add_half(0, qry, RING * few)

    @pl.loop(1, 3)
    def _(plane):
        add_half(plane, rows, RING * mem)

    heads = low.shape[2] // HEAD
    scale = 1.0 / math.sqrt(HEAD)

    def heads_of(count):
        column = lax.broadcasted_iota(jnp.int32, (count, mem), 1)

        @pl.loop(0, RING)
        def _(slot):
            own = pl.ds(pl.multiple_of(slot * count, count), count)
            keys = pl.ds(pl.multiple_of(slot * mem, mem), mem)
            length = lengths[slot, pl.ds(0, 1), pl.ds(0, 1)].astype(F32).astype(jnp.int32)
            valid = column < length
            for head in range(heads):
                at = pl.ds(head * HEAD, HEAD)
                scores = (
                    lax.dot_general(
                        low[0, own, at],
                        low[1, keys, at],
                        (((1,), (1,)), ((), ())),
                        preferred_element_type=F32,
                    )
                    * scale
                )
                scores = jnp.where(valid, scores, -1e30)
                expo = jnp.exp(scores - jnp.max(scores, axis=-1, keepdims=True))
                probs = (expo / jnp.sum(expo, axis=-1, keepdims=True)).astype(BF16)
                mixed[slot, pl.ds(0, count), at] = jnp.dot(
                    probs, low[2, keys, at], preferred_element_type=F32
                ).astype(BF16)

    @pl.when(encoder == 1)
    def _():
        heads_of(mem)

    @pl.when(encoder == 0)
    def _():
        heads_of(few)

    for slot in range(RING):
        outs[slot][...] = mixed[slot]


def start_projections(where, mem, few, rows, parts):
    width = rows[0].shape[1]
    _, planes, block, part = parts[0].shape
    half = width // 2
    return call(
        start_kernel,
        (
            jax.ShapeDtypeStruct((planes, RING * mem, 2 * part), F32),
            jax.ShapeDtypeStruct((RING * mem, half), BF16),
            jax.ShapeDtypeStruct((RING * few, half), BF16),
            jax.ShapeDtypeStruct((RING, TAIL, 128), BF16),
        ),
        [SMEM] + [HBM] * 7,
        (VMEM,) * 4,
        [
            pltpu.VMEM((RING * mem, half), BF16),
            pltpu.VMEM((RING * few, half), BF16),
            pltpu.VMEM((planes, half, 2 * part), BF16),
            pltpu.SemaphoreType.DMA((64,)),
        ],
        limit=14,
    )(where, *rows, *parts)


def attend(where, mem, started, far):
    total = started[0]
    planes, _, columns = total.shape
    out = jax.ShapeDtypeStruct((mem, columns), BF16)
    return call(
        attend_kernel,
        (out,) * RING,
        [SMEM] + [VMEM] * 7,
        (VMEM,) * RING,
        [
            pltpu.VMEM((planes, RING * mem, columns), BF16),
            pltpu.VMEM((RING, mem, columns), BF16),
        ],
        limit=14,
    )(where, *started, *far)


def project_kernel(part, where, context, queries, *refs):
    mixed = refs[:4]
    weights = refs[4:6]
    few_in = refs[6] if part else None
    out, few_out = refs[6 + part : 8 + part]
    heads, base, sems = refs[8 + part :]
    x, z, encoder, core = where[0], where[1], where[2], where[3]
    quarter = mixed[0].shape[1] // 2
    inner = quarter * RING
    block = weights[0].shape[1]
    few = queries.shape[1]
    columns = pl.ds(part * RING * block, RING * block)
    rows_base = pltpu.make_async_copy(context.at[core, :, columns], base, sems.at[0])
    few_base = pltpu.make_async_copy(
        queries.at[core, :, columns], base.at[pl.ds(0, few)], sems.at[0]
    )
    copies = []
    for step in range(RING):
        for side in range(2):
            at = pl.multiple_of(side * inner + ((x + step) % RING) * quarter, quarter)
            copies.append(
                pltpu.make_async_copy(
                    mixed[step].at[:, pl.ds(side * quarter, quarter)],
                    heads.at[:, pl.ds(at, quarter)],
                    sems.at[1 + step * 2 + side],
                )
            )
    crossed = z if part == 0 else 1 - z

    @pl.when(encoder == 1)
    def _():
        rows_base.start()

    @pl.when(encoder == 0)
    def _():
        few_base.start()

    copy_all(copies)

    @pl.when(encoder == 1)
    def _():
        rows_base.wait()

    @pl.when(encoder == 0)
    def _():
        few_base.wait()

    if part:
        few_out[:, pl.ds(0, RING * block)] = few_in[...]
    wait_all(copies)
    for i in range(RING):
        place = (x - i + RING) % RING
        start = pl.ds(pl.multiple_of((2 * i + crossed) * inner, inner), inner)
        at = pl.ds(pl.multiple_of(place * block, block), block)
        update = sum(
            jnp.dot(
                heads[:, pl.ds(side * inner, inner)],
                weights[side][start, :],
                preferred_element_type=F32,
            )
            for side in range(2)
        )
        result = (base[:, at].astype(F32) + update).astype(BF16)
        out[:, at] = result
        at = pl.ds(pl.multiple_of((part * RING + place) * block, block), block)
        few_out[:, at] = result[:few]


def project(part, where, context, queries, mixed, weights, few_in=()):
    mem, few = context.shape[1], queries.shape[1]
    inner, block = mixed[0].shape[1] // 2 * RING, weights[0].shape[1]
    return call(
        functools.partial(project_kernel, part),
        (
            jax.ShapeDtypeStruct((mem, RING * block), BF16),
            jax.ShapeDtypeStruct((few, (1 + part) * RING * block), BF16),
        ),
        [SMEM] + [HBM] * 6 + [VMEM] * (2 + part),
        (VMEM, VMEM),
        [
            pltpu.VMEM((mem, 2 * inner), BF16),
            pltpu.VMEM((mem, RING * block), BF16),
            pltpu.SemaphoreType.DMA((9,)),
        ],
    )(where, context, queries, *mixed, *weights, *few_in)


def gather_kernel(where, *refs):
    halves = (refs[0:2], refs[2:4])
    ctx_early, qry_early, qry_late = refs[4:6], refs[6:8], refs[8:10]
    ctx_out, qry_out, ctx, qry, sems = refs[10:]
    core, from_encoder = where[3], where[4]
    width = halves[0][0].shape[1]

    def build(rows, few):
        copies = []
        for side in range(2):
            scene = core if side == 0 else 1 - core
            for piece, at in rows[side]:
                target = ctx.at[scene, :, at]
                copies.append(pltpu.make_async_copy(piece, target, sems.at[len(copies)]))
            copies.append(
                pltpu.make_async_copy(few[side], qry.at[scene], sems.at[len(copies)])
            )
        wait_all(copy_all(copies))

    @pl.when(from_encoder == 1)
    def _():
        build(
            [[(halves[i][side], pl.ds(i * width, width)) for i in range(2)] for side in range(2)],
            qry_early,
        )

    @pl.when(from_encoder == 0)
    def _():
        build([[(ctx_early[side], pl.ds(0, 2 * width))] for side in range(2)], qry_late)

    wait_all(
        copy_all(
            [
                pltpu.make_async_copy(ctx, ctx_out, sems.at[0]),
                pltpu.make_async_copy(qry, qry_out, sems.at[1]),
            ]
        )
    )


def gather_result(where, first, second, ctx_early, qry_early, qry_late):
    ctx_shape = (2,) + ctx_early[0].shape
    qry_shape = (2,) + qry_early[0].shape
    return call(
        gather_kernel,
        (jax.ShapeDtypeStruct(ctx_shape, BF16), jax.ShapeDtypeStruct(qry_shape, BF16)),
        [SMEM] + [HBM] * 10,
        (HBM, HBM),
        [
            pltpu.VMEM(ctx_shape, BF16),
            pltpu.VMEM(qry_shape, BF16),
            pltpu.SemaphoreType.DMA((6,)),
        ],
    )(where, *first, *second, *ctx_early, *qry_early, *qry_late)


def both(array):
    return array, other_core(array)


def per_device(context, queries, lengths, norm_gain, qkv_weight, out_weight):
    count = lax.axis_size("section")
    section = lax.axis_index("section")
    place = lax.axis_index("dp")
    core = lax.axis_index("tensor")
    encoders = list(range(count // 2))
    decoders = list(range(count // 2, count))
    before = (section + count - 1) % count
    where = jnp.stack(
        [
            place % RING,
            place // RING,
            (section < count // 2).astype(jnp.int32),
            core,
            (before < count // 2).astype(jnp.int32),
        ]
    ).astype(jnp.int32)
    context, queries = context[0], queries[0]

    mem, few = context.shape[1], queries.shape[1]
    out_shard = out_weight[0]
    out_far = across_z(out_shard)
    own = quarters(where, jnp.swapaxes(qkv_weight[0], 0, 1))
    out_pair = jnp.concatenate([out_shard, out_far])
    near = [own[0]] + [around_x(own[step], step) for step in range(1, RING)]
    arrived = near[1:]
    near = jnp.stack(near)
    far = across_z(after(near, out_pair))

    ctx, qry, normed = norm_scene(
        after(where, *own), context, queries, norm_gain, lengths[0]
    )
    cut = (normed.shape[0] // 32 + 1) * 16
    rows = round_ring(after(normed, out_pair, *arrived), cut)
    started = start_projections(where, mem, few, rows, (near, other_core(near)))

    weights = round_ring(after(out_pair, *rows), out_shard.shape[0], started[0])
    far_other = [other_core(after(far[i : i + 2], started[0])) for i in (0, 2)]

    ctx_early = relay(after(ctx, *far_other), decoders, count)
    mixed = attend(after(where, weights[1], weights[4]), mem, started, (far, *far_other))
    weights = both(jnp.concatenate(after(weights, mixed[0])))
    mixed = [mixed[0]] + [around_x(mixed[step], -step) for step in range(1, RING)]
    qry_early = relay(after(qry, *mixed), encoders, count)

    first, few_first = project(0, where, context, queries, mixed, weights)
    first = relay(first, encoders, count)
    second, few_new = project(1, where, context, queries, mixed, weights, (few_first,))
    qry_early = (qry_early, other_core(qry_early))
    second = relay(after(second, qry_early[1]), encoders, count)
    few_new = relay(few_new, decoders, count)
    ctx_new, qry_new = gather_result(
        where,
        both(first),
        (second, other_core(after(second, few_new))),
        (ctx_early, other_core(after(ctx_early, first, few_new))),
        qry_early,
        both(few_new),
    )
    return ctx_new[None], qry_new[None]


def solution(mesh):
    return jax.shard_map(
        per_device,
        mesh=mesh,
        in_specs=(
            P("section", "dp", None, None),
            P("section", "dp", None, None),
            P("section", "dp"),
            P("section", None),
            P("section", "dp", None, "tensor"),
            P("section", "tensor", "dp"),
        ),
        out_specs=(P("section", "dp", None, None), P("section", "dp", None, None)),
        check_vma=False,
    )
```

```python
import functools
import math

import jax
import jax.numpy as jnp
from jax import lax
from jax.experimental import pallas as pl
from jax.experimental.pallas import tpu as pltpu
from jax.sharding import PartitionSpec as P

HEAD = 128
RING = 4
TAIL = 16
HBM = pl.BlockSpec(memory_space=pltpu.HBM)
SMEM = pl.BlockSpec(memory_space=pltpu.SMEM)
VMEM = pl.BlockSpec(memory_space=pltpu.VMEM)
BF16 = jnp.bfloat16
F32 = jnp.float32


def around_x(array, by):
    pairs = [
        (z * RING + x, z * RING + (x + by) % RING) for z in range(2) for x in range(RING)
    ]
    return lax.ppermute(array, "dp", pairs)


def across_z(array):
    return lax.ppermute(array, "dp", [(d, (d + RING) % (2 * RING)) for d in range(2 * RING)])


def other_core(array):
    return lax.ppermute(array, "tensor", [(0, 1), (1, 0)])


def relay(array, sections, count):
    return lax.ppermute(array, "section", [(s, (s + 1) % count) for s in sections])


def round_ring(array, cut, *before_right):
    left, right = around_x(array, 1), around_x(after(array, *before_right), -1)
    return array, left, around_x(left[:cut], 1), around_x(right[cut:], -1), right


def after(array, *others):
    return lax.optimization_barrier((array,) + others)[0]


def copy_all(copies):
    for copy in copies:
        copy.start()
    return copies


def wait_all(copies):
    for copy in copies:
        copy.wait()


def call(kernel, outs, in_specs, out_specs, scratch=(), limit=16):
    return pl.pallas_call(
        kernel,
        out_shape=outs,
        in_specs=in_specs,
        out_specs=out_specs,
        scratch_shapes=list(scratch),
        compiler_params=pltpu.CompilerParams(vmem_limit_bytes=limit * 1024 * 1024),
        cost_estimate=pl.CostEstimate(flops=1, bytes_accessed=1, transcendentals=0),
    )


def quarter_kernel(where, weight, *pieces):
    x = where[0]
    width = pieces[0].shape[2]
    for step, piece in enumerate(pieces):
        start = pl.multiple_of(((x + step) % RING) * width, width)
        piece[...] = weight[:, :, pl.ds(start, width)]


def quarters(where, weight):
    planes, rows, columns = weight.shape
    piece = jax.ShapeDtypeStruct((planes, rows, columns // RING), BF16)
    return call(
        quarter_kernel, (piece,) * RING, [SMEM, VMEM], (VMEM,) * RING
    )(where, weight)


def norm_kernel(where, context, queries, gain, lengths, ctx_out, qry_out, normed, *scratch):
    ctx, qry, sems = scratch
    core = where[3]
    copies = copy_all(
        [
            pltpu.make_async_copy(context.at[core], ctx, sems.at[0]),
            pltpu.make_async_copy(queries.at[core], qry, sems.at[1]),
        ]
    )
    step = 32

    def rows_of(source, raw, below):
        @pl.loop(0, source.shape[0] // step)
        def _(i):
            first = pl.multiple_of(i * step, step)
            low = source[pl.ds(first, step), :]
            wide = low.astype(F32)
            mean = jnp.mean(wide * wide, axis=-1, keepdims=True)
            normed[pl.ds(below + first, step), :] = (
                wide * lax.rsqrt(mean + 1e-06) * gain[...]
            ).astype(BF16)
            raw[pl.ds(first, step), :] = low

    length = lengths[core].astype(F32)
    normed[pl.ds(normed.shape[0] - TAIL, TAIL), :] = jnp.full(
        (TAIL, normed.shape[1]), length
    ).astype(BF16)
    copies[0].wait()
    rows_of(ctx, ctx_out, 0)
    copies[1].wait()
    rows_of(qry, qry_out, ctx.shape[0])


def norm_scene(where, context, queries, gain, lengths):
    ctx = jax.ShapeDtypeStruct(context.shape[1:], BF16)
    qry = jax.ShapeDtypeStruct(queries.shape[1:], BF16)
    rows = ctx.shape[0] + qry.shape[0] + TAIL
    return call(
        norm_kernel,
        (ctx, qry, jax.ShapeDtypeStruct((rows, ctx.shape[1]), BF16)),
        [SMEM, HBM, HBM, VMEM, SMEM],
        (VMEM,) * 3,
        [
            pltpu.VMEM(ctx.shape, BF16),
            pltpu.VMEM(qry.shape, BF16),
            pltpu.SemaphoreType.DMA((2,)),
        ],
    )(where, context, queries, gain, lengths)


def start_kernel(where, *refs):
    rows, parts = refs[:5], refs[5:7]
    total, far_rows, far_qry, lengths, near_rows, near_qry, weight, sems = refs[7:]
    x, z = where[0], where[1]
    mem, few = far_rows.shape[0] // RING, far_qry.shape[0] // RING
    width = far_rows.shape[1]
    copies = []

    def take(slot, first, count, columns, target):
        cut = rows[2].shape[0]
        pieces = [(rows[slot if slot < 2 else 4], first, count, 0)]
        if slot == 2:
            low = min(max(cut - first, 0), count)
            pieces = [(rows[2], first, low, 0), (rows[3], first + low - cut, count - low, low)]
        for source, start, size, at in pieces:
            if size > 0:
                copies.append(
                    pltpu.make_async_copy(
                        source.at[pl.ds(start, size), columns],
                        target.at[pl.ds(at, size)],
                        sems.at[len(copies)],
                    )
                )

    for part, first in ((parts[0], 0), (parts[1], parts[0].shape[3])):
        for step in range(RING):
            _, _, block, columns = part.shape
            at = pl.multiple_of(((x - step + RING) % RING) * block, block)
            target = weight.at[:, pl.ds(at, block), pl.ds(first, columns)]
            copies.append(
                pltpu.make_async_copy(part.at[step], target, sems.at[len(copies)])
            )
    for slot in range(RING):
        columns = pl.ds(pl.multiple_of(z * width, width), width)
        take(slot, 0, mem, columns, near_rows.at[pl.ds(slot * mem, mem)])
        take(slot, mem, few, columns, near_qry.at[pl.ds(slot * few, few)])
        take(slot, mem + few, TAIL, pl.ds(0, 128), lengths.at[slot])
    for step in range(RING):
        at = ((1 - z) * RING + (x - step + RING) % RING) * block
        columns = pl.ds(pl.multiple_of(at, block), block)
        here = pl.ds(step * block, block)
        for slot in range(RING):
            take(slot, 0, mem, columns, far_rows.at[pl.ds(slot * mem, mem), here])
            take(slot, mem, few, columns, far_qry.at[pl.ds(slot * few, few), here])
    wait_all(copy_all(copies))

    @pl.when(where[2] == 1)
    def _():
        total[0] = jnp.dot(near_rows[...], weight[0], preferred_element_type=F32)

    @pl.when(where[2] == 0)
    def _():
        total[0, pl.ds(0, RING * few)] = jnp.dot(
            near_qry[...], weight[0], preferred_element_type=F32
        )

    @pl.loop(1, 3)
    def _(plane):
        total[plane] = jnp.dot(near_rows[...], weight[plane], preferred_element_type=F32)


def attend_kernel(where, total, rows, qry, lengths, *refs):
    sides = (refs[:1], refs[1:3])
    outs = refs[3:7]
    low, mixed = refs[7:]
    mem, few = mixed.shape[1], qry.shape[0] // RING
    encoder = where[2]

    def add_half(plane, source, count):
        for side, pieces in enumerate(sides):
            part = pieces[0].shape[3]
            at = pl.ds(side * part, part)
            result = total[plane, pl.ds(0, count), at]
            first = 0
            for piece in pieces:
                depth = piece.shape[0] * piece.shape[2]
                result += jnp.dot(
                    source[:, pl.ds(first, depth)],
                    piece[:, plane].reshape(depth, part),
                    preferred_element_type=F32,
                )
                first += depth
            low[plane, pl.ds(0, count), at] = result.astype(BF16)

    @pl.when(encoder == 1)
    def _():
        add_half(0, rows, RING * mem)

    @pl.when(encoder == 0)
    def _():
        add_half(0, qry, RING * few)

    @pl.loop(1, 3)
    def _(plane):
        add_half(plane, rows, RING * mem)

    heads = low.shape[2] // HEAD
    scale = 1.0 / math.sqrt(HEAD)

    def heads_of(count):
        column = lax.broadcasted_iota(jnp.int32, (count, mem), 1)

        @pl.loop(0, RING)
        def _(slot):
            own = pl.ds(pl.multiple_of(slot * count, count), count)
            keys = pl.ds(pl.multiple_of(slot * mem, mem), mem)
            length = lengths[slot, pl.ds(0, 1), pl.ds(0, 1)].astype(F32).astype(jnp.int32)
            valid = column < length
            for head in range(heads):
                at = pl.ds(head * HEAD, HEAD)
                scores = (
                    lax.dot_general(
                        low[0, own, at],
                        low[1, keys, at],
                        (((1,), (1,)), ((), ())),
                        preferred_element_type=F32,
                    )
                    * scale
                )
                scores = jnp.where(valid, scores, -1e30)
                expo = jnp.exp(scores - jnp.max(scores, axis=-1, keepdims=True))
                inverse = 1.0 / jnp.sum(expo, axis=-1, keepdims=True)
                probs = (expo * inverse).astype(BF16)
                mixed[slot, pl.ds(0, count), at] = jnp.dot(
                    probs, low[2, keys, at], preferred_element_type=F32
                ).astype(BF16)

    @pl.when(encoder == 1)
    def _():
        heads_of(mem)

    @pl.when(encoder == 0)
    def _():
        heads_of(few)

    for slot in range(RING):
        outs[slot][...] = mixed[slot]


def start_projections(where, mem, few, rows, parts):
    width = rows[0].shape[1]
    _, planes, block, part = parts[0].shape
    half = width // 2
    return call(
        start_kernel,
        (
            jax.ShapeDtypeStruct((planes, RING * mem, 2 * part), F32),
            jax.ShapeDtypeStruct((RING * mem, half), BF16),
            jax.ShapeDtypeStruct((RING * few, half), BF16),
            jax.ShapeDtypeStruct((RING, TAIL, 128), BF16),
        ),
        [SMEM] + [HBM] * 7,
        (VMEM,) * 4,
        [
            pltpu.VMEM((RING * mem, half), BF16),
            pltpu.VMEM((RING * few, half), BF16),
            pltpu.VMEM((planes, half, 2 * part), BF16),
            pltpu.SemaphoreType.DMA((64,)),
        ],
        limit=14,
    )(where, *rows, *parts)


def attend(where, mem, started, far):
    total = started[0]
    planes, _, columns = total.shape
    out = jax.ShapeDtypeStruct((mem, columns), BF16)
    return call(
        attend_kernel,
        (out,) * RING,
        [SMEM] + [VMEM] * 7,
        (VMEM,) * RING,
        [
            pltpu.VMEM((planes, RING * mem, columns), BF16),
            pltpu.VMEM((RING, mem, columns), BF16),
        ],
        limit=14,
    )(where, *started, *far)


def project_kernel(part, where, context, queries, *refs):
    mixed = refs[:4]
    weights = refs[4:6]
    few_in = refs[6] if part else None
    out, few_out = refs[6 + part : 8 + part]
    heads, base, sems = refs[8 + part :]
    x, z, encoder, core = where[0], where[1], where[2], where[3]
    quarter = mixed[0].shape[1] // 2
    inner = quarter * RING
    block = weights[0].shape[1]
    few = queries.shape[1]
    columns = pl.ds(part * RING * block, RING * block)
    rows_base = pltpu.make_async_copy(context.at[core, :, columns], base, sems.at[0])
    few_base = pltpu.make_async_copy(
        queries.at[core, :, columns], base.at[pl.ds(0, few)], sems.at[0]
    )
    copies = []
    for step in range(RING):
        for side in range(2):
            at = pl.multiple_of(side * inner + ((x + step) % RING) * quarter, quarter)
            copies.append(
                pltpu.make_async_copy(
                    mixed[step].at[:, pl.ds(side * quarter, quarter)],
                    heads.at[:, pl.ds(at, quarter)],
                    sems.at[1 + step * 2 + side],
                )
            )
    crossed = z if part == 0 else 1 - z

    @pl.when(encoder == 1)
    def _():
        rows_base.start()

    @pl.when(encoder == 0)
    def _():
        few_base.start()

    copy_all(copies)

    @pl.when(encoder == 1)
    def _():
        rows_base.wait()

    @pl.when(encoder == 0)
    def _():
        few_base.wait()

    if part:
        few_out[:, pl.ds(0, RING * block)] = few_in[...]
    wait_all(copies)
    for i in range(RING):
        place = (x - i + RING) % RING
        start = pl.ds(pl.multiple_of((2 * i + crossed) * inner, inner), inner)
        at = pl.ds(pl.multiple_of(place * block, block), block)
        update = sum(
            jnp.dot(
                heads[:, pl.ds(side * inner, inner)],
                weights[side][start, :],
                preferred_element_type=F32,
            )
            for side in range(2)
        )
        result = (base[:, at].astype(F32) + update).astype(BF16)
        out[:, at] = result
        at = pl.ds(pl.multiple_of((part * RING + place) * block, block), block)
        few_out[:, at] = result[:few]


def project(part, where, context, queries, mixed, weights, few_in=()):
    mem, few = context.shape[1], queries.shape[1]
    inner, block = mixed[0].shape[1] // 2 * RING, weights[0].shape[1]
    return call(
        functools.partial(project_kernel, part),
        (
            jax.ShapeDtypeStruct((mem, RING * block), BF16),
            jax.ShapeDtypeStruct((few, (1 + part) * RING * block), BF16),
        ),
        [SMEM] + [HBM] * 6 + [VMEM] * (2 + part),
        (VMEM, VMEM),
        [
            pltpu.VMEM((mem, 2 * inner), BF16),
            pltpu.VMEM((mem, RING * block), BF16),
            pltpu.SemaphoreType.DMA((9,)),
        ],
    )(where, context, queries, *mixed, *weights, *few_in)


def gather_kernel(where, *refs):
    halves = (refs[0:2], refs[2:4])
    ctx_early, qry_early, qry_late = refs[4:6], refs[6:8], refs[8:10]
    ctx_out, qry_out, ctx, qry, sems = refs[10:]
    core, from_encoder = where[3], where[4]
    width = halves[0][0].shape[1]

    def build(rows, few):
        copies = []
        for side in range(2):
            scene = core if side == 0 else 1 - core
            for piece, at in rows[side]:
                target = ctx.at[scene, :, at]
                copies.append(pltpu.make_async_copy(piece, target, sems.at[len(copies)]))
            copies.append(
                pltpu.make_async_copy(few[side], qry.at[scene], sems.at[len(copies)])
            )
        wait_all(copy_all(copies))

    @pl.when(from_encoder == 1)
    def _():
        build(
            [[(halves[i][side], pl.ds(i * width, width)) for i in range(2)] for side in range(2)],
            qry_early,
        )

    @pl.when(from_encoder == 0)
    def _():
        build([[(ctx_early[side], pl.ds(0, 2 * width))] for side in range(2)], qry_late)

    wait_all(
        copy_all(
            [
                pltpu.make_async_copy(ctx, ctx_out, sems.at[0]),
                pltpu.make_async_copy(qry, qry_out, sems.at[1]),
            ]
        )
    )


def gather_result(where, first, second, ctx_early, qry_early, qry_late):
    ctx_shape = (2,) + ctx_early[0].shape
    qry_shape = (2,) + qry_early[0].shape
    return call(
        gather_kernel,
        (jax.ShapeDtypeStruct(ctx_shape, BF16), jax.ShapeDtypeStruct(qry_shape, BF16)),
        [SMEM] + [HBM] * 10,
        (HBM, HBM),
        [
            pltpu.VMEM(ctx_shape, BF16),
            pltpu.VMEM(qry_shape, BF16),
            pltpu.SemaphoreType.DMA((6,)),
        ],
    )(where, *first, *second, *ctx_early, *qry_early, *qry_late)


def both(array):
    return array, other_core(array)


def per_device(context, queries, lengths, norm_gain, qkv_weight, out_weight):
    count = lax.axis_size("section")
    section = lax.axis_index("section")
    place = lax.axis_index("dp")
    core = lax.axis_index("tensor")
    encoders = list(range(count // 2))
    decoders = list(range(count // 2, count))
    before = (section + count - 1) % count
    where = jnp.stack(
        [
            place % RING,
            place // RING,
            (section < count // 2).astype(jnp.int32),
            core,
            (before < count // 2).astype(jnp.int32),
        ]
    ).astype(jnp.int32)
    context, queries = context[0], queries[0]

    mem, few = context.shape[1], queries.shape[1]
    out_shard = out_weight[0]
    out_far = across_z(out_shard)
    own = quarters(where, jnp.swapaxes(qkv_weight[0], 0, 1))
    out_pair = jnp.concatenate([out_shard, out_far])
    near = [own[0]] + [around_x(own[step], step) for step in range(1, RING)]
    arrived = near[1:]
    near = jnp.stack(near)
    far = across_z(after(near, out_pair))

    ctx, qry, normed = norm_scene(
        after(where, *own), context, queries, norm_gain, lengths[0]
    )
    cut = (normed.shape[0] // 32 + 1) * 16
    rows = round_ring(after(normed, out_pair, *arrived), cut)
    started = start_projections(where, mem, few, rows, (near, other_core(near)))

    weights = round_ring(after(out_pair, *rows), out_shard.shape[0], started[0])
    far_other = [other_core(after(far[i : i + 2], started[0])) for i in (0, 2)]

    ctx_early = relay(after(ctx, *far_other), decoders, count)
    mixed = attend(after(where, weights[1], weights[4]), mem, started, (far, *far_other))
    weights = both(jnp.concatenate(after(weights, mixed[0])))
    mixed = [mixed[0]] + [around_x(mixed[step], -step) for step in range(1, RING)]
    qry_early = relay(after(qry, *mixed), encoders, count)

    first, few_first = project(0, where, context, queries, mixed, weights)
    first = relay(first, encoders, count)
    second, few_new = project(1, where, context, queries, mixed, weights, (few_first,))
    qry_early = (qry_early, other_core(qry_early))
    second = relay(after(second, qry_early[1]), encoders, count)
    few_new = relay(few_new, decoders, count)
    ctx_new, qry_new = gather_result(
        where,
        both(first),
        (second, other_core(after(second, few_new))),
        (ctx_early, other_core(after(ctx_early, first, few_new))),
        qry_early,
        both(few_new),
    )
    return ctx_new[None], qry_new[None]


def solution(mesh):
    return jax.shard_map(
        per_device,
        mesh=mesh,
        in_specs=(
            P("section", "dp", None, None),
            P("section", "dp", None, None),
            P("section", "dp"),
            P("section", None),
            P("section", "dp", None, "tensor"),
            P("section", "tensor", "dp"),
        ),
        out_specs=(P("section", "dp", None, None), P("section", "dp", None, None)),
        check_vma=False,
    )
```
